512 devices in a mesh: wide: 64 (over x, z_lo, core), narrow: 8 (over y, z_hi).
Axes of the slice: x: 4, y: 4, z: 16 (z_hi: 2, z_lo: 8; z = z_hi * 8 + z_lo), core: 2. Of those that a mesh axis runs over, the one named last changes fastest.
Arguments:
- surface_prev: float32 [8192, 1024], P('wide', 'narrow'), may hold values from -6 to 6
- surface_now: float32 [8192, 1024], P('wide', 'narrow'), may hold values from -6 to 6
- eastward_prev: float32 [8192, 1024], P('wide', 'narrow'), may hold values from -6 to 6
- eastward_now: float32 [8192, 1024], P('wide', 'narrow'), may hold values from -6 to 6
- northward_prev: float32 [8192, 1024], P('wide', 'narrow'), may hold values from -6 to 6
- northward_now: float32 [8192, 1024], P('wide', 'narrow'), may hold values from -6 to 6
- depth_west: float32 [8192, 1024], P('wide', 'narrow'), may hold values from 0 to 1.2, as said below
- depth_south: float32 [8192, 1024], P('wide', 'narrow'), may hold values from 0 to 1.2, as said below
- edge_links: int32 [8, 4, 3], replicated, may hold values from 0 to 7, as said below
- phase_start: float32 [8], replicated, may hold values from -3.140625 to 3.140625
Outputs:
- surface_last: float32 [8192, 1024], P('wide', 'narrow')
- eastward_last: float32 [8192, 1024], P('wide', 'narrow')
- northward_last: float32 [8192, 1024], P('wide', 'narrow')
- harmonics: float32 [16, 8192, 1024], P(None, 'wide', 'narrow')
The draws below stay inside these ranges and needn't reach their ends.
Inputs may be any that keep to these rules, and one draw needn't show every extreme that they name: edge_links[f, e] = (g, k, r) says that edge e of face f (0 west, 1 south, 2 east, 3 north) is glued to edge k of face g, with cells in opposite order along the edge when r = 1. The relation is symmetric: edge_links[g, k] = (f, e, r). West and south edges are glued only to east and north edges, and the reverse. `depth_west`: zero at land sides, positive elsewhere. `depth_south`: zero at land sides, positive elsewhere.
All inputs are finite; a program needn't handle non-finite values.
Results may differ from the reference program's by a relative error of at most 0.000071.
Values sent between devices are 32-bit elements; how exact they have to be, the bound alone decides.
A program may use at most 64 MiB of HBM per device.

```python
import jax
import jax.numpy as jnp
from jax import lax

SUBSTEPS = 4
CONSTITUENTS = 8
FACE = 1024
NF = 8
ROWS = 8192


def draw_depth_west(key, part):
    depth_values = jax.random.uniform(jax.random.fold_in(key, 11), (ROWS, FACE), jnp.float32, 0.3, 1.2)
    land_draw = jax.random.uniform(jax.random.fold_in(key, 12), (ROWS, FACE), jnp.float32)
    return jnp.where(land_draw < 0.15, 0.0, depth_values).astype(jnp.float32)


def draw_depth_south(key, part):
    depth_values = jax.random.uniform(jax.random.fold_in(key, 21), (ROWS, FACE), jnp.float32, 0.3, 1.2)
    land_draw = jax.random.uniform(jax.random.fold_in(key, 22), (ROWS, FACE), jnp.float32)
    return jnp.where(land_draw < 0.15, 0.0, depth_values).astype(jnp.float32)


def draw_edge_links(key, part):
    edge_total = 2 * NF
    targets = jax.random.permutation(jax.random.fold_in(key, 31), edge_total).astype(jnp.int32)
    flipped = jax.random.randint(jax.random.fold_in(key, 32), (edge_total,), 0, 2).astype(jnp.int32)
    owners = jnp.arange(edge_total, dtype=jnp.int32)
    owner_face = owners // 2
    owner_edge = owners % 2
    target_face = targets // 2
    target_edge = targets % 2 + 2
    linked = jnp.zeros((NF, 4, 3), jnp.int32)
    linked = linked.at[owner_face, owner_edge].set(jnp.stack([target_face, target_edge, flipped], axis=-1))
    linked = linked.at[target_face, target_edge].set(jnp.stack([owner_face, owner_edge, flipped], axis=-1))
    return linked.astype(jnp.int32)


def block_scale(rng, extent, cuts, low, largest):
    level, own = 1.0, jax.random.fold_in(rng, 6)
    for dim, parts in cuts:
        draws = jnp.exp(jax.random.uniform(jax.random.fold_in(own, dim), (parts,), jnp.float32, low / len(cuts), largest / len(cuts)))
        level = level * jnp.repeat(draws, extent[dim] // parts).reshape([-1 if axis == dim else 1 for axis in range(len(extent))])
    return level


def bell_draw(key, extent, deviation, bound, split=(), kind=jnp.bfloat16):
    result = jax.random.normal(key, extent, jnp.float32) * deviation
    if len(split) > 0:
        result = block_scale(key, extent, split, -0.22, 0.18) * result
    return jnp.clip(result, min=-bound, max=bound).astype(kind)


def setup_inputs(seed: int = 0) -> dict:
    key_list = jax.random.split(jax.random.key(seed), 11)
    surface_prev = bell_draw(key_list[0], (ROWS, FACE), 1.0, 6.0, ((0, 64), (1, 8)), jnp.float32)
    surface_now = bell_draw(key_list[1], (ROWS, FACE), 1.0, 6.0, ((0, 64), (1, 8)), jnp.float32)
    eastward_prev = bell_draw(key_list[2], (ROWS, FACE), 1.0, 6.0, ((0, 64), (1, 8)), jnp.float32)
    eastward_now = bell_draw(key_list[3], (ROWS, FACE), 1.0, 6.0, ((0, 64), (1, 8)), jnp.float32)
    northward_prev = bell_draw(key_list[4], (ROWS, FACE), 1.0, 6.0, ((0, 64), (1, 8)), jnp.float32)
    northward_now = bell_draw(key_list[5], (ROWS, FACE), 1.0, 6.0, ((0, 64), (1, 8)), jnp.float32)
    depth_west = draw_depth_west(jax.random.fold_in(key_list[10], 71), 0)
    depth_south = draw_depth_south(jax.random.fold_in(key_list[10], 71), 0)
    edge_links = draw_edge_links(jax.random.fold_in(key_list[10], 71), 0)
    phase_start = jnp.clip(jax.random.uniform(key_list[9], (CONSTITUENTS,), jnp.float32, -3.140625, 3.140625), -3.140625, 3.140625)
    return dict(surface_prev=surface_prev, surface_now=surface_now, eastward_prev=eastward_prev, eastward_now=eastward_now, northward_prev=northward_prev, northward_now=northward_now, depth_west=depth_west, depth_south=depth_south, edge_links=edge_links, phase_start=phase_start)


tide_omega = (1.405189e-4, 1.454441e-4, 1.378797e-4, 1.458423e-4, 7.292117e-5, 6.759774e-5, 7.251056e-5, 6.495854e-5)
step_seconds = 25.0
mass_factor = 0.3
flow_factor = 0.3
filter_weight = 0.1


def phase_rows(phase_start):
    counter_values = jnp.arange(1, SUBSTEPS + 1).astype(jnp.float32)
    tide_rates = jnp.array(tide_omega, jnp.float32) * step_seconds
    angles = phase_start[:, None] + tide_rates[:, None] * counter_values[None, :]
    return jnp.concatenate([jnp.cos(angles), jnp.sin(angles)], axis=0)


def partner_lines(link_rows, first_kind, first_lines, second_lines):
    face_ids = link_rows[:, 0].astype(jnp.int32)
    first_pick = jnp.take(first_lines, face_ids, axis=0)
    second_pick = jnp.take(second_lines, face_ids, axis=0)
    chosen = jnp.where((link_rows[:, 1] == first_kind)[:, None], first_pick, second_pick)
    return jnp.where((link_rows[:, 2] == 1)[:, None], chosen[:, ::-1], chosen)


def reference(surface_prev, surface_now, eastward_prev, eastward_now, northward_prev, northward_now, depth_west, depth_south, edge_links, phase_start):
    face_shape = (NF, FACE, FACE)
    surface_prev = surface_prev.reshape(face_shape)
    surface_now = surface_now.reshape(face_shape)
    eastward_prev = eastward_prev.reshape(face_shape)
    eastward_now = eastward_now.reshape(face_shape)
    northward_prev = northward_prev.reshape(face_shape)
    northward_now = northward_now.reshape(face_shape)
    depth_west = depth_west.reshape(face_shape)
    depth_south = depth_south.reshape(face_shape)
    snapshots = []
    for substep in range(SUBSTEPS):
        flux_west = depth_west * eastward_now
        flux_south = depth_south * northward_now
        west_line = partner_lines(edge_links[:, 0], 2, surface_now[:, :, -1], surface_now[:, -1, :])
        south_line = partner_lines(edge_links[:, 1], 2, surface_now[:, :, -1], surface_now[:, -1, :])
        east_line = partner_lines(edge_links[:, 2], 0, flux_west[:, :, 0], flux_south[:, 0, :])
        north_line = partner_lines(edge_links[:, 3], 0, flux_west[:, :, 0], flux_south[:, 0, :])
        flux_east = jnp.concatenate([flux_west[:, :, 1:], east_line[:, :, None]], axis=2)
        flux_north = jnp.concatenate([flux_south[:, 1:, :], north_line[:, None, :]], axis=1)
        surface_west = jnp.concatenate([west_line[:, :, None], surface_now[:, :, :-1]], axis=2)
        surface_south = jnp.concatenate([south_line[:, None, :], surface_now[:, :-1, :]], axis=1)
        divergence = (flux_east - flux_west) + (flux_north - flux_south)
        surface_next = surface_prev - 2.0 * mass_factor * divergence
        eastward_next = eastward_prev - 2.0 * flow_factor * (surface_now - surface_west)
        northward_next = northward_prev - 2.0 * flow_factor * (surface_now - surface_south)
        surface_prev = surface_now + filter_weight * (surface_prev - 2.0 * surface_now + surface_next)
        eastward_prev = eastward_now + filter_weight * (eastward_prev - 2.0 * eastward_now + eastward_next)
        northward_prev = northward_now + filter_weight * (northward_prev - 2.0 * northward_now + northward_next)
        surface_now = surface_next
        eastward_now = eastward_next
        northward_now = northward_next
        snapshots.append(surface_now)
    stacked = jnp.stack(snapshots).reshape(SUBSTEPS, NF * FACE * FACE)
    harmonics = jnp.dot(phase_rows(phase_start), stacked, precision=lax.Precision.HIGHEST)
    return (surface_now.reshape(ROWS, FACE), eastward_now.reshape(ROWS, FACE), northward_now.reshape(ROWS, FACE), harmonics.reshape(2 * CONSTITUENTS, ROWS, FACE))
```

```python
import functools

import jax
import jax.numpy as jnp
from jax import lax
from jax.experimental import pallas as pl
from jax.experimental.pallas import tpu as pltpu
from jax.sharding import PartitionSpec as P

MESH = pl.DeviceIdType.MESH
SUBSTEPS = 4
CONSTITUENTS = 8
tide_omega = (
    0.0001405189,
    0.0001454441,
    0.0001378797,
    0.0001458423,
    7.292117e-05,
    6.759774e-05,
    7.251056e-05,
    6.495854e-05,
)
step_seconds = 25.0
G = 0.6
W, S, E, N = range(4)
LINES = 9


def rims(s, sp, n, np_, t, tp, dn, dt):
    last = s.shape[0] - 1
    row = lambda x, i: x[i : i + 1, :]
    a, b = last, last - 1
    n1 = row(np_, a) - G * (row(s, a) - row(s, b))
    fa = row(dn, a) * row(n, a)
    fb = row(dn, b) * row(n, b)
    back = G * row(dn, a)
    older = 0.8 * row(n, a) + 0.1 * row(np_, a) + 0.1 * n1
    high = [
        row(s, a),
        row(sp, a) + G * fa,
        0.8 * row(s, a) + 0.1 * row(sp, a) + G * (row(dn, a) * n1),
        0.08 * row(s, a)
        + 0.01 * row(sp, a)
        + G * (row(dn, a) * older + back * (row(sp, b) - G * (fa - fb))),
        back,
        row(dt, a) * row(t, a),
        row(dt, a) * row(tp, a),
        G * row(dt, a),
        row(dt, b) * row(t, b),
    ]
    a, b = 0, 1
    n1 = row(np_, b) - G * (row(s, b) - row(s, a))
    fa = row(dn, a) * row(n, a)
    fb = row(dn, b) * row(n, b)
    low = [
        row(s, a),
        row(sp, a) - G * (fb - fa),
        0.8 * row(s, a) + 0.1 * row(sp, a) - G * (row(dn, b) * n1),
        row(dn, a) * row(np_, a),
        G * row(dn, a),
        row(dt, a) * row(t, a),
        row(dt, a) * row(tp, a),
        G * row(dt, a),
        fa,
    ]
    return low, high


def exchange(
    sides, faces, ph, sp, s, up, u, vp, v, dw, ds,
    ws_ref, en_ref, wx_ref, ex_ref, cx_ref, dx_ref, coef_ref,
    pack, ends,
    near_send, near_recv, diag_send, diag_recv, main_send, ext_send, ws_recv, en_recv, wx_recv, ex_recv, own_sem, corner_send, corner_recv,
):
    last = sides - 1
    w = lax.axis_index("wide")
    c = lax.axis_index("narrow")
    f = w // sides
    r = w % sides
    at = lambda face, row, col: (face * sides + row, col)
    signal = lambda bar, d: pl.semaphore_signal(bar, inc=1, device_id=d, device_id_type=MESH)
    is_end = lambda q: (q == 0) | (q == last)
    corner = is_end(r) & is_end(c)
    has_ws = (c == 0) | (r == 0)
    has_en = (c == last) | (r == last)
    seg_ws = jnp.where(c == 0, r, c)
    seg_en = jnp.where(c == last, r, c)
    corner_at = lambda i: at(i // 4, (i // 2) % 2 * last, i % 2 * last)
    me_corner = f * 4 + (r // last) * 2 + c // last

    bar = pltpu.get_barrier_semaphore()
    around = [
        (dr, dc, (r + dr >= 0) & (r + dr <= last) & (c + dc >= 0) & (c + dc <= last))
        for dr in (-1, 0, 1)
        for dc in (-1, 0, 1)
        if (dr, dc) != (0, 0)
    ]
    awaited = jnp.int32(0)
    for dr, dc, there in around:
        awaited += there.astype(jnp.int32)

        @pl.when(there)
        def _(dr=dr, dc=dc):
            signal(bar, at(f, r + dr, c + dc))

    def greet(seg, line):
        def body(g, _):
            for q in (seg, last - seg):
                for row, col in ((q, line), (line, q)):

                    @pl.when(~((g == f) & (row == r) & (col == c)))
                    def _(row=row, col=col):
                        signal(bar, at(g, row, col))

            for q in (seg - 1, seg + 1, last - 1 - seg, last + 1 - seg):

                @pl.when((q >= 0) & (q <= last))
                def _(q=q):
                    signal(bar, at(g, q, line))
                    signal(bar, at(g, line, q))

            return 0

        lax.fori_loop(0, faces, body, 0)

    @pl.when(has_ws)
    def _():
        greet(seg_ws, last)

    @pl.when(has_en)
    def _():
        greet(seg_en, 0)

    @pl.when(corner)
    def _():
        def body(i, _):
            @pl.when(i != me_corner)
            def _():
                signal(bar, corner_at(i))

            return 0

        lax.fori_loop(0, 4 * faces, body, 0)

    lo, hi = rims(s[...], sp[...], v[...], vp[...], u[...], up[...], ds[...], dw[...])
    for k in range(LINES):
        pack[S, k : k + 1, :] = lo[k]
        pack[N, k : k + 1, :] = hi[k]
    flip = lambda x: jnp.transpose(x[...])
    lo, hi = rims(flip(s), flip(sp), flip(u), flip(up), flip(v), flip(vp), flip(dw), flip(ds))
    for k in range(LINES):
        pack[W, k : k + 1, :] = lo[k]
        pack[E, k : k + 1, :] = hi[k]
    side = s.shape[0]
    for e in range(4):
        pack[e, LINES:16, :] = jnp.zeros((16 - LINES, side), jnp.float32)
    stacked = jnp.concatenate([pack[e] for e in range(4)] + [jnp.zeros((side - 64, side), jnp.float32)], axis=0)
    turned = jnp.transpose(stacked)
    lane = lax.broadcasted_iota(jnp.int32, (1, side), 1)
    for e in range(4):
        gathered = jnp.zeros((1, side), jnp.float32)
        for k, i in enumerate((0, 1, side - 2, side - 1)):
            moved = turned[i : i + 1, :]
            by = (16 * k - 16 * e) % side
            if by:
                moved = pltpu.roll(moved, by, 1)
            gathered = jnp.where((lane >= 16 * k) & (lane < 16 * k + 16), moved, gathered)
        ends[e] = gathered

    which = lax.broadcasted_iota(jnp.int32, (CONSTITUENTS, side), 0)
    count = (lax.broadcasted_iota(jnp.int32, (CONSTITUENTS, side), 1) + 1).astype(jnp.float32)
    start = jnp.zeros((CONSTITUENTS, side), jnp.float32)
    rate = jnp.zeros((CONSTITUENTS, side), jnp.float32)
    for k in range(CONSTITUENTS):
        start = jnp.where(which == k, ph[k], start)
        rate = jnp.where(which == k, jnp.float32(tide_omega[k]) * jnp.float32(step_seconds), rate)
    angle = start + rate * count
    coef_ref[0:CONSTITUENTS, :] = jnp.cos(angle)
    coef_ref[CONSTITUENTS:, :] = jnp.sin(angle)

    edges = [
        (E, 0, True, c == last, r, r == 0),
        (N, 1, True, r == last, c, c == 0),
        (W, 0, False, c == 0, r, r == last),
        (S, 1, False, r == 0, c, c == last),
    ]
    n_main = lambda q, own: jnp.where(is_end(q), 3 * faces - own.astype(jnp.int32), 4 * faces)
    n_ext = lambda q: jnp.where(is_end(q), 4 * faces, jnp.where((q == 1) | (q == last - 1), 7 * faces, 8 * faces))
    for _, _, _, has, q, own in edges:
        awaited += jnp.where(has, n_main(q, own) + n_ext(q), 0)
    awaited += jnp.where(corner, 4 * faces - 1, 0)
    pl.semaphore_wait(bar, awaited)

    block = pl.ds(0, LINES)
    for e, kind, to_ws, has, q, own in edges:
        dst, dst_x = (ws_ref, wx_ref) if to_ws else (en_ref, ex_ref)
        got, got_x = (ws_recv, wx_recv) if to_ws else (en_recv, ex_recv)
        line = 0 if to_ws else last

        @pl.when(has)
        def _(e=e, kind=kind, q=q, own=own, dst=dst, dst_x=dst_x, got=got, got_x=got_x, line=line):
            def send_main(g, _):
                for par in range(2):
                    to = q if par == 0 else last - q
                    slot = (f * 2 + kind) * 2 + par
                    for k, (row, col) in enumerate(((to, line), (line, to))):
                        mine = (g == f) & (row == r) & (col == c)
                        once = ~mine if k == 0 else ~mine & (to != line)

                        @pl.when(once)
                        def _(slot=slot, row=row, col=col):
                            pltpu.make_async_remote_copy(
                                pack.at[e, block], dst.at[slot, block], main_send.at[e], got.at[0],
                                device_id=at(g, row, col), device_id_type=MESH,
                            ).start()

                        if k == 0:
                            local = mine
                        else:
                            local = mine & (to != line)

                        @pl.when(local)
                        def _(slot=slot):
                            pltpu.make_async_copy(pack.at[e, block], dst.at[slot, block], got.at[0]).start()

                return 0

            lax.fori_loop(0, faces, send_main, 0)

            def send_ext(g, _):
                for kind_x, to in enumerate((q + 1, q - 1, last - 1 - q, last + 1 - q)):
                    slot = (f * 2 + kind) * 4 + kind_x
                    there = (to >= 0) & (to <= last)
                    for k, (row, col) in enumerate(((to, line), (line, to))):

                        @pl.when(there if k == 0 else there & (to != line))
                        def _(slot=slot, row=row, col=col):
                            pltpu.make_async_remote_copy(
                                ends.at[e], dst_x.at[slot], ext_send.at[e], got_x.at[0],
                                device_id=at(g, row, col), device_id_type=MESH,
                            ).start()

                return 0

            lax.fori_loop(0, faces, send_ext, 0)

    @pl.when(corner)
    def _():
        def body(i, _):
            @pl.when(i != me_corner)
            def _():
                pltpu.make_async_remote_copy(
                    ends, cx_ref.at[me_corner], corner_send.at[0], corner_recv.at[0], device_id=corner_at(i), device_id_type=MESH
                ).start()

            @pl.when(i == me_corner)
            def _():
                pltpu.make_async_copy(ends, cx_ref.at[me_corner], corner_recv.at[0]).start()

            return 0

        lax.fori_loop(0, 4 * faces, body, 0)

    near = [
        (E, ws_ref, 4 * faces, 0, 1),
        (N, ws_ref, 4 * faces + 1, 1, 0),
        (W, en_ref, 4 * faces, 0, -1),
        (S, en_ref, 4 * faces + 1, -1, 0),
    ]
    diagonal = [(0, 1, 1), (1, 1, -1), (2, -1, 1), (3, -1, -1)]
    inside = lambda row, col: (row >= 0) & (row <= last) & (col >= 0) & (col <= last)
    for e, dst, slot, dr, dc in near:

        @pl.when(inside(r + dr, c + dc))
        def _(e=e, dst=dst, slot=slot, dr=dr, dc=dc):
            pltpu.make_async_remote_copy(
                pack.at[e, block], dst.at[slot, block], near_send.at[e], near_recv.at[e],
                device_id=at(f, r + dr, c + dc), device_id_type=MESH,
            ).start()

    for k, dr, dc in diagonal:

        @pl.when(inside(r + dr, c + dc))
        def _(k=k, dr=dr, dc=dc):
            pltpu.make_async_remote_copy(
                ends, dx_ref.at[k], diag_send.at[k], diag_recv.at[k], device_id=at(f, r + dr, c + dc), device_id_type=MESH
            ).start()

    here = (w, c)
    take = lambda ref, ss, rs: pltpu.make_async_remote_copy(ref, ref, ss, rs, device_id=here, device_id_type=MESH)
    for e, dst, slot, dr, dc in near:

        @pl.when(inside(r - dr, c - dc))
        def _(e=e, dst=dst, slot=slot):
            take(dst.at[slot, block], near_send.at[e], near_recv.at[e]).wait_recv()

    for k, dr, dc in diagonal:

        @pl.when(inside(r - dr, c - dc))
        def _(k=k):
            take(dx_ref.at[k], diag_send.at[k], diag_recv.at[k]).wait_recv()

    for has, seg, main, ext, got, got_x in (
        (has_ws, seg_ws, ws_ref, wx_ref, ws_recv, wx_recv),
        (has_en, seg_en, en_ref, ex_ref, en_recv, ex_recv),
    ):

        @pl.when(has)
        def _(seg=seg, main=main, ext=ext, got=got, got_x=got_x):
            take(main.at[pl.ds(0, 4 * faces), block], main_send.at[0], got.at[0]).wait_recv()

            @pl.when(is_end(seg))
            def _():
                take(ext.at[pl.ds(0, 4 * faces)], ext_send.at[0], got_x.at[0]).wait_recv()

            @pl.when(~is_end(seg))
            def _():
                take(ext, ext_send.at[0], got_x.at[0]).wait_recv()

    @pl.when(corner)
    def _():
        take(cx_ref, corner_send.at[0], corner_recv.at[0]).wait_recv()

    for e, dst, slot, dr, dc in near:

        @pl.when(inside(r + dr, c + dc))
        def _(e=e):
            take(pack.at[e, block], near_send.at[e], near_recv.at[e]).wait_send()

    for k, dr, dc in diagonal:

        @pl.when(inside(r + dr, c + dc))
        def _(k=k):
            take(ends, diag_send.at[k], diag_recv.at[k]).wait_send()

    for e, kind, to_ws, has, q, own in edges:
        for n in (3 * faces - 1, 3 * faces, 4 * faces):

            @pl.when(has & (n_main(q, own) == n))
            def _(e=e, n=n):
                take(ws_ref.at[pl.ds(0, n), block], main_send.at[e], ws_recv.at[0]).wait_send()

        for n in (4 * faces, 7 * faces, 8 * faces):

            @pl.when(has & (n_ext(q) == n))
            def _(e=e, n=n):
                take(wx_ref.at[pl.ds(0, n)], ext_send.at[e], wx_recv.at[0]).wait_send()

    @pl.when(corner)
    def _():
        take(cx_ref.at[pl.ds(0, 4 * faces - 1)], corner_send.at[0], corner_recv.at[0]).wait_send()


def substeps(
    sides, faces, links, sp, s, up, u, vp, v, dw, ds, ws, en, wx, ex, cx, dx, coef, s_out, u_out, v_out, h_out,
):
    last = sides - 1
    side = s.shape[0]
    w = lax.axis_index("wide")
    c = lax.axis_index("narrow")
    f = w // sides
    r = w % sides
    lane = lax.broadcasted_iota(jnp.int32, (1, side), 1)
    rows = lax.broadcasted_iota(jnp.int32, (side, side), 0)
    cols = lax.broadcasted_iota(jnp.int32, (side, side), 1)
    mirror = (rows + cols == side - 1).astype(jnp.float32)
    diagonal = rows == cols
    pick = lambda cond, a, b: jnp.where(cond, a, b)
    up_by = lambda x, fill: jnp.where(lane == side - 1, fill, pltpu.roll(x, side - 1, 1))
    down_by = lambda x, fill: jnp.where(lane == 0, fill, pltpu.roll(x, 1, 1))
    head = lambda x: x[:, 0:1]
    tail = lambda x: x[:, side - 1 : side]

    def end(x, k, line):
        return x[:, 16 * k + line : 16 * k + line + 1]

    def corner_of(face, edge, high):
        row = jnp.where(edge == S, 0, jnp.where(edge == N, 1, high))
        col = jnp.where(edge == W, 0, jnp.where(edge == E, 1, high))
        return cx[face * 4 + row * 2 + col, edge]

    def at_end(x, high, k, line):
        return pick(high == 1, end(x, 3 - k, line), end(x, k, line))

    def beyond(face, edge, high):
        far, far_edge, turn = links[face, edge, 0], links[face, edge, 1], links[face, edge, 2]
        stop = high ^ turn
        return at_end(corner_of(far, far_edge, stop), stop, 0, 8)

    def at_corner(face, edge, low_end, inner):
        vertical = (edge == W) | (edge == E)
        side_edge = jnp.where(vertical, S, W) if low_end else jnp.where(vertical, N, E)
        start = (edge >= E).astype(jnp.int32)
        far, far_edge, turn = links[face, side_edge, 0], links[face, side_edge, 1], links[face, side_edge, 2]
        high = start ^ turn
        x = corner_of(far, far_edge, high)
        far_vertical = (far_edge == W) | (far_edge == E)
        third = beyond(far, jnp.where(far_vertical, N, E), (far_edge >= E).astype(jnp.int32))
        ahead = pick(high == 1, third, end(x, 1, 5))
        s1 = at_end(x, high, 0, 1) - G * (ahead - at_end(x, high, 0, 5))
        got = dict(s0=at_end(x, high, 0, 0), s1=s1)
        if low_end:
            got["s1"] = s1 - G * inner
        else:
            got.update(
                T0=at_end(x, high, 0, 8),
                Q=at_end(x, high, 0, 3),
                D=at_end(x, high, 0, 4),
                Tb=at_end(x, high, 1, 8),
            )
        return got

    def ghost(edge, to_ws):
        main, ext = (ws, wx) if to_ws else (en, ex)
        on_face = {W: c == 0, S: r == 0, E: c == last, N: r == last}[edge]
        across = edge in (W, E)
        seg = r if across else c
        face, partner, turn = links[f, edge, 0], links[f, edge, 1], links[f, edge, 2]
        flipped = on_face & (turn == 1)
        kind = (partner == (N if to_ws else S)).astype(jnp.int32)
        q = jnp.where(turn == 1, last - seg, seg)
        slot = jnp.where(on_face, (face * 2 + kind) * 2 + turn, 4 * faces + (0 if across else 1))
        block = main[slot]
        line = [block[k : k + 1, :] for k in range(LINES)]
        slot_x = jnp.where(on_face, (face * 2 + kind) * 4 + 2 * turn, 0)
        strip = (edge + 2) % 4
        lo_at, hi_at = {W: (0, 2), S: (0, 1), E: (1, 3), N: (2, 3)}[edge]
        lo_x = pick(on_face, wx_row(ext, slot_x), dx[lo_at, strip])
        hi_x = pick(on_face, wx_row(ext, slot_x + 1), dx[hi_at, strip])
        first = head(line[5])
        lo = dict(
            s0=end(lo_x, 3, 0), s1=end(lo_x, 3, 1) - G * (first - end(lo_x, 3, 5)),
            F=end(lo_x, 3, 8), R=end(lo_x, 3, 3), Dn=end(lo_x, 3, 4), Fb=end(lo_x, 2, 8),
        )
        hi = dict(
            s0=end(hi_x, 0, 0), s1=end(hi_x, 0, 1) - G * (end(hi_x, 1, 5) - end(hi_x, 0, 5)),
            T0=end(hi_x, 0, 5), Q=end(hi_x, 0, 6), D=end(hi_x, 0, 7), Tb=end(hi_x, 0, 8),
            F=end(hi_x, 0, 8), R=end(hi_x, 0, 3), Dn=end(hi_x, 0, 4), Fb=end(hi_x, 1, 8),
        )
        lo_corner = on_face & (q == 0)
        hi_corner = on_face & (q == last)
        safe = lambda x, top: jnp.where(on_face, x, top)
        g_face, g_edge = safe(face, 0), safe(partner, E if to_ws else W)
        third_lo = at_corner(g_face, g_edge, True, first)
        third_hi = at_corner(g_face, g_edge, False, first)
        for name, value in third_lo.items():
            lo[name] = pick(lo_corner, value, lo[name])
        for name, value in third_hi.items():
            hi[name] = pick(hi_corner, value, hi[name])
        lo["done"], hi["done"] = lo_corner, hi_corner
        turned = jnp.dot(block, mirror, precision=lax.Precision.HIGHEST, preferred_element_type=jnp.float32)
        turned = [turned[k : k + 1, :] for k in range(LINES)]
        along = {5: ("T0", -1.0), 6: ("Q", -1.0), 7: ("D", 1.0)}
        if to_ws:
            along[8] = ("Tb", -1.0)
        out = []
        for k in range(LINES):
            if k in along:
                name, sign = along[k]
                other = sign * down_by(turned[k], hi[name])
            else:
                other = turned[k]
            out.append(pick(flipped, other, line[k]))
        new_lo = {n: pick(flipped, hi[n], lo[n]) for n in ("s0", "s1", "F", "R", "Dn", "Fb")}
        new_hi = {n: pick(flipped, lo[n], hi[n]) for n in ("s0", "s1", "F", "R", "Dn", "Fb")}
        for k, (name, sign) in along.items():
            new_hi[name] = pick(flipped, sign * head(line[k]), hi[name])
        new_lo["done"] = jnp.where(flipped, hi_corner, lo_corner)
        new_hi["done"] = jnp.where(flipped, lo_corner, hi_corner)
        return out, new_lo, new_hi

    def wx_row(ext, slot):
        return ext[slot]

    (wl, w_lo, w_hi), (sl, s_lo, s_hi) = ghost(W, True), ghost(S, True)
    (el, e_lo, e_hi), (nl, n_lo, n_hi) = ghost(E, False), ghost(N, False)

    for d, x in ((w_lo, sl), (w_hi, nl), (s_lo, wl), (s_hi, el)):
        d["s1"] = pick(d["done"], d["s1"], d["s1"] - G * head(x[5]))

    west, south, east, north = c == 0, r == 0, c == last, r == last
    take_w, take_s = west & ~south, south & ~west
    sw_w = {n: pick(take_s, s_lo[n], w_lo[n]) for n in ("s0", "s1")}
    sw_s = {n: pick(take_w, w_lo[n], s_lo[n]) for n in ("s0", "s1")}
    w_lo.update(sw_w)
    s_lo.update(sw_s)
    share = (("s0", "s0"), ("s1", "s1"), ("T0", "F"), ("Q", "R"), ("D", "Dn"), ("Tb", "Fb"))
    take_e, take_s = east & ~south, south & ~east
    se_s = {a: pick(take_e, e_lo[b], s_hi[a]) for a, b in share}
    e_lo["s0"] = pick(take_s, s_hi["s0"], e_lo["s0"])
    s_hi.update(se_s)
    take_n, take_w = north & ~west, west & ~north
    nw_w = {a: pick(take_n, n_lo[b], w_hi[a]) for a, b in share}
    n_lo["s0"] = pick(take_w, w_hi["s0"], n_lo["s0"])
    w_hi.update(nw_w)
    take_e, take_n = east & ~north, north & ~east
    share = (("s0", "s0"), ("T0", "F"), ("Q", "R"), ("D", "Dn"))
    ne_n = {a: pick(take_e, e_hi[b], n_hi[a]) for a, b in share}
    ne_e = {a: pick(take_n, n_hi[b], e_hi[a]) for a, b in share}
    n_hi.update(ne_n)
    e_hi.update(ne_e)

    class HeightRim:
        def __init__(self, line, lo, hi):
            self.line, self.lo, self.hi = line, lo, hi

        def at(self, n, flux):
            s0, y1, y2, z, back, t0, q, d, tb = self.line
            lo, hi = self.lo, self.hi
            if n == 0:
                return s0
            if n == 1:
                self.s1 = y1 - G * flux - G * (up_by(t0, hi["T0"]) - t0)
                return self.s1
            if n == 2:
                self.t1 = q - d * (s0 - down_by(s0, lo["s0"]))
                self.t1hi = hi["Q"] - hi["D"] * (hi["s0"] - tail(s0))
                self.s2 = y2 + 0.1 * self.s1 - G * flux - G * (up_by(self.t1, self.t1hi) - self.t1)
                return self.s2
            s1 = self.s1
            t2 = 0.8 * t0 + 0.1 * q + 0.1 * self.t1 - d * (s1 - down_by(s1, lo["s1"]))
            t2hi = 0.8 * hi["T0"] + 0.1 * hi["Q"] + 0.1 * self.t1hi - hi["D"] * (hi["s1"] - tail(s1))
            inner = s1 + G * (up_by(tb, hi["Tb"]) - tb)
            return 0.81 * s1 + 0.1 * self.s2 + z - G * back * inner - G * flux - G * (up_by(t2, t2hi) - t2)

    class FluxRim:
        def __init__(self, line, lo, hi):
            self.line, self.lo, self.hi = line, lo, hi

        def at(self, n, height):
            s0, u1, u2, r_, d_, t0, q, d, f0 = self.line
            lo, hi = self.lo, self.hi
            if n == 0:
                return f0
            if n == 1:
                self.f1 = r_ - d_ * (s0 - height)
                return self.f1
            if n == 2:
                self.s1 = u1 - G * (up_by(t0, hi["T0"]) - t0)
                self.older = 0.8 * f0 + 0.1 * r_ + 0.1 * self.f1
                self.f2 = self.older - d_ * (self.s1 - height)
                return self.f2
            t1 = q - d * (s0 - down_by(s0, lo["s0"]))
            t1hi = hi["Q"] - hi["D"] * (hi["s0"] - tail(s0))
            s2 = u2 + 0.1 * self.s1 + G * self.f1 - G * (up_by(t1, t1hi) - t1)
            return 0.8 * self.f1 + 0.1 * self.f2 + 0.1 * self.older - d_ * (s2 - height)

    rim_w, rim_s = HeightRim(wl, w_lo, w_hi), HeightRim(sl, s_lo, s_hi)
    rim_e, rim_n = FluxRim(el, e_lo, e_hi), FluxRim(nl, n_lo, n_hi)
    as_row = lambda col: jnp.sum(jnp.where(diagonal, col, 0.0), axis=0, keepdims=True)
    as_col = lambda row: jnp.sum(jnp.where(diagonal, row, 0.0), axis=1, keepdims=True)
    s_, u_, v_ = s[...], u[...], v[...]
    sp_, up_, vp_ = sp[...], up[...], vp[...]
    dw_, ds_ = dw[...], ds[...]
    first_col, last_col = cols == 0, cols == side - 1
    first_row, last_row = rows == 0, rows == side - 1
    flux_w = flux_s = height_e = height_n = None
    snaps = []
    for n in range(SUBSTEPS):
        fw, fs = dw_ * u_, ds_ * v_
        west_line, south_line = rim_w.at(n, flux_w), rim_s.at(n, flux_s)
        east_line, north_line = rim_e.at(n, height_e), rim_n.at(n, height_n)
        flux_w, flux_s = as_row(fw[:, 0:1]), fs[0:1, :]
        height_e, height_n = as_row(s_[:, side - 1 : side]), s_[side - 1 : side, :]
        fe = jnp.where(last_col, as_col(east_line), pltpu.roll(fw, side - 1, 1))
        fn = jnp.where(last_row, north_line, pltpu.roll(fs, side - 1, 0))
        sw = jnp.where(first_col, as_col(west_line), pltpu.roll(s_, 1, 1))
        ss = jnp.where(first_row, south_line, pltpu.roll(s_, 1, 0))
        s_next = sp_ - G * ((fe - fw) + (fn - fs))
        u_next = up_ - G * (s_ - sw)
        v_next = vp_ - G * (s_ - ss)
        sp_ = s_ + 0.1 * (sp_ - 2.0 * s_ + s_next)
        up_ = u_ + 0.1 * (up_ - 2.0 * u_ + u_next)
        vp_ = v_ + 0.1 * (vp_ - 2.0 * v_ + v_next)
        s_, u_, v_ = s_next, u_next, v_next
        snaps.append(s_)
    s_out[...] = s_
    u_out[...] = u_
    v_out[...] = v_
    for k in range(2 * CONSTITUENTS):
        total = coef[k : k + 1, 0:1] * snaps[0]
        for n in range(1, SUBSTEPS):
            total += coef[k : k + 1, n : n + 1] * snaps[n]
        h_out[k] = total


def solution(mesh):
    def body(sp, s, up, u, vp, v, dw, ds, links, ph):
        side = s.shape[0]
        sides = mesh.shape["narrow"]
        faces = mesh.shape["wide"] // sides
        f32 = jnp.float32
        shape = lambda *dims: jax.ShapeDtypeStruct(dims, f32)
        vmem = pl.BlockSpec(memory_space=pltpu.VMEM)
        smem = pl.BlockSpec(memory_space=pltpu.SMEM)
        dma = pltpu.SemaphoreType.DMA
        got = pl.pallas_call(
            functools.partial(exchange, sides, faces),
            out_shape=(
                shape(4 * faces + 2, 16, side),
                shape(4 * faces + 2, 16, side),
                shape(8 * faces, 1, side),
                shape(8 * faces, 1, side),
                shape(4 * faces, 4, 1, side),
                shape(4, 4, 1, side),
                shape(2 * CONSTITUENTS, side),
            ),
            in_specs=[smem] + [vmem] * 8,
            out_specs=(vmem,) * 7,
            scratch_shapes=[
                pltpu.VMEM((4, 16, side), f32),
                pltpu.VMEM((4, 1, side), f32),
                dma((4,)), dma((4,)), dma((4,)), dma((4,)), dma((4,)), dma((4,)),
                dma((1,)), dma((1,)), dma((1,)), dma((1,)), dma((1,)), dma((1,)), dma((1,)),
            ],
            compiler_params=pltpu.CompilerParams(collective_id=0, has_side_effects=True),
        )(ph, sp, s, up, u, vp, v, dw, ds)
        tile = shape(side, side)
        return pl.pallas_call(
            functools.partial(substeps, sides, faces),
            out_shape=(tile, tile, tile, shape(2 * CONSTITUENTS, side, side)),
            in_specs=[smem] + [vmem] * 15,
            out_specs=(vmem,) * 4,
        )(links, sp, s, up, u, vp, v, dw, ds, *got)

    tiles = P("wide", "narrow")
    return jax.shard_map(
        body,
        mesh=mesh,
        in_specs=(tiles,) * 8 + (P(), P()),
        out_specs=(tiles, tiles, tiles, P(None, "wide", "narrow")),
        check_vma=False,
    )
```

```python
import functools

import jax
import jax.numpy as jnp
from jax import lax
from jax.experimental import pallas as pl
from jax.experimental.pallas import tpu as pltpu
from jax.sharding import PartitionSpec as P

MESH = pl.DeviceIdType.MESH
SUBSTEPS = 4
CONSTITUENTS = 8
tide_omega = (
    0.0001405189,
    0.0001454441,
    0.0001378797,
    0.0001458423,
    7.292117e-05,
    6.759774e-05,
    7.251056e-05,
    6.495854e-05,
)
step_seconds = 25.0
G = 0.6
W, S, E, N = range(4)
LINES = 9


def rims(s, sp, n, np_, t, tp, dn, dt):
    last = s.shape[0] - 1
    row = lambda x, i: x[i : i + 1, :]
    a, b = last, last - 1
    n1 = row(np_, a) - G * (row(s, a) - row(s, b))
    fa = row(dn, a) * row(n, a)
    fb = row(dn, b) * row(n, b)
    back = G * row(dn, a)
    older = 0.8 * row(n, a) + 0.1 * row(np_, a) + 0.1 * n1
    high = [
        row(s, a),
        row(sp, a) + G * fa,
        0.8 * row(s, a) + 0.1 * row(sp, a) + G * (row(dn, a) * n1),
        0.08 * row(s, a)
        + 0.01 * row(sp, a)
        + G * (row(dn, a) * older + back * (row(sp, b) - G * (fa - fb))),
        back,
        row(dt, a) * row(t, a),
        row(dt, a) * row(tp, a),
        G * row(dt, a),
        row(dt, b) * row(t, b),
    ]
    a, b = 0, 1
    n1 = row(np_, b) - G * (row(s, b) - row(s, a))
    fa = row(dn, a) * row(n, a)
    fb = row(dn, b) * row(n, b)
    low = [
        row(s, a),
        row(sp, a) - G * (fb - fa),
        0.8 * row(s, a) + 0.1 * row(sp, a) - G * (row(dn, b) * n1),
        row(dn, a) * row(np_, a),
        G * row(dn, a),
        row(dt, a) * row(t, a),
        row(dt, a) * row(tp, a),
        G * row(dt, a),
        fa,
    ]
    return low, high


def exchange(sides, faces, links, ph, *refs):
    fields, refs = refs[:8], refs[8:]
    (
        rims_ref, ends_ref, table_ref, diag_ref, coef_ref,
        held, pack, ends, ring, ring_ends, chosen, coef,
        load_sem, coef_sem, near_send, near_recv, diag_send, diag_recv, ring_send, ring_recv, ring_ends_send, ring_ends_recv,
        main_send, main_recv, ext_send, ext_recv, corner_send, corner_recv,
    ) = refs
    last = sides - 1
    pairs = faces // 2
    side = held.shape[1]
    w = lax.axis_index("wide")
    c = lax.axis_index("narrow")
    f = w // sides
    r = w % sides
    x, half = f // 2, f % 2
    at = lambda face, row, col: (face * sides + row, col)
    signal = lambda bar, d: pl.semaphore_signal(bar, inc=1, device_id=d, device_id_type=MESH)
    is_end = lambda q: (q == 0) | (q == last)
    corner = is_end(r) & is_end(c)
    rim = is_end(r) | is_end(c)
    inside = lambda row, col: (row >= 0) & (row <= last) & (col >= 0) & (col <= last)
    edges = [(W, c == 0, r, last), (S, r == 0, c, last), (E, c == last, r, 0), (N, r == last, c, 0)]
    ext_to = lambda q: (q + 1, q - 1, last - 1 - q, last + 1 - q)
    ext_from = lambda q: (q - 1, q + 1, last - 1 - q, last + 1 - q)
    corner_at = lambda i: at(x * 2 + i // 4, (i // 2) % 2 * last, i % 2 * last)
    me_corner = half * 4 + (r // last) * 2 + c // last
    ring_at = lambda k: at((f + 2 * k) % faces, r, c)

    bar = pltpu.get_barrier_semaphore()
    awaited = jnp.int32(0)
    for e, has, q, line in edges:

        @pl.when(has)
        def _(q=q, line=line):
            for h in range(2):
                g = x * 2 + h
                for p in (q, last - q):
                    for row, col in ((p, line), (line, p)):

                        @pl.when(~((g == f) & (row == r) & (col == c)))
                        def _(g=g, row=row, col=col):
                            signal(bar, at(g, row, col))

                for p in ext_from(q):

                    @pl.when((p >= 0) & (p <= last))
                    def _(g=g, p=p):
                        signal(bar, at(g, p, line))
                        signal(bar, at(g, line, p))

        ext = jnp.where(is_end(q), 8, 16)
        awaited += jnp.where(has, 8 + ext, 0)
    own = corner & (r != c)
    awaited -= jnp.where(own, 2, 0)

    @pl.when(rim)
    def _():
        for k in range(1, pairs):
            signal(bar, ring_at(k))

    @pl.when(corner)
    def _():
        for i in range(8):

            @pl.when(i != me_corner)
            def _(i=i):
                signal(bar, corner_at(i))

    awaited += jnp.where(rim, pairs - 1, 0) + jnp.where(corner, 7, 0)
    for dr in (-1, 0, 1):
        for dc in (-1, 0, 1):
            if (dr, dc) != (0, 0):
                there = inside(r + dr, c + dc)
                awaited += there.astype(jnp.int32)

                @pl.when(there)
                def _(dr=dr, dc=dc):
                    signal(bar, at(f, r + dr, c + dc))

    loads = [pltpu.make_async_copy(ref, held.at[k], load_sem.at[k]) for k, ref in enumerate(fields)]
    for copy in loads:
        copy.start()

    which = lax.broadcasted_iota(jnp.int32, (CONSTITUENTS, side), 0)
    count = (lax.broadcasted_iota(jnp.int32, (CONSTITUENTS, side), 1) + 1).astype(jnp.float32)
    start = jnp.zeros((CONSTITUENTS, side), jnp.float32)
    rate = jnp.zeros((CONSTITUENTS, side), jnp.float32)
    for k in range(CONSTITUENTS):
        start = jnp.where(which == k, ph[k], start)
        rate = jnp.where(which == k, jnp.float32(tide_omega[k]) * jnp.float32(step_seconds), rate)
    angle = start + rate * count
    coef[0:CONSTITUENTS, :] = jnp.cos(angle)
    coef[CONSTITUENTS:, :] = jnp.sin(angle)
    keep = pltpu.make_async_copy(coef, coef_ref, coef_sem.at[0])
    keep.start()

    for copy in loads:
        copy.wait()
    sp, s, up, u, vp, v, dw, ds = (held.at[k] for k in range(8))
    lo, hi = rims(s[...], sp[...], v[...], vp[...], u[...], up[...], ds[...], dw[...])
    for k in range(LINES):
        pack[S, k : k + 1, :] = lo[k]
        pack[N, k : k + 1, :] = hi[k]
    flip = lambda ref: jnp.transpose(ref[...])
    lo, hi = rims(flip(s), flip(sp), flip(u), flip(up), flip(v), flip(vp), flip(dw), flip(ds))
    for k in range(LINES):
        pack[W, k : k + 1, :] = lo[k]
        pack[E, k : k + 1, :] = hi[k]
    for e in range(4):
        pack[e, LINES:16, :] = jnp.zeros((16 - LINES, side), jnp.float32)
    stacked = jnp.concatenate([pack[e] for e in range(4)] + [jnp.zeros((side - 64, side), jnp.float32)], axis=0)
    turned = jnp.transpose(stacked)
    lane = lax.broadcasted_iota(jnp.int32, (1, side), 1)
    for e in range(4):
        gathered = jnp.zeros((1, side), jnp.float32)
        for k, i in enumerate((0, 1, side - 2, side - 1)):
            moved = turned[i : i + 1, :]
            by = (16 * k - 16 * e) % side
            if by:
                moved = pltpu.roll(moved, by, 1)
            gathered = jnp.where((lane >= 16 * k) & (lane < 16 * k + 16), moved, gathered)
        ends[e] = gathered
        pack[e, LINES : LINES + 1, :] = gathered

    pl.semaphore_wait(bar, awaited)

    full = pl.ds(0, LINES + 1)
    block = pl.ds(0, LINES)
    here = (w, c)
    remote = lambda a, b, ss, rs, d: pltpu.make_async_remote_copy(
        a, b, ss, rs, device_id=d, device_id_type=MESH
    )
    ring_copies = lambda e: [
        remote(pack.at[e, full], ring.at[e, k, full], ring_send.at[e, k], ring_recv.at[e, k], ring_at(k))
        for k in range(1, pairs)
    ]
    ends_copies = lambda: [
        remote(ends, ring_ends.at[k], ring_ends_send.at[k], ring_ends_recv.at[k], ring_at(k)) for k in range(1, pairs)
    ]
    for e, has, q, line in edges:

        @pl.when(has)
        def _(e=e):
            for copy in ring_copies(e):
                copy.start()

    @pl.when(corner)
    def _():
        for copy in ends_copies():
            copy.start()

    near = [(E, W, 0, 1), (N, S, 1, 0), (W, E, 0, -1), (S, N, -1, 0)]
    diagonal = [(0, 1, 1), (1, 1, -1), (2, -1, 1), (3, -1, -1)]
    near_copy = lambda e, to, dr, dc: remote(
        pack.at[e, block], rims_ref.at[to, 8, block], near_send.at[e], near_recv.at[e], at(f, r + dr, c + dc)
    )
    diag_copy = lambda k, dr, dc: remote(ends, diag_ref.at[k], diag_send.at[k], diag_recv.at[k], at(f, r + dr, c + dc))
    for e, to, dr, dc in near:

        @pl.when(inside(r + dr, c + dc))
        def _(e=e, to=to, dr=dr, dc=dc):
            near_copy(e, to, dr, dc).start()

    for k, dr, dc in diagonal:

        @pl.when(inside(r + dr, c + dc))
        def _(k=k, dr=dr, dc=dc):
            diag_copy(k, dr, dc).start()

    for e, has, q, line in edges:

        @pl.when(has)
        def _(e=e):
            for copy in ring_copies(e):
                copy.wait_recv()

    for e, has, q, line in edges:
        to_ws = e in (E, N)
        kind = 1 if e in (N, S) else 0
        lines = [(h, to) for h in range(2) for to in ((W, S) if to_ws else (E, N))]

        @pl.when(has)
        def _(e=e, q=q, line=line, kind=kind, lines=lines):
            ring[e, 0] = pack[e]
            for j, (h, to) in enumerate(lines):
                far_x = links[0, to, x * 2 + h] // 2
                chosen[e, j] = ring[e, lax.rem(x - far_x + pairs, pairs)]
            for j, (h, to) in enumerate(lines):
                g = x * 2 + h
                place = lambda p, to=to: (p, line) if to in (W, E) else (line, p)
                for par, p in enumerate((q, last - q)):
                    slot = (half * 2 + kind) * 2 + par
                    row, col = place(p)
                    mine = (g == f) & (row == r) & (col == c)

                    @pl.when(~mine)
                    def _(j=j, to=to, slot=slot, g=g, row=row, col=col):
                        remote(
                            chosen.at[e, j, block], rims_ref.at[to, slot, block], main_send.at[e], main_recv.at[to], at(g, row, col)
                        ).start()

                    @pl.when(mine)
                    def _(j=j, to=to, slot=slot):
                        pltpu.make_async_copy(chosen.at[e, j, block], rims_ref.at[to, slot, block], main_recv.at[to]).start()

            for j, (h, to) in enumerate(lines):
                g = x * 2 + h
                place = lambda p, to=to: (p, line) if to in (W, E) else (line, p)
                for kind_x, p in enumerate(ext_to(q)):
                    slot = (half * 2 + kind) * 4 + kind_x
                    row, col = place(p)

                    @pl.when((p >= 0) & (p <= last))
                    def _(j=j, to=to, slot=slot, g=g, row=row, col=col):
                        remote(
                            chosen.at[e, j, pl.ds(LINES, 1)], ends_ref.at[to, slot], ext_send.at[e], ext_recv.at[to], at(g, row, col)
                        ).start()

    corner_copy = lambda i: remote(ring_ends, table_ref.at[me_corner], corner_send.at[0], corner_recv.at[0], corner_at(i))

    @pl.when(corner)
    def _():
        for copy in ends_copies():
            copy.wait_recv()
        ring_ends[0] = ends[...]
        for i in range(8):

            @pl.when(i != me_corner)
            def _(i=i):
                corner_copy(i).start()

        pltpu.make_async_copy(ring_ends, table_ref.at[me_corner], corner_recv.at[0]).start()

    take = lambda ref, ss, rs: remote(ref, ref, ss, rs, here)
    for e, to, dr, dc in near:

        @pl.when(inside(r - dr, c - dc))
        def _(e=e, to=to):
            take(rims_ref.at[to, 8, block], near_send.at[e], near_recv.at[e]).wait_recv()

    for k, dr, dc in diagonal:

        @pl.when(inside(r - dr, c - dc))
        def _(k=k):
            take(diag_ref.at[k], diag_send.at[k], diag_recv.at[k]).wait_recv()

    for e, has, q, line in edges:

        @pl.when(has)
        def _(e=e, q=q):
            take(rims_ref.at[e, pl.ds(0, 8), block], main_send.at[0], main_recv.at[e]).wait_recv()

            @pl.when(is_end(q))
            def _():
                take(ends_ref.at[e, pl.ds(0, 8)], ext_send.at[0], ext_recv.at[e]).wait_recv()

            @pl.when(~is_end(q))
            def _():
                take(ends_ref.at[e], ext_send.at[0], ext_recv.at[e]).wait_recv()

    @pl.when(corner)
    def _():
        take(table_ref, corner_send.at[0], corner_recv.at[0]).wait_recv()

    keep.wait()
    for e, to, dr, dc in near:

        @pl.when(inside(r + dr, c + dc))
        def _(e=e, to=to, dr=dr, dc=dc):
            near_copy(e, to, dr, dc).wait_send()

    for k, dr, dc in diagonal:

        @pl.when(inside(r + dr, c + dc))
        def _(k=k, dr=dr, dc=dc):
            diag_copy(k, dr, dc).wait_send()

    for e, has, q, line in edges:

        @pl.when(has)
        def _(e=e, q=q):
            for copy in ring_copies(e):
                copy.wait_send()

            @pl.when(~own)
            def _():
                take(rims_ref.at[e, pl.ds(0, 8), block], main_send.at[e], main_recv.at[e]).wait_send()

            @pl.when(own)
            def _():
                take(rims_ref.at[e, pl.ds(0, 7), block], main_send.at[e], main_recv.at[e]).wait_send()

            @pl.when(is_end(q))
            def _():
                take(ends_ref.at[e, pl.ds(0, 8)], ext_send.at[e], ext_recv.at[e]).wait_send()

            @pl.when(~is_end(q))
            def _():
                take(ends_ref.at[e], ext_send.at[e], ext_recv.at[e]).wait_send()

    @pl.when(corner)
    def _():
        for copy in ends_copies():
            copy.wait_send()
        take(table_ref.at[pl.ds(0, 7)], corner_send.at[0], corner_recv.at[0]).wait_send()


def substeps(
    sides, faces, links, *refs
):
    fields, refs = refs[:8], refs[8:]
    (
        rims_ref, ends_ref, cx_ref, dx_ref, coef_ref, s_out, u_out, v_out, h_out,
        held, mains, exts, cx, dx, coef, levels, sums, load_sem, main_sem, ext_sem, table_sem, out_sem, sum_sem,
    ) = refs
    last = sides - 1
    side = held.shape[1]
    link = lambda face, edge, k: links[k, edge, face]
    w = lax.axis_index("wide")
    c = lax.axis_index("narrow")
    f = w // sides
    r = w % sides
    lane = lax.broadcasted_iota(jnp.int32, (1, side), 1)
    rows = lax.broadcasted_iota(jnp.int32, (side, side), 0)
    cols = lax.broadcasted_iota(jnp.int32, (side, side), 1)
    mirror = (rows + cols == side - 1).astype(jnp.float32)
    diagonal = rows == cols
    pick = lambda cond, a, b: jnp.where(cond, a, b)
    up_by = lambda x, fill: jnp.where(lane == side - 1, fill, pltpu.roll(x, side - 1, 1))
    down_by = lambda x, fill: jnp.where(lane == 0, fill, pltpu.roll(x, 1, 1))
    head = lambda x: x[:, 0:1]
    tail = lambda x: x[:, side - 1 : side]

    def end(x, k, line):
        return x[:, 16 * k + line : 16 * k + line + 1]

    def corner_of(face, edge, high):
        row = jnp.where(edge == S, 0, jnp.where(edge == N, 1, high))
        col = jnp.where(edge == W, 0, jnp.where(edge == E, 1, high))
        pairs = faces // 2
        return cx[face % 2 * 4 + row * 2 + col, lax.rem(f // 2 - face // 2 + pairs, pairs), edge]

    def at_end(x, high, k, line):
        return pick(high == 1, end(x, 3 - k, line), end(x, k, line))

    def beyond(face, edge, high):
        far, far_edge, turn = (link(face, edge, k) for k in range(3))
        stop = high ^ turn
        return at_end(corner_of(far, far_edge, stop), stop, 0, 8)

    def at_corner(face, edge, low_end, inner):
        vertical = (edge == W) | (edge == E)
        side_edge = jnp.where(vertical, S, W) if low_end else jnp.where(vertical, N, E)
        start = (edge >= E).astype(jnp.int32)
        far, far_edge, turn = (link(face, side_edge, k) for k in range(3))
        high = start ^ turn
        x = corner_of(far, far_edge, high)
        far_vertical = (far_edge == W) | (far_edge == E)
        third = beyond(far, jnp.where(far_vertical, N, E), (far_edge >= E).astype(jnp.int32))
        ahead = pick(high == 1, third, end(x, 1, 5))
        s1 = at_end(x, high, 0, 1) - G * (ahead - at_end(x, high, 0, 5))
        got = dict(s0=at_end(x, high, 0, 0), s1=s1)
        if low_end:
            got["s1"] = s1 - G * inner
        else:
            got.update(
                T0=at_end(x, high, 0, 8),
                Q=at_end(x, high, 0, 3),
                D=at_end(x, high, 0, 4),
                Tb=at_end(x, high, 1, 8),
            )
        return got

    def place(edge, to_ws):
        on_face = {W: c == 0, S: r == 0, E: c == last, N: r == last}[edge]
        across = edge in (W, E)
        seg = r if across else c
        face, partner, turn = (link(f, edge, k) for k in range(3))
        flipped = on_face & (turn == 1)
        kind = (partner == (N if to_ws else S)).astype(jnp.int32)
        q = jnp.where(turn == 1, last - seg, seg)
        slot = jnp.where(on_face, (face % 2 * 2 + kind) * 2 + turn, 8)
        slot_x = jnp.where(on_face, (face % 2 * 2 + kind) * 4 + 2 * turn, 0)
        return on_face, face, partner, flipped, q, slot, slot_x

    places = {e: place(e, e in (W, S)) for e in range(4)}
    loads = [pltpu.make_async_copy(x, held.at[k], load_sem.at[k]) for k, x in enumerate(fields)]
    tables = [
        pltpu.make_async_copy(a, b, table_sem.at[k])
        for k, (a, b) in enumerate(((cx_ref, cx), (dx_ref, dx), (coef_ref, coef)))
    ]
    arrivals = []
    for e in range(4):
        slot, slot_x = places[e][5:]
        arrivals.append(pltpu.make_async_copy(rims_ref.at[e, slot], mains.at[e], main_sem.at[e]))
        for k in range(2):
            arrivals.append(pltpu.make_async_copy(ends_ref.at[e, slot_x + k], exts.at[e, k], ext_sem.at[e, k]))
    for copy in arrivals + tables + loads:
        copy.start()
    for copy in arrivals + tables:
        copy.wait()

    def ghost(edge, to_ws):
        on_face, face, partner, flipped, q, slot, slot_x = places[edge]
        block = mains[edge]
        line = [block[k : k + 1, :] for k in range(LINES)]
        strip = (edge + 2) % 4
        lo_at, hi_at = {W: (0, 2), S: (0, 1), E: (1, 3), N: (2, 3)}[edge]
        lo_x = pick(on_face, exts[edge, 0], dx[lo_at, strip])
        hi_x = pick(on_face, exts[edge, 1], dx[hi_at, strip])
        first = head(line[5])
        lo = dict(
            s0=end(lo_x, 3, 0), s1=end(lo_x, 3, 1) - G * (first - end(lo_x, 3, 5)),
            F=end(lo_x, 3, 8), R=end(lo_x, 3, 3), Dn=end(lo_x, 3, 4), Fb=end(lo_x, 2, 8),
        )
        hi = dict(
            s0=end(hi_x, 0, 0), s1=end(hi_x, 0, 1) - G * (end(hi_x, 1, 5) - end(hi_x, 0, 5)),
            T0=end(hi_x, 0, 5), Q=end(hi_x, 0, 6), D=end(hi_x, 0, 7), Tb=end(hi_x, 0, 8),
            F=end(hi_x, 0, 8), R=end(hi_x, 0, 3), Dn=end(hi_x, 0, 4), Fb=end(hi_x, 1, 8),
        )
        lo_corner = on_face & (q == 0)
        hi_corner = on_face & (q == last)
        safe = lambda x, top: jnp.where(on_face, x, top)
        g_face, g_edge = safe(face, 0), safe(partner, E if to_ws else W)
        third_lo = at_corner(g_face, g_edge, True, first)
        third_hi = at_corner(g_face, g_edge, False, first)
        for name, value in third_lo.items():
            lo[name] = pick(lo_corner, value, lo[name])
        for name, value in third_hi.items():
            hi[name] = pick(hi_corner, value, hi[name])
        lo["done"], hi["done"] = lo_corner, hi_corner
        turned = jnp.dot(block, mirror, precision=lax.Precision.HIGHEST, preferred_element_type=jnp.float32)
        turned = [turned[k : k + 1, :] for k in range(LINES)]
        along = {5: ("T0", -1.0), 6: ("Q", -1.0), 7: ("D", 1.0)}
        if to_ws:
            along[8] = ("Tb", -1.0)
        out = []
        for k in range(LINES):
            if k in along:
                name, sign = along[k]
                other = sign * down_by(turned[k], hi[name])
            else:
                other = turned[k]
            out.append(pick(flipped, other, line[k]))
        new_lo = {n: pick(flipped, hi[n], lo[n]) for n in ("s0", "s1", "F", "R", "Dn", "Fb")}
        new_hi = {n: pick(flipped, lo[n], hi[n]) for n in ("s0", "s1", "F", "R", "Dn", "Fb")}
        for k, (name, sign) in along.items():
            new_hi[name] = pick(flipped, sign * head(line[k]), hi[name])
        new_lo["done"] = jnp.where(flipped, hi_corner, lo_corner)
        new_hi["done"] = jnp.where(flipped, lo_corner, hi_corner)
        return out, new_lo, new_hi

    (wl, w_lo, w_hi), (sl, s_lo, s_hi) = ghost(W, True), ghost(S, True)
    (el, e_lo, e_hi), (nl, n_lo, n_hi) = ghost(E, False), ghost(N, False)

    for d, x in ((w_lo, sl), (w_hi, nl), (s_lo, wl), (s_hi, el)):
        d["s1"] = pick(d["done"], d["s1"], d["s1"] - G * head(x[5]))

    west, south, east, north = c == 0, r == 0, c == last, r == last
    take_w, take_s = west & ~south, south & ~west
    sw_w = {n: pick(take_s, s_lo[n], w_lo[n]) for n in ("s0", "s1")}
    sw_s = {n: pick(take_w, w_lo[n], s_lo[n]) for n in ("s0", "s1")}
    w_lo.update(sw_w)
    s_lo.update(sw_s)
    share = (("s0", "s0"), ("s1", "s1"), ("T0", "F"), ("Q", "R"), ("D", "Dn"), ("Tb", "Fb"))
    take_e, take_s = east & ~south, south & ~east
    se_s = {a: pick(take_e, e_lo[b], s_hi[a]) for a, b in share}
    e_lo["s0"] = pick(take_s, s_hi["s0"], e_lo["s0"])
    s_hi.update(se_s)
    take_n, take_w = north & ~west, west & ~north
    nw_w = {a: pick(take_n, n_lo[b], w_hi[a]) for a, b in share}
    n_lo["s0"] = pick(take_w, w_hi["s0"], n_lo["s0"])
    w_hi.update(nw_w)
    take_e, take_n = east & ~north, north & ~east
    share = (("s0", "s0"), ("T0", "F"), ("Q", "R"), ("D", "Dn"))
    ne_n = {a: pick(take_e, e_hi[b], n_hi[a]) for a, b in share}
    ne_e = {a: pick(take_n, n_hi[b], e_hi[a]) for a, b in share}
    n_hi.update(ne_n)
    e_hi.update(ne_e)

    class HeightRim:
        def __init__(self, line, lo, hi):
            self.line, self.lo, self.hi = line, lo, hi

        def at(self, n, flux):
            s0, y1, y2, z, back, t0, q, d, tb = self.line
            lo, hi = self.lo, self.hi
            if n == 0:
                return s0
            if n == 1:
                self.s1 = y1 - G * flux - G * (up_by(t0, hi["T0"]) - t0)
                return self.s1
            if n == 2:
                self.t1 = q - d * (s0 - down_by(s0, lo["s0"]))
                self.t1hi = hi["Q"] - hi["D"] * (hi["s0"] - tail(s0))
                self.s2 = y2 + 0.1 * self.s1 - G * flux - G * (up_by(self.t1, self.t1hi) - self.t1)
                return self.s2
            s1 = self.s1
            t2 = 0.8 * t0 + 0.1 * q + 0.1 * self.t1 - d * (s1 - down_by(s1, lo["s1"]))
            t2hi = 0.8 * hi["T0"] + 0.1 * hi["Q"] + 0.1 * self.t1hi - hi["D"] * (hi["s1"] - tail(s1))
            inner = s1 + G * (up_by(tb, hi["Tb"]) - tb)
            return 0.81 * s1 + 0.1 * self.s2 + z - G * back * inner - G * flux - G * (up_by(t2, t2hi) - t2)

    class FluxRim:
        def __init__(self, line, lo, hi):
            self.line, self.lo, self.hi = line, lo, hi

        def at(self, n, height):
            s0, u1, u2, r_, d_, t0, q, d, f0 = self.line
            lo, hi = self.lo, self.hi
            if n == 0:
                return f0
            if n == 1:
                self.f1 = r_ - d_ * (s0 - height)
                return self.f1
            if n == 2:
                self.s1 = u1 - G * (up_by(t0, hi["T0"]) - t0)
                self.older = 0.8 * f0 + 0.1 * r_ + 0.1 * self.f1
                self.f2 = self.older - d_ * (self.s1 - height)
                return self.f2
            t1 = q - d * (s0 - down_by(s0, lo["s0"]))
            t1hi = hi["Q"] - hi["D"] * (hi["s0"] - tail(s0))
            s2 = u2 + 0.1 * self.s1 + G * self.f1 - G * (up_by(t1, t1hi) - t1)
            return 0.8 * self.f1 + 0.1 * self.f2 + 0.1 * self.older - d_ * (s2 - height)

    rim_w, rim_s = HeightRim(wl, w_lo, w_hi), HeightRim(sl, s_lo, s_hi)
    rim_e, rim_n = FluxRim(el, e_lo, e_hi), FluxRim(nl, n_lo, n_hi)
    as_row = lambda col: jnp.sum(jnp.where(diagonal, col, 0.0), axis=0, keepdims=True)
    as_col = lambda row: jnp.sum(jnp.where(diagonal, row, 0.0), axis=1, keepdims=True)
    for copy in loads:
        copy.wait()
    sp_, s_, up_, u_, vp_, v_, dw_, ds_ = (held[k] for k in range(8))
    first_col, last_col = cols == 0, cols == side - 1
    first_row, last_row = rows == 0, rows == side - 1
    flux_w = flux_s = height_e = height_n = None
    snaps = []
    for n in range(SUBSTEPS):
        fw, fs = dw_ * u_, ds_ * v_
        west_line, south_line = rim_w.at(n, flux_w), rim_s.at(n, flux_s)
        east_line, north_line = rim_e.at(n, height_e), rim_n.at(n, height_n)
        flux_w, flux_s = as_row(fw[:, 0:1]), fs[0:1, :]
        height_e, height_n = as_row(s_[:, side - 1 : side]), s_[side - 1 : side, :]
        fe = jnp.where(last_col, as_col(east_line), pltpu.roll(fw, side - 1, 1))
        fn = jnp.where(last_row, north_line, pltpu.roll(fs, side - 1, 0))
        sw = jnp.where(first_col, as_col(west_line), pltpu.roll(s_, 1, 1))
        ss = jnp.where(first_row, south_line, pltpu.roll(s_, 1, 0))
        s_next = sp_ - G * ((fe - fw) + (fn - fs))
        u_next = up_ - G * (s_ - sw)
        v_next = vp_ - G * (s_ - ss)
        sp_ = s_ + 0.1 * (sp_ - 2.0 * s_ + s_next)
        up_ = u_ + 0.1 * (up_ - 2.0 * u_ + u_next)
        vp_ = v_ + 0.1 * (vp_ - 2.0 * v_ + v_next)
        s_, u_, v_ = s_next, u_next, v_next
        snaps.append(s_)
    stores = []
    for k, (x, out) in enumerate(((s_, s_out), (u_, u_out), (v_, v_out))):
        levels[k] = x
        stores.append(pltpu.make_async_copy(levels.at[k], out, out_sem.at[k]))
        stores[-1].start()
    for k in range(2 * CONSTITUENTS):
        total = coef[k : k + 1, 0:1] * snaps[0]
        for n in range(1, SUBSTEPS):
            total += coef[k : k + 1, n : n + 1] * snaps[n]
        sums[k] = total
        stores.append(pltpu.make_async_copy(sums.at[k], h_out.at[k], sum_sem.at[k]))
        stores[-1].start()
    for copy in stores:
        copy.wait()


def solution(mesh):
    def body(sp, s, up, u, vp, v, dw, ds, links, ph):
        side = s.shape[0]
        sides = mesh.shape["narrow"]
        faces = mesh.shape["wide"] // sides
        f32 = jnp.float32
        shape = lambda *dims: jax.ShapeDtypeStruct(dims, f32)
        hbm = pl.BlockSpec(memory_space=pl.ANY)
        smem = pl.BlockSpec(memory_space=pltpu.SMEM)
        dma = pltpu.SemaphoreType.DMA
        links = jnp.transpose(links, (2, 1, 0))
        got = pl.pallas_call(
            functools.partial(exchange, sides, faces),
            out_shape=(
                shape(4, 9, 16, side),
                shape(4, 16, 1, side),
                shape(8, faces // 2, 4, 1, side),
                shape(4, 4, 1, side),
                shape(2 * CONSTITUENTS, side),
            ),
            in_specs=[smem] * 2 + [hbm] * 8,
            out_specs=(hbm,) * 5,
            scratch_shapes=[
                pltpu.VMEM((8, side, side), f32),
                pltpu.VMEM((4, 16, side), f32),
                pltpu.VMEM((4, 1, side), f32),
                pltpu.VMEM((4, faces // 2, 16, side), f32),
                pltpu.VMEM((faces // 2, 4, 1, side), f32),
                pltpu.VMEM((4, 4, 16, side), f32),
                pltpu.VMEM((2 * CONSTITUENTS, side), f32),
                dma((8,)), dma((1,)), dma((4,)), dma((4,)), dma((4,)), dma((4,)),
                dma((4, faces // 2)), dma((4, faces // 2)), dma((faces // 2,)), dma((faces // 2,)),
                dma((4,)), dma((4,)), dma((4,)), dma((4,)), dma((1,)), dma((1,)),
            ],
            compiler_params=pltpu.CompilerParams(collective_id=0, has_side_effects=True),
        )(links, ph, sp, s, up, u, vp, v, dw, ds)
        tile = shape(side, side)
        return pl.pallas_call(
            functools.partial(substeps, sides, faces),
            out_shape=(tile, tile, tile, shape(2 * CONSTITUENTS, side, side)),
            in_specs=[smem] + [hbm] * 13,
            out_specs=(hbm,) * 4,
            scratch_shapes=[
                pltpu.VMEM((8, side, side), f32),
                pltpu.VMEM((4, 16, side), f32),
                pltpu.VMEM((4, 2, 1, side), f32),
                pltpu.VMEM((8, faces // 2, 4, 1, side), f32),
                pltpu.VMEM((4, 4, 1, side), f32),
                pltpu.VMEM((2 * CONSTITUENTS, side), f32),
                pltpu.VMEM((3, side, side), f32),
                pltpu.VMEM((2 * CONSTITUENTS, side, side), f32),
                dma((8,)),
                dma((4,)),
                dma((4, 2)),
                dma((3,)),
                dma((3,)),
                dma((2 * CONSTITUENTS,)),
            ],
        )(links, sp, s, up, u, vp, v, dw, ds, *got)

    tiles = P("wide", "narrow")
    return jax.shard_map(
        body,
        mesh=mesh,
        in_specs=(tiles,) * 8 + (P(), P()),
        out_specs=(tiles, tiles, tiles, P(None, "wide", "narrow")),
        check_vma=False,
    )
```

```python
import functools

import jax
import jax.numpy as jnp
from jax import lax
from jax.experimental import pallas as pl
from jax.experimental.pallas import tpu as pltpu
from jax.sharding import PartitionSpec as P

MESH = pl.DeviceIdType.MESH
SUBSTEPS = 4
CONSTITUENTS = 8
tide_omega = (
    0.0001405189,
    0.0001454441,
    0.0001378797,
    0.0001458423,
    7.292117e-05,
    6.759774e-05,
    7.251056e-05,
    6.495854e-05,
)
step_seconds = 25.0
G = 0.6
W, S, E, N = range(4)
LINES = 9


def rims(s, sp, n, np_, t, tp, dn, dt):
    last = s.shape[0] - 1
    row = lambda x, i: x[i : i + 1, :]
    a, b = last, last - 1
    n1 = row(np_, a) - G * (row(s, a) - row(s, b))
    fa = row(dn, a) * row(n, a)
    fb = row(dn, b) * row(n, b)
    back = G * row(dn, a)
    older = 0.8 * row(n, a) + 0.1 * row(np_, a) + 0.1 * n1
    high = [
        row(s, a),
        row(sp, a) + G * fa,
        0.8 * row(s, a) + 0.1 * row(sp, a) + G * (row(dn, a) * n1),
        0.08 * row(s, a)
        + 0.01 * row(sp, a)
        + G * (row(dn, a) * older + back * (row(sp, b) - G * (fa - fb))),
        back,
        row(dt, a) * row(t, a),
        row(dt, a) * row(tp, a),
        G * row(dt, a),
        row(dt, b) * row(t, b),
    ]
    a, b = 0, 1
    n1 = row(np_, b) - G * (row(s, b) - row(s, a))
    fa = row(dn, a) * row(n, a)
    fb = row(dn, b) * row(n, b)
    low = [
        row(s, a),
        row(sp, a) - G * (fb - fa),
        0.8 * row(s, a) + 0.1 * row(sp, a) - G * (row(dn, b) * n1),
        row(dn, a) * row(np_, a),
        G * row(dn, a),
        row(dt, a) * row(t, a),
        row(dt, a) * row(tp, a),
        G * row(dt, a),
        fa,
    ]
    return low, high


def exchange(sides, faces, links_ref, ph_ref, *refs):
    fields, refs = refs[:8], refs[8:]
    (
        picked, coef,
        links, ph, rims_ref, ends_ref, table_ref, diag_ref,
        held, pack, ends, ring, ring_ends, chosen,
        load_sem, links_sem, near_send, near_recv, diag_send, diag_recv, ring_send, ring_recv, ring_ends_send, ring_ends_recv,
        main_send, main_recv, ext_send, ext_recv, corner_send, corner_recv,
    ) = refs
    last = sides - 1
    pairs = faces // 2
    side = held.shape[1]
    w = lax.axis_index("wide")
    c = lax.axis_index("narrow")
    f = w // sides
    r = w % sides
    x, half = f // 2, f % 2
    at = lambda face, row, col: (face * sides + row, col)
    signal = lambda bar, d: pl.semaphore_signal(bar, inc=1, device_id=d, device_id_type=MESH)
    is_end = lambda q: (q == 0) | (q == last)
    corner = is_end(r) & is_end(c)
    rim = is_end(r) | is_end(c)
    inside = lambda row, col: (row >= 0) & (row <= last) & (col >= 0) & (col <= last)
    edges = [(W, c == 0, r, last), (S, r == 0, c, last), (E, c == last, r, 0), (N, r == last, c, 0)]
    ext_to = lambda q: (q + 1, q - 1, last - 1 - q, last + 1 - q)
    ext_from = lambda q: (q - 1, q + 1, last - 1 - q, last + 1 - q)
    corner_at = lambda i: at(x * 2 + i // 4, (i // 2) % 2 * last, i % 2 * last)
    me_corner = half * 4 + (r // last) * 2 + c // last
    ring_at = lambda k: at((f + 2 * k) % faces, r, c)

    bar = pltpu.get_barrier_semaphore()
    awaited = jnp.int32(0)
    for e, has, q, line in edges:

        @pl.when(has)
        def _(q=q, line=line):
            for h in range(2):
                g = x * 2 + h
                for p in (q, last - q):
                    for row, col in ((p, line), (line, p)):

                        @pl.when(~((g == f) & (row == r) & (col == c)))
                        def _(g=g, row=row, col=col):
                            signal(bar, at(g, row, col))

                for p in ext_from(q):

                    @pl.when((p >= 0) & (p <= last))
                    def _(g=g, p=p):
                        signal(bar, at(g, p, line))
                        signal(bar, at(g, line, p))

        ext = jnp.where(is_end(q), 8, 16)
        awaited += jnp.where(has, 8 + ext, 0)
    own = corner & (r != c)
    awaited -= jnp.where(own, 2, 0)

    @pl.when(rim)
    def _():
        for k in range(1, pairs):
            signal(bar, ring_at(k))

    @pl.when(corner)
    def _():
        for i in range(8):

            @pl.when(i != me_corner)
            def _(i=i):
                signal(bar, corner_at(i))

    awaited += jnp.where(rim, pairs - 1, 0) + jnp.where(corner, 7, 0)
    for dr in (-1, 0, 1):
        for dc in (-1, 0, 1):
            if (dr, dc) != (0, 0):
                there = inside(r + dr, c + dc)
                awaited += there.astype(jnp.int32)

                @pl.when(there)
                def _(dr=dr, dc=dc):
                    signal(bar, at(f, r + dr, c + dc))

    loads = [
        pltpu.make_async_copy(ph_ref, ph, links_sem.at[0]),
        pltpu.make_async_copy(links_ref, links, links_sem.at[1]),
    ] + [pltpu.make_async_copy(ref, held.at[k], load_sem.at[k]) for k, ref in enumerate(fields)]
    for copy in loads:
        copy.start()
    for copy in loads:
        copy.wait()

    which = lax.broadcasted_iota(jnp.int32, (CONSTITUENTS, side), 0)
    count = (lax.broadcasted_iota(jnp.int32, (CONSTITUENTS, side), 1) + 1).astype(jnp.float32)
    start = jnp.zeros((CONSTITUENTS, side), jnp.float32)
    rate = jnp.zeros((CONSTITUENTS, side), jnp.float32)
    for k in range(CONSTITUENTS):
        start = jnp.where(which == k, ph[k], start)
        rate = jnp.where(which == k, jnp.float32(tide_omega[k]) * jnp.float32(step_seconds), rate)
    angle = start + rate * count
    coef[0:CONSTITUENTS, :] = jnp.cos(angle)
    coef[CONSTITUENTS:, :] = jnp.sin(angle)

    sp, s, up, u, vp, v, dw, ds = (held.at[k] for k in range(8))
    lo, hi = rims(s[...], sp[...], v[...], vp[...], u[...], up[...], ds[...], dw[...])
    for k in range(LINES):
        pack[S, 0, k : k + 1, :] = lo[k]
        pack[N, 0, k : k + 1, :] = hi[k]
    flip = lambda ref: jnp.transpose(ref[...])
    lo, hi = rims(flip(s), flip(sp), flip(u), flip(up), flip(v), flip(vp), flip(dw), flip(ds))
    for k in range(LINES):
        pack[W, 0, k : k + 1, :] = lo[k]
        pack[E, 0, k : k + 1, :] = hi[k]
    for e in range(4):
        pack[e, 0, LINES:16, :] = jnp.full((16 - LINES, side), G, jnp.float32)
    whole = jnp.concatenate([pack[e, 0] for e in range(4)], axis=0)
    stacked = jnp.concatenate([whole, jnp.zeros((side - 64, side), jnp.float32)], axis=0)
    turned = jnp.transpose(stacked)
    lane = lax.broadcasted_iota(jnp.int32, (1, side), 1)
    for e in range(4):
        gathered = jnp.zeros((1, side), jnp.float32)
        for k, i in enumerate((0, 1, side - 2, side - 1)):
            moved = turned[i : i + 1, :]
            by = (16 * k - 16 * e) % side
            if by:
                moved = pltpu.roll(moved, by, 1)
            gathered = jnp.where((lane >= 16 * k) & (lane < 16 * k + 16), moved, gathered)
        ends[e] = gathered
        for k in range(2):
            pack[e, k, LINES : LINES + 1, :] = gathered
    total = lax.broadcasted_iota(jnp.int32, (side, side), 0) + lax.broadcasted_iota(jnp.int32, (side, side), 1)
    mirror = (total == side - 1).astype(jnp.float32)
    turned = jnp.dot(whole, mirror, precision=lax.Precision.HIGHEST, preferred_element_type=jnp.float32)
    for e in range(4):
        for k in range(LINES):
            line_k = turned[16 * e + k : 16 * e + k + 1, :]
            if k in (5, 6, 7) or (k == 8 and e in (E, N)):
                line_k = jnp.where(lane == 0, 0.0, pltpu.roll(line_k, 1, 1))
                line_k = line_k if k == 7 else -line_k
            pack[e, 1, k : k + 1, :] = line_k

    pl.semaphore_wait(bar, awaited)

    full = pl.ds(0, LINES + 1)
    block = full
    here = (w, c)
    remote = lambda a, b, ss, rs, d: pltpu.make_async_remote_copy(
        a, b, ss, rs, device_id=d, device_id_type=MESH
    )
    ring_copies = lambda e: [
        remote(pack.at[e, :, full], ring.at[e, k, :, full], ring_send.at[e, k], ring_recv.at[e, k], ring_at(k))
        for k in range(1, pairs)
    ]
    ends_copies = lambda: [
        remote(ends, ring_ends.at[k], ring_ends_send.at[k], ring_ends_recv.at[k], ring_at(k)) for k in range(1, pairs)
    ]
    for e, has, q, line in edges:

        @pl.when(has)
        def _(e=e):
            for copy in ring_copies(e):
                copy.start()

    @pl.when(corner)
    def _():
        for copy in ends_copies():
            copy.start()

    near = [(E, W, 0, 1), (N, S, 1, 0), (W, E, 0, -1), (S, N, -1, 0)]
    diagonal = [(0, 1, 1), (1, 1, -1), (2, -1, 1), (3, -1, -1)]
    near_copy = lambda e, to, dr, dc: remote(
        pack.at[e, 0, block], rims_ref.at[to, 8, block], near_send.at[e], near_recv.at[e], at(f, r + dr, c + dc)
    )
    diag_copy = lambda k, dr, dc: remote(ends, diag_ref.at[k], diag_send.at[k], diag_recv.at[k], at(f, r + dr, c + dc))
    for e, to, dr, dc in near:

        @pl.when(inside(r + dr, c + dc))
        def _(e=e, to=to, dr=dr, dc=dc):
            near_copy(e, to, dr, dc).start()

    for k, dr, dc in diagonal:

        @pl.when(inside(r + dr, c + dc))
        def _(k=k, dr=dr, dc=dc):
            diag_copy(k, dr, dc).start()

    for e, has, q, line in edges:

        @pl.when(has)
        def _(e=e):
            for copy in ring_copies(e):
                copy.wait_recv()

    for e, has, q, line in edges:
        to_ws = e in (E, N)
        kind = 1 if e in (N, S) else 0
        lines = [(h, to) for h in range(2) for to in ((W, S) if to_ws else (E, N))]

        @pl.when(has)
        def _(e=e, q=q, line=line, kind=kind, lines=lines):
            ring[e, 0] = pack[e]
            for j, (h, to) in enumerate(lines):
                far_x = links[0, to, x * 2 + h] // 2
                chosen[e, j] = ring[e, lax.rem(x - far_x + pairs, pairs), links[2, to, x * 2 + h]]
            for j, (h, to) in enumerate(lines):
                g = x * 2 + h
                place = lambda p, to=to: (p, line) if to in (W, E) else (line, p)
                for par, p in enumerate((q, last - q)):
                    slot = (half * 2 + kind) * 2 + par
                    row, col = place(p)
                    mine = (g == f) & (row == r) & (col == c)

                    @pl.when(~mine)
                    def _(j=j, to=to, slot=slot, g=g, row=row, col=col):
                        remote(
                            chosen.at[e, j, block], rims_ref.at[to, slot, block], main_send.at[e], main_recv.at[to], at(g, row, col)
                        ).start()

                    @pl.when(mine)
                    def _(j=j, to=to, slot=slot):
                        pltpu.make_async_copy(chosen.at[e, j, block], rims_ref.at[to, slot, block], main_recv.at[to]).start()

            for j, (h, to) in enumerate(lines):
                g = x * 2 + h
                place = lambda p, to=to: (p, line) if to in (W, E) else (line, p)
                for kind_x, p in enumerate(ext_to(q)):
                    slot = (half * 2 + kind) * 4 + kind_x
                    row, col = place(p)

                    @pl.when((p >= 0) & (p <= last))
                    def _(j=j, to=to, slot=slot, g=g, row=row, col=col):
                        remote(
                            chosen.at[e, j, pl.ds(LINES, 1)], ends_ref.at[to, slot], ext_send.at[e], ext_recv.at[to], at(g, row, col)
                        ).start()

    corner_copy = lambda i: remote(ring_ends, table_ref.at[me_corner], corner_send.at[0], corner_recv.at[0], corner_at(i))

    @pl.when(corner)
    def _():
        for copy in ends_copies():
            copy.wait_recv()
        ring_ends[0] = ends[...]
        for i in range(8):

            @pl.when(i != me_corner)
            def _(i=i):
                corner_copy(i).start()

        pltpu.make_async_copy(ring_ends, table_ref.at[me_corner], corner_recv.at[0]).start()

    take = lambda ref, ss, rs: remote(ref, ref, ss, rs, here)
    for e, to, dr, dc in near:

        @pl.when(inside(r - dr, c - dc))
        def _(e=e, to=to):
            take(rims_ref.at[to, 8, block], near_send.at[e], near_recv.at[e]).wait_recv()

    for k, dr, dc in diagonal:

        @pl.when(inside(r - dr, c - dc))
        def _(k=k):
            take(diag_ref.at[k], diag_send.at[k], diag_recv.at[k]).wait_recv()

    for e, has, q, line in edges:

        @pl.when(has)
        def _(e=e, q=q):
            take(rims_ref.at[e, pl.ds(0, 8), block], main_send.at[0], main_recv.at[e]).wait_recv()

            @pl.when(is_end(q))
            def _():
                take(ends_ref.at[e, pl.ds(0, 8)], ext_send.at[0], ext_recv.at[e]).wait_recv()

            @pl.when(~is_end(q))
            def _():
                take(ends_ref.at[e], ext_send.at[0], ext_recv.at[e]).wait_recv()

    @pl.when(corner)
    def _():
        take(table_ref, corner_send.at[0], corner_recv.at[0]).wait_recv()

    link = lambda face, edge, k: links[k, edge, face]
    end = lambda row, k, line: row[:, 16 * k + line : 16 * k + line + 1]
    at_end = lambda row, high, k, line: jnp.where(high == 1, end(row, 3 - k, line), end(row, k, line))

    def corner_of(face, edge, high):
        row = jnp.where(edge == S, 0, jnp.where(edge == N, 1, high))
        col = jnp.where(edge == W, 0, jnp.where(edge == E, 1, high))
        return table_ref[face % 2 * 4 + row * 2 + col, lax.rem(x - face // 2 + pairs, pairs), edge]

    def beyond(face, edge, high):
        far, far_edge, turn = (link(face, edge, k) for k in range(3))
        stop = high ^ turn
        return at_end(corner_of(far, far_edge, stop), stop, 0, 8)

    def at_corner(face, edge, low_end):
        vertical = (edge == W) | (edge == E)
        side_edge = jnp.where(vertical, S, W) if low_end else jnp.where(vertical, N, E)
        start = (edge >= E).astype(jnp.int32)
        far, far_edge, turn = (link(face, side_edge, k) for k in range(3))
        high = start ^ turn
        row = corner_of(far, far_edge, high)
        far_vertical = (far_edge == W) | (far_edge == E)
        third = beyond(far, jnp.where(far_vertical, N, E), (far_edge >= E).astype(jnp.int32))
        ahead = jnp.where(high == 1, third, end(row, 1, 5))
        s1 = at_end(row, high, 0, 1) - G * (ahead - at_end(row, high, 0, 5))
        if low_end:
            parts = {(3, 0): at_end(row, high, 0, 0), (3, 1): s1}
        else:
            parts = {(0, 0): at_end(row, high, 0, 0)}
            across = at_end(row, high, 0, 8)
            parts.update({(0, 1): s1, (0, 5): across, (1, 5): across, (0, 6): at_end(row, high, 0, 3)})
            parts.update({(0, 7): at_end(row, high, 0, 4), (0, 8): at_end(row, high, 1, 8)})
        made = jnp.zeros((1, side), jnp.float32)
        for (k, line), value in parts.items():
            made = jnp.where(lane == 16 * k + line, value, made)
        return made

    for e, on_face, seg, _ in edges:
        to_ws = e in (W, S)
        across = e in (W, E)
        face, partner, turn = (link(f, e, k) for k in range(3))
        kind = (partner == (N if to_ws else S)).astype(jnp.int32)
        q = jnp.where(turn == 1, last - seg, seg)
        slot = jnp.where(on_face, (face % 2 * 2 + kind) * 2 + turn, 8)
        slot_x = jnp.where(on_face, (face % 2 * 2 + kind) * 4 + 2 * turn, 0)
        strip = (e + 2) % 4
        lo_at, hi_at = {W: (0, 2), S: (0, 1), E: (1, 3), N: (2, 3)}[e]
        picked[e] = rims_ref[e, slot]
        picked[e, 10:11, :] = jnp.where(on_face, ends_ref[e, slot_x], diag_ref[lo_at, strip])
        picked[e, 11:12, :] = jnp.where(on_face, ends_ref[e, slot_x + 1], diag_ref[hi_at, strip])
        flag = jnp.where(on_face, turn, 0).astype(jnp.float32)
        picked[e, 12:13, :] = jnp.zeros((1, side), jnp.float32) + flag

        @pl.when(corner & on_face)
        def _(e=e, face=face, partner=partner, q=q):
            picked[e, 10:11, :] = jnp.where(q == 0, at_corner(face, partner, True), picked[e, 10:11, :])
            picked[e, 11:12, :] = jnp.where(q == last, at_corner(face, partner, False), picked[e, 11:12, :])

    for e, to, dr, dc in near:

        @pl.when(inside(r + dr, c + dc))
        def _(e=e, to=to, dr=dr, dc=dc):
            near_copy(e, to, dr, dc).wait_send()

    for k, dr, dc in diagonal:

        @pl.when(inside(r + dr, c + dc))
        def _(k=k, dr=dr, dc=dc):
            diag_copy(k, dr, dc).wait_send()

    for e, has, q, line in edges:

        @pl.when(has)
        def _(e=e, q=q):
            for copy in ring_copies(e):
                copy.wait_send()

            @pl.when(~own)
            def _():
                take(rims_ref.at[e, pl.ds(0, 8), block], main_send.at[e], main_recv.at[e]).wait_send()

            @pl.when(own)
            def _():
                take(rims_ref.at[e, pl.ds(0, 7), block], main_send.at[e], main_recv.at[e]).wait_send()

            @pl.when(is_end(q))
            def _():
                take(ends_ref.at[e, pl.ds(0, 8)], ext_send.at[e], ext_recv.at[e]).wait_send()

            @pl.when(~is_end(q))
            def _():
                take(ends_ref.at[e], ext_send.at[e], ext_recv.at[e]).wait_send()

    @pl.when(corner)
    def _():
        for copy in ends_copies():
            copy.wait_send()
        take(table_ref.at[pl.ds(0, 7)], corner_send.at[0], corner_recv.at[0]).wait_send()


def substeps(sides, picked, coef, *refs):
    fields, refs = refs[:8], refs[8:]
    s_out, u_out, v_out, h_out, levels, sums, out_sem, sum_sem = refs
    last = sides - 1
    side = levels.shape[1]
    c = lax.axis_index("narrow")
    r = lax.rem(lax.axis_index("wide"), sides)
    lane = lax.broadcasted_iota(jnp.int32, (1, side), 1)
    rows = lax.broadcasted_iota(jnp.int32, (side, side), 0)
    cols = lax.broadcasted_iota(jnp.int32, (side, side), 1)
    diagonal = rows == cols
    pick = lambda cond, a, b: jnp.where(cond, a, b)
    up_by = lambda x, fill: jnp.where(lane == side - 1, fill, pltpu.roll(x, side - 1, 1))
    down_by = lambda x, fill: jnp.where(lane == 0, fill, pltpu.roll(x, 1, 1))
    head = lambda x: x[:, 0:1]
    tail = lambda x: x[:, side - 1 : side]
    end = lambda row, k, line: row[:, 16 * k + line : 16 * k + line + 1]

    def ghost(edge, to_ws):
        block = picked[edge]
        line = [block[k : k + 1, :] for k in range(LINES)]
        own, lo_x, hi_x = (block[k : k + 1, :] for k in (9, 10, 11))
        flipped = block[12:13, 0:1] > 0.5
        lo = dict(
            s0=end(lo_x, 3, 0), s1=end(lo_x, 3, 1) - G * (end(own, 0, 5) - end(lo_x, 3, 5)),
            F=end(lo_x, 3, 8), R=end(lo_x, 3, 3), Dn=end(lo_x, 3, 4), Fb=end(lo_x, 2, 8), g=end(lo_x, 3, 15),
        )
        hi = dict(
            s0=end(hi_x, 0, 0), s1=end(hi_x, 0, 1) - G * (end(hi_x, 1, 5) - end(hi_x, 0, 5)),
            T0=end(hi_x, 0, 5), Q=end(hi_x, 0, 6), D=end(hi_x, 0, 7), Tb=end(hi_x, 0, 8),
            F=end(hi_x, 0, 8), R=end(hi_x, 0, 3), Dn=end(hi_x, 0, 4), Fb=end(hi_x, 1, 8), g=end(hi_x, 0, 15),
        )
        shared = ("s0", "s1", "F", "R", "Dn", "Fb", "g")
        new_lo = {n: pick(flipped, hi[n], lo[n]) for n in shared}
        new_hi = {n: pick(flipped, lo[n], hi[n]) for n in shared}
        along = {5: ("T0", -1.0), 6: ("Q", -1.0), 7: ("D", 1.0)}
        if to_ws:
            along[8] = ("Tb", -1.0)
        for k, (name, sign) in along.items():
            line[k] = pick((lane == 0) & flipped, sign * hi[name], line[k])
            new_hi[name] = pick(flipped, sign * end(own, 0, k), hi[name])
        return line, new_lo, new_hi

    (wl, w_lo, w_hi), (sl, s_lo, s_hi) = ghost(W, True), ghost(S, True)
    (el, e_lo, e_hi), (nl, n_lo, n_hi) = ghost(E, False), ghost(N, False)

    for d, x in ((w_lo, sl), (w_hi, nl), (s_lo, wl), (s_hi, el)):
        d["s1"] = d["s1"] - d["g"] * head(x[5])

    west, south, east, north = c == 0, r == 0, c == last, r == last
    take_w, take_s = west & ~south, south & ~west
    sw_w = {n: pick(take_s, s_lo[n], w_lo[n]) for n in ("s0", "s1")}
    sw_s = {n: pick(take_w, w_lo[n], s_lo[n]) for n in ("s0", "s1")}
    w_lo.update(sw_w)
    s_lo.update(sw_s)
    share = (("s0", "s0"), ("s1", "s1"), ("T0", "F"), ("Q", "R"), ("D", "Dn"), ("Tb", "Fb"))
    take_e, take_s = east & ~south, south & ~east
    se_s = {a: pick(take_e, e_lo[b], s_hi[a]) for a, b in share}
    e_lo["s0"] = pick(take_s, s_hi["s0"], e_lo["s0"])
    s_hi.update(se_s)
    take_n, take_w = north & ~west, west & ~north
    nw_w = {a: pick(take_n, n_lo[b], w_hi[a]) for a, b in share}
    n_lo["s0"] = pick(take_w, w_hi["s0"], n_lo["s0"])
    w_hi.update(nw_w)
    take_e, take_n = east & ~north, north & ~east
    share = (("s0", "s0"), ("T0", "F"), ("Q", "R"), ("D", "Dn"))
    ne_n = {a: pick(take_e, e_hi[b], n_hi[a]) for a, b in share}
    ne_e = {a: pick(take_n, n_hi[b], e_hi[a]) for a, b in share}
    n_hi.update(ne_n)
    e_hi.update(ne_e)

    class HeightRim:
        def __init__(self, line, lo, hi):
            self.line, self.lo, self.hi = line, lo, hi

        def at(self, n, flux):
            s0, y1, y2, z, back, t0, q, d, tb = self.line
            lo, hi = self.lo, self.hi
            if n == 0:
                return s0
            if n == 1:
                self.s1 = y1 - G * flux - G * (up_by(t0, hi["T0"]) - t0)
                return self.s1
            if n == 2:
                self.t1 = q - d * (s0 - down_by(s0, lo["s0"]))
                self.t1hi = hi["Q"] - hi["D"] * (hi["s0"] - tail(s0))
                self.s2 = y2 + 0.1 * self.s1 - G * flux - G * (up_by(self.t1, self.t1hi) - self.t1)
                return self.s2
            s1 = self.s1
            t2 = 0.8 * t0 + 0.1 * q + 0.1 * self.t1 - d * (s1 - down_by(s1, lo["s1"]))
            t2hi = 0.8 * hi["T0"] + 0.1 * hi["Q"] + 0.1 * self.t1hi - hi["D"] * (hi["s1"] - tail(s1))
            inner = s1 + G * (up_by(tb, hi["Tb"]) - tb)
            return 0.81 * s1 + 0.1 * self.s2 + z - G * back * inner - G * flux - G * (up_by(t2, t2hi) - t2)

    class FluxRim:
        def __init__(self, line, lo, hi):
            self.line, self.lo, self.hi = line, lo, hi

        def at(self, n, height):
            s0, u1, u2, r_, d_, t0, q, d, f0 = self.line
            lo, hi = self.lo, self.hi
            if n == 0:
                return f0
            if n == 1:
                self.f1 = r_ - d_ * (s0 - height)
                return self.f1
            if n == 2:
                self.s1 = u1 - G * (up_by(t0, hi["T0"]) - t0)
                self.older = 0.8 * f0 + 0.1 * r_ + 0.1 * self.f1
                self.f2 = self.older - d_ * (self.s1 - height)
                return self.f2
            t1 = q - d * (s0 - down_by(s0, lo["s0"]))
            t1hi = hi["Q"] - hi["D"] * (hi["s0"] - tail(s0))
            s2 = u2 + 0.1 * self.s1 + G * self.f1 - G * (up_by(t1, t1hi) - t1)
            return 0.8 * self.f1 + 0.1 * self.f2 + 0.1 * self.older - d_ * (s2 - height)

    rim_w, rim_s = HeightRim(wl, w_lo, w_hi), HeightRim(sl, s_lo, s_hi)
    rim_e, rim_n = FluxRim(el, e_lo, e_hi), FluxRim(nl, n_lo, n_hi)
    as_row = lambda col: jnp.sum(jnp.where(diagonal, col, 0.0), axis=0, keepdims=True)
    as_col = lambda row: jnp.sum(jnp.where(diagonal, row, 0.0), axis=1, keepdims=True)
    sp_, s_, up_, u_, vp_, v_, dw_, ds_ = (x[...] for x in fields)
    first_col, last_col = cols == 0, cols == side - 1
    first_row, last_row = rows == 0, rows == side - 1
    flux_w = flux_s = height_e = height_n = None
    snaps = []
    for n in range(SUBSTEPS):
        fw, fs = dw_ * u_, ds_ * v_
        west_line, south_line = rim_w.at(n, flux_w), rim_s.at(n, flux_s)
        east_line, north_line = rim_e.at(n, height_e), rim_n.at(n, height_n)
        flux_w, flux_s = as_row(fw[:, 0:1]), fs[0:1, :]
        height_e, height_n = as_row(s_[:, side - 1 : side]), s_[side - 1 : side, :]
        fe = jnp.where(last_col, as_col(east_line), pltpu.roll(fw, side - 1, 1))
        fn = jnp.where(last_row, north_line, pltpu.roll(fs, side - 1, 0))
        sw = jnp.where(first_col, as_col(west_line), pltpu.roll(s_, 1, 1))
        ss = jnp.where(first_row, south_line, pltpu.roll(s_, 1, 0))
        s_next = sp_ - G * ((fe - fw) + (fn - fs))
        u_next = up_ - G * (s_ - sw)
        v_next = vp_ - G * (s_ - ss)
        sp_ = s_ + 0.1 * (sp_ - 2.0 * s_ + s_next)
        up_ = u_ + 0.1 * (up_ - 2.0 * u_ + u_next)
        vp_ = v_ + 0.1 * (vp_ - 2.0 * v_ + v_next)
        s_, u_, v_ = s_next, u_next, v_next
        snaps.append(s_)
    stores = []
    for k, (x, out) in enumerate(((s_, s_out), (u_, u_out), (v_, v_out))):
        levels[k] = x
        stores.append(pltpu.make_async_copy(levels.at[k], out, out_sem.at[k]))
        stores[-1].start()
    for k in range(2 * CONSTITUENTS):
        total = coef[k : k + 1, 0:1] * snaps[0]
        for n in range(1, SUBSTEPS):
            total += coef[k : k + 1, n : n + 1] * snaps[n]
        sums[k] = total
        stores.append(pltpu.make_async_copy(sums.at[k], h_out.at[k], sum_sem.at[k]))
        stores[-1].start()
    for copy in stores:
        copy.wait()


def solution(mesh):
    def body(sp, s, up, u, vp, v, dw, ds, links, ph):
        side = s.shape[0]
        sides = mesh.shape["narrow"]
        faces = mesh.shape["wide"] // sides
        f32 = jnp.float32
        shape = lambda *dims: jax.ShapeDtypeStruct(dims, f32)
        hbm = pl.BlockSpec(memory_space=pl.ANY)
        vmem = pl.BlockSpec(memory_space=pltpu.VMEM)
        dma = pltpu.SemaphoreType.DMA
        scratch = lambda *dims: pltpu.VMEM(dims, f32)
        pairs = faces // 2
        links = jnp.transpose(links, (2, 1, 0))
        fields = (sp, s, up, u, vp, v, dw, ds)
        grant = 8 << 20
        in_hbm = [pltpu.with_memory_space_constraint(a, pltpu.HBM) for a in (links, ph, *fields)]
        got = pl.pallas_call(
            functools.partial(exchange, sides, faces),
            out_shape=(shape(4, 16, side), shape(2 * CONSTITUENTS, side)),
            in_specs=[hbm] * 10,
            out_specs=(vmem,) * 2,
            scratch_shapes=[
                pltpu.SMEM(links.shape, jnp.int32),
                pltpu.SMEM(ph.shape, f32),
                scratch(4, 9, 16, side),
                scratch(4, 16, 1, side),
                scratch(8, pairs, 4, 1, side),
                scratch(4, 4, 1, side),
                scratch(8, side, side),
                scratch(4, 2, 16, side),
                scratch(4, 1, side),
                scratch(4, pairs, 2, 16, side),
                scratch(pairs, 4, 1, side),
                scratch(4, 4, 16, side),
                dma((8,)), dma((2,)), dma((4,)), dma((4,)), dma((4,)), dma((4,)),
                dma((4, pairs)), dma((4, pairs)), dma((pairs,)), dma((pairs,)),
                dma((4,)), dma((4,)), dma((4,)), dma((4,)), dma((1,)), dma((1,)),
            ],
            compiler_params=pltpu.CompilerParams(collective_id=0, has_side_effects=True, vmem_limit_bytes=grant),
        )(*in_hbm)
        tile = shape(side, side)
        return pl.pallas_call(
            functools.partial(substeps, sides),
            out_shape=(tile, tile, tile, shape(2 * CONSTITUENTS, side, side)),
            in_specs=[vmem] * 10,
            out_specs=(hbm,) * 4,
            scratch_shapes=[scratch(3, side, side), scratch(2 * CONSTITUENTS, side, side), dma((3,)), dma((2 * CONSTITUENTS,))],
            compiler_params=pltpu.CompilerParams(vmem_limit_bytes=grant),
        )(*got, *fields)

    tiles = P("wide", "narrow")
    return jax.shard_map(
        body,
        mesh=mesh,
        in_specs=(tiles,) * 8 + (P(), P()),
        out_specs=(tiles, tiles, tiles, P(None, "wide", "narrow")),
        check_vma=False,
    )
```

```python
import functools

import jax
import jax.numpy as jnp
from jax import lax
from jax.experimental import pallas as pl
from jax.experimental.pallas import tpu as pltpu
from jax.sharding import PartitionSpec as P

MESH = pl.DeviceIdType.MESH
SUBSTEPS = 4
CONSTITUENTS = 8
tide_omega = (
    0.0001405189,
    0.0001454441,
    0.0001378797,
    0.0001458423,
    7.292117e-05,
    6.759774e-05,
    7.251056e-05,
    6.495854e-05,
)
step_seconds = 25.0
G = 0.6
W, S, E, N = range(4)
LINES = 9


def rims(s, sp, n, np_, t, tp, dn, dt):
    last = s.shape[0] - 1
    row = lambda x, i: x[i : i + 1, :]
    a, b = last, last - 1
    n1 = row(np_, a) - G * (row(s, a) - row(s, b))
    fa = row(dn, a) * row(n, a)
    fb = row(dn, b) * row(n, b)
    back = G * row(dn, a)
    older = 0.8 * row(n, a) + 0.1 * row(np_, a) + 0.1 * n1
    high = [
        row(s, a),
        row(sp, a) + G * fa,
        0.8 * row(s, a) + 0.1 * row(sp, a) + G * (row(dn, a) * n1),
        0.08 * row(s, a)
        + 0.01 * row(sp, a)
        + G * (row(dn, a) * older + back * (row(sp, b) - G * (fa - fb))),
        back,
        row(dt, a) * row(t, a),
        row(dt, a) * row(tp, a),
        G * row(dt, a),
        row(dt, b) * row(t, b),
    ]
    a, b = 0, 1
    n1 = row(np_, b) - G * (row(s, b) - row(s, a))
    fa = row(dn, a) * row(n, a)
    fb = row(dn, b) * row(n, b)
    low = [
        row(s, a),
        row(sp, a) - G * (fb - fa),
        0.8 * row(s, a) + 0.1 * row(sp, a) - G * (row(dn, b) * n1),
        row(dn, a) * row(np_, a),
        G * row(dn, a),
        row(dt, a) * row(t, a),
        row(dt, a) * row(tp, a),
        G * row(dt, a),
        fa,
    ]
    return low, high


def exchange(sides, faces, links_ref, ph_ref, *refs):
    fields, refs = refs[:8], refs[8:]
    (
        picked, coef,
        links, ph, rims_ref, ends_ref, table_ref, diag_ref,
        held, pack, ends, ring, ring_ends, chosen,
        load_sem, links_sem, near_send, near_recv, diag_send, diag_recv, ring_send, ring_recv, ring_ends_send, ring_ends_recv,
        main_send, main_recv, ext_send, ext_recv, corner_send, corner_recv,
    ) = refs
    last = sides - 1
    pairs = faces // 2
    side = held.shape[1]
    w = lax.axis_index("wide")
    c = lax.axis_index("narrow")
    f = w // sides
    r = w % sides
    x, half = f // 2, f % 2
    at = lambda face, row, col: (face * sides + row, col)
    signal = lambda bar, d: pl.semaphore_signal(bar, inc=1, device_id=d, device_id_type=MESH)
    is_end = lambda q: (q == 0) | (q == last)
    corner = is_end(r) & is_end(c)
    rim = is_end(r) | is_end(c)
    inside = lambda row, col: (row >= 0) & (row <= last) & (col >= 0) & (col <= last)
    edges = [(W, c == 0, r, last), (S, r == 0, c, last), (E, c == last, r, 0), (N, r == last, c, 0)]
    ext_to = lambda q: (q + 1, q - 1, last - 1 - q, last + 1 - q)
    ext_from = lambda q: (q - 1, q + 1, last - 1 - q, last + 1 - q)
    corner_at = lambda i: at(x * 2 + i // 4, (i // 2) % 2 * last, i % 2 * last)
    me_corner = half * 4 + (r // last) * 2 + c // last
    ring_at = lambda k: at((f + 2 * k) % faces, r, c)

    bar = pltpu.get_barrier_semaphore()
    awaited = jnp.int32(0)
    for e, has, q, line in edges:

        @pl.when(has)
        def _(q=q, line=line):
            for h in range(2):
                g = x * 2 + h
                for p in (q, last - q):
                    for row, col in ((p, line), (line, p)):

                        @pl.when(~((g == f) & (row == r) & (col == c)))
                        def _(g=g, row=row, col=col):
                            signal(bar, at(g, row, col))

                for p in ext_from(q):

                    @pl.when((p >= 0) & (p <= last))
                    def _(g=g, p=p):
                        signal(bar, at(g, p, line))
                        signal(bar, at(g, line, p))

        ext = jnp.where(is_end(q), 8, 16)
        awaited += jnp.where(has, 8 + ext, 0)
    own = corner & (r != c)
    awaited -= jnp.where(own, 2, 0)

    @pl.when(rim)
    def _():
        for k in range(1, pairs):
            signal(bar, ring_at(k))

    @pl.when(corner)
    def _():
        for i in range(8):

            @pl.when(i != me_corner)
            def _(i=i):
                signal(bar, corner_at(i))

    awaited += jnp.where(rim, pairs - 1, 0) + jnp.where(corner, 7, 0)
    for dr in (-1, 0, 1):
        for dc in (-1, 0, 1):
            if (dr, dc) != (0, 0):
                there = inside(r + dr, c + dc)
                awaited += there.astype(jnp.int32)

                @pl.when(there)
                def _(dr=dr, dc=dc):
                    signal(bar, at(f, r + dr, c + dc))

    loads = [
        pltpu.make_async_copy(ph_ref, ph, links_sem.at[0]),
        pltpu.make_async_copy(links_ref, links, links_sem.at[1]),
    ] + [pltpu.make_async_copy(ref, held.at[k], load_sem.at[k]) for k, ref in enumerate(fields)]
    for copy in loads:
        copy.start()
    for copy in loads:
        copy.wait()

    which = lax.broadcasted_iota(jnp.int32, (CONSTITUENTS, side), 0)
    count = (lax.broadcasted_iota(jnp.int32, (CONSTITUENTS, side), 1) + 1).astype(jnp.float32)
    start = jnp.zeros((CONSTITUENTS, side), jnp.float32)
    rate = jnp.zeros((CONSTITUENTS, side), jnp.float32)
    for k in range(CONSTITUENTS):
        start = jnp.where(which == k, ph[k], start)
        rate = jnp.where(which == k, jnp.float32(tide_omega[k]) * jnp.float32(step_seconds), rate)
    angle = start + rate * count
    coef[0:CONSTITUENTS, :] = jnp.cos(angle)
    coef[CONSTITUENTS:, :] = jnp.sin(angle)

    sp, s, up, u, vp, v, dw, ds = (held.at[k] for k in range(8))
    lo, hi = rims(s[...], sp[...], v[...], vp[...], u[...], up[...], ds[...], dw[...])
    for k in range(LINES):
        pack[S, 0, k : k + 1, :] = lo[k]
        pack[N, 0, k : k + 1, :] = hi[k]
    flip = lambda ref: jnp.transpose(ref[...])
    lo, hi = rims(flip(s), flip(sp), flip(u), flip(up), flip(v), flip(vp), flip(dw), flip(ds))
    for k in range(LINES):
        pack[W, 0, k : k + 1, :] = lo[k]
        pack[E, 0, k : k + 1, :] = hi[k]
    for e in range(4):
        pack[e, 0, LINES:16, :] = jnp.full((16 - LINES, side), G, jnp.float32)
    whole = jnp.concatenate([pack[e, 0] for e in range(4)], axis=0)
    stacked = jnp.concatenate([whole, jnp.zeros((side - 64, side), jnp.float32)], axis=0)
    turned = jnp.transpose(stacked)
    lane = lax.broadcasted_iota(jnp.int32, (1, side), 1)
    for e in range(4):
        gathered = jnp.zeros((1, side), jnp.float32)
        for k, i in enumerate((0, 1, side - 2, side - 1)):
            moved = turned[i : i + 1, :]
            by = (16 * k - 16 * e) % side
            if by:
                moved = pltpu.roll(moved, by, 1)
            gathered = jnp.where((lane >= 16 * k) & (lane < 16 * k + 16), moved, gathered)
        ends[e] = gathered
        pack[e, 0, LINES : LINES + 1, :] = gathered
        pack[e, 1, LINES : LINES + 1, :] = gathered
    total = lax.broadcasted_iota(jnp.int32, (side, side), 0) + lax.broadcasted_iota(jnp.int32, (side, side), 1)
    mirror = (total == side - 1).astype(jnp.float32)
    turned = jnp.dot(whole, mirror, precision=lax.Precision.HIGHEST, preferred_element_type=jnp.float32)
    for e in range(4):
        for k in range(LINES):
            line_k = turned[16 * e + k : 16 * e + k + 1, :]
            if k in (5, 6, 7) or (k == 8 and e in (E, N)):
                line_k = jnp.where(lane == 0, 0.0, pltpu.roll(line_k, 1, 1))
                line_k = line_k if k == 7 else -line_k
            pack[e, 1, k : k + 1, :] = jnp.where(links[2, e, f] == 1, line_k, pack[e, 0, k : k + 1, :])

    pl.semaphore_wait(bar, awaited)

    full = pl.ds(0, LINES + 1)
    block = full
    here = (w, c)
    remote = lambda a, b, ss, rs, d: pltpu.make_async_remote_copy(
        a, b, ss, rs, device_id=d, device_id_type=MESH
    )
    ring_copies = lambda e: [
        remote(pack.at[e, 1, full], ring.at[e, k, full], ring_send.at[e, k], ring_recv.at[e, k], ring_at(k))
        for k in range(1, pairs)
    ]
    ends_copies = lambda: [
        remote(ends, ring_ends.at[k], ring_ends_send.at[k], ring_ends_recv.at[k], ring_at(k)) for k in range(1, pairs)
    ]
    for e, has, q, line in edges:

        @pl.when(has)
        def _(e=e):
            for copy in ring_copies(e):
                copy.start()

    @pl.when(corner)
    def _():
        for copy in ends_copies():
            copy.start()

    near = [(E, W, 0, 1), (N, S, 1, 0), (W, E, 0, -1), (S, N, -1, 0)]
    diagonal = [(0, 1, 1), (1, 1, -1), (2, -1, 1), (3, -1, -1)]
    near_copy = lambda e, to, dr, dc: remote(
        pack.at[e, 0, block], rims_ref.at[to, 8, block], near_send.at[e], near_recv.at[e], at(f, r + dr, c + dc)
    )
    diag_copy = lambda k, dr, dc: remote(ends, diag_ref.at[k], diag_send.at[k], diag_recv.at[k], at(f, r + dr, c + dc))
    for e, to, dr, dc in near:

        @pl.when(inside(r + dr, c + dc))
        def _(e=e, to=to, dr=dr, dc=dc):
            near_copy(e, to, dr, dc).start()

    for k, dr, dc in diagonal:

        @pl.when(inside(r + dr, c + dc))
        def _(k=k, dr=dr, dc=dc):
            diag_copy(k, dr, dc).start()

    for e, has, q, line in edges:

        @pl.when(has)
        def _(e=e):
            for copy in ring_copies(e):
                copy.wait_recv()

    for e, has, q, line in edges:
        to_ws = e in (E, N)
        kind = 1 if e in (N, S) else 0
        lines = [(h, to) for h in range(2) for to in ((W, S) if to_ws else (E, N))]

        @pl.when(has)
        def _(e=e, q=q, line=line, kind=kind, lines=lines):
            ring[e, 0] = pack[e, 1]
            for j, (h, to) in enumerate(lines):
                far_x = links[0, to, x * 2 + h] // 2
                chosen[e, j] = ring[e, lax.rem(x - far_x + pairs, pairs)]
            for j, (h, to) in enumerate(lines):
                g = x * 2 + h
                place = lambda p, to=to: (p, line) if to in (W, E) else (line, p)
                for par, p in enumerate((q, last - q)):
                    slot = (half * 2 + kind) * 2 + par
                    row, col = place(p)
                    mine = (g == f) & (row == r) & (col == c)

                    @pl.when(~mine)
                    def _(j=j, to=to, slot=slot, g=g, row=row, col=col):
                        remote(
                            chosen.at[e, j, block], rims_ref.at[to, slot, block], main_send.at[e], main_recv.at[to], at(g, row, col)
                        ).start()

                    @pl.when(mine)
                    def _(j=j, to=to, slot=slot):
                        pltpu.make_async_copy(chosen.at[e, j, block], rims_ref.at[to, slot, block], main_recv.at[to]).start()

            for j, (h, to) in enumerate(lines):
                g = x * 2 + h
                place = lambda p, to=to: (p, line) if to in (W, E) else (line, p)
                for kind_x, p in enumerate(ext_to(q)):
                    slot = (half * 2 + kind) * 4 + kind_x
                    row, col = place(p)

                    @pl.when((p >= 0) & (p <= last))
                    def _(j=j, to=to, slot=slot, g=g, row=row, col=col):
                        remote(
                            chosen.at[e, j, pl.ds(LINES, 1)], ends_ref.at[to, slot], ext_send.at[e], ext_recv.at[to], at(g, row, col)
                        ).start()

    corner_copy = lambda i: remote(ring_ends, table_ref.at[me_corner], corner_send.at[0], corner_recv.at[0], corner_at(i))

    @pl.when(corner)
    def _():
        for copy in ends_copies():
            copy.wait_recv()
        ring_ends[0] = ends[...]
        for i in range(8):

            @pl.when(i != me_corner)
            def _(i=i):
                corner_copy(i).start()

        pltpu.make_async_copy(ring_ends, table_ref.at[me_corner], corner_recv.at[0]).start()

    take = lambda ref, ss, rs: remote(ref, ref, ss, rs, here)
    for e, to, dr, dc in near:

        @pl.when(inside(r + dr, c + dc))
        def _(e=e, to=to, dr=dr, dc=dc):
            near_copy(e, to, dr, dc).wait_send()

    for k, dr, dc in diagonal:

        @pl.when(inside(r + dr, c + dc))
        def _(k=k, dr=dr, dc=dc):
            diag_copy(k, dr, dc).wait_send()

    for e, has, q, line in edges:

        @pl.when(has)
        def _(e=e, q=q):
            for copy in ring_copies(e):
                copy.wait_send()

            @pl.when(~own)
            def _():
                take(rims_ref.at[e, pl.ds(0, 8), block], main_send.at[e], main_recv.at[e]).wait_send()

            @pl.when(own)
            def _():
                take(rims_ref.at[e, pl.ds(0, 7), block], main_send.at[e], main_recv.at[e]).wait_send()

            @pl.when(is_end(q))
            def _():
                take(ends_ref.at[e, pl.ds(0, 8)], ext_send.at[e], ext_recv.at[e]).wait_send()

            @pl.when(~is_end(q))
            def _():
                take(ends_ref.at[e], ext_send.at[e], ext_recv.at[e]).wait_send()

    @pl.when(corner)
    def _():
        for copy in ends_copies():
            copy.wait_send()
        take(table_ref.at[pl.ds(0, 7)], corner_send.at[0], corner_recv.at[0]).wait_send()

    for e, to, dr, dc in near:

        @pl.when(inside(r - dr, c - dc))
        def _(e=e, to=to):
            take(rims_ref.at[to, 8, block], near_send.at[e], near_recv.at[e]).wait_recv()

    for k, dr, dc in diagonal:

        @pl.when(inside(r - dr, c - dc))
        def _(k=k):
            take(diag_ref.at[k], diag_send.at[k], diag_recv.at[k]).wait_recv()

    link = lambda face, edge, k: links[k, edge, face]
    end = lambda row, k, line: row[:, 16 * k + line : 16 * k + line + 1]
    at_end = lambda row, high, k, line: jnp.where(high == 1, end(row, 3 - k, line), end(row, k, line))

    def corner_of(face, edge, high):
        row = jnp.where(edge == S, 0, jnp.where(edge == N, 1, high))
        col = jnp.where(edge == W, 0, jnp.where(edge == E, 1, high))
        return table_ref[face % 2 * 4 + row * 2 + col, lax.rem(x - face // 2 + pairs, pairs), edge]

    def beyond(face, edge, high):
        far, far_edge, turn = (link(face, edge, k) for k in range(3))
        stop = high ^ turn
        return at_end(corner_of(far, far_edge, stop), stop, 0, 8)

    def at_corner(face, edge, low_end):
        vertical = (edge == W) | (edge == E)
        side_edge = jnp.where(vertical, S, W) if low_end else jnp.where(vertical, N, E)
        start = (edge >= E).astype(jnp.int32)
        far, far_edge, turn = (link(face, side_edge, k) for k in range(3))
        high = start ^ turn
        row = corner_of(far, far_edge, high)
        far_vertical = (far_edge == W) | (far_edge == E)
        third = beyond(far, jnp.where(far_vertical, N, E), (far_edge >= E).astype(jnp.int32))
        ahead = jnp.where(high == 1, third, end(row, 1, 5))
        s1 = at_end(row, high, 0, 1) - G * (ahead - at_end(row, high, 0, 5))
        if low_end:
            parts = {(3, 0): at_end(row, high, 0, 0), (3, 1): s1}
        else:
            parts = {(0, 0): at_end(row, high, 0, 0)}
            across = at_end(row, high, 0, 8)
            parts.update({(0, 1): s1, (0, 5): across, (1, 5): across, (0, 6): at_end(row, high, 0, 3)})
            parts.update({(0, 7): at_end(row, high, 0, 4), (0, 8): at_end(row, high, 1, 8)})
        made = jnp.zeros((1, side), jnp.float32)
        for (k, line), value in parts.items():
            made = jnp.where(lane == 16 * k + line, value, made)
        return made

    choices = []
    for e, on_face, seg, _ in edges:
        to_ws = e in (W, S)
        across = e in (W, E)
        face, partner, turn = (link(f, e, k) for k in range(3))
        kind = (partner == (N if to_ws else S)).astype(jnp.int32)
        q = jnp.where(turn == 1, last - seg, seg)
        slot = jnp.where(on_face, (face % 2 * 2 + kind) * 2 + turn, 8)
        slot_x = jnp.where(on_face, (face % 2 * 2 + kind) * 4 + 2 * turn, 0)
        strip = (e + 2) % 4
        lo_at, hi_at = {W: (0, 2), S: (0, 1), E: (1, 3), N: (2, 3)}[e]
        flag = jnp.where(on_face, turn, 0).astype(jnp.float32)
        picked[e, 12:13, :] = jnp.zeros((1, side), jnp.float32) + flag
        choices.append((e, on_face, face, partner, q, slot, slot_x, strip, lo_at, hi_at))

    for e, has, q, line in edges:

        @pl.when(has)
        def _(e=e, q=q):
            take(rims_ref.at[e, pl.ds(0, 8), block], main_send.at[0], main_recv.at[e]).wait_recv()

            @pl.when(is_end(q))
            def _():
                take(ends_ref.at[e, pl.ds(0, 8)], ext_send.at[0], ext_recv.at[e]).wait_recv()

            @pl.when(~is_end(q))
            def _():
                take(ends_ref.at[e], ext_send.at[0], ext_recv.at[e]).wait_recv()

    @pl.when(corner)
    def _():
        take(table_ref, corner_send.at[0], corner_recv.at[0]).wait_recv()

    for e, on_face, face, partner, q, slot, slot_x, strip, lo_at, hi_at in choices:
        picked[e, 0:10, :] = rims_ref[e, slot, 0:10, :]
        picked[e, 10:11, :] = jnp.where(on_face, ends_ref[e, slot_x], diag_ref[lo_at, strip])
        picked[e, 11:12, :] = jnp.where(on_face, ends_ref[e, slot_x + 1], diag_ref[hi_at, strip])

        @pl.when(corner & on_face)
        def _(e=e, face=face, partner=partner, q=q):
            picked[e, 10:11, :] = jnp.where(q == 0, at_corner(face, partner, True), picked[e, 10:11, :])
            picked[e, 11:12, :] = jnp.where(q == last, at_corner(face, partner, False), picked[e, 11:12, :])


def substeps(sides, picked, coef, *refs):
    fields, refs = refs[:8], refs[8:]
    s_out, u_out, v_out, h_out, levels, sums, out_sem, sum_sem = refs
    last = sides - 1
    side = levels.shape[1]
    c = lax.axis_index("narrow")
    r = lax.rem(lax.axis_index("wide"), sides)
    lane = lax.broadcasted_iota(jnp.int32, (1, side), 1)
    rows = lax.broadcasted_iota(jnp.int32, (side, side), 0)
    cols = lax.broadcasted_iota(jnp.int32, (side, side), 1)
    diagonal = rows == cols
    pick = lambda cond, a, b: jnp.where(cond, a, b)
    up_by = lambda x, fill: jnp.where(lane == side - 1, fill, pltpu.roll(x, side - 1, 1))
    down_by = lambda x, fill: jnp.where(lane == 0, fill, pltpu.roll(x, 1, 1))
    head = lambda x: x[:, 0:1]
    tail = lambda x: x[:, side - 1 : side]
    end = lambda row, k, line: row[:, 16 * k + line : 16 * k + line + 1]

    def ghost(edge, to_ws):
        block = picked[edge]
        line = [block[k : k + 1, :] for k in range(LINES)]
        own, lo_x, hi_x = (block[k : k + 1, :] for k in (9, 10, 11))
        flipped = block[12:13, 0:1] > 0.5
        lo = dict(
            s0=end(lo_x, 3, 0), s1=end(lo_x, 3, 1) - G * (end(own, 0, 5) - end(lo_x, 3, 5)),
            F=end(lo_x, 3, 8), R=end(lo_x, 3, 3), Dn=end(lo_x, 3, 4), Fb=end(lo_x, 2, 8), g=end(lo_x, 3, 15),
        )
        hi = dict(
            s0=end(hi_x, 0, 0), s1=end(hi_x, 0, 1) - G * (end(hi_x, 1, 5) - end(hi_x, 0, 5)),
            T0=end(hi_x, 0, 5), Q=end(hi_x, 0, 6), D=end(hi_x, 0, 7), Tb=end(hi_x, 0, 8),
            F=end(hi_x, 0, 8), R=end(hi_x, 0, 3), Dn=end(hi_x, 0, 4), Fb=end(hi_x, 1, 8), g=end(hi_x, 0, 15),
        )
        shared = ("s0", "s1", "F", "R", "Dn", "Fb", "g")
        new_lo = {n: pick(flipped, hi[n], lo[n]) for n in shared}
        new_hi = {n: pick(flipped, lo[n], hi[n]) for n in shared}
        along = {5: ("T0", -1.0), 6: ("Q", -1.0), 7: ("D", 1.0)}
        if to_ws:
            along[8] = ("Tb", -1.0)
        for k, (name, sign) in along.items():
            line[k] = pick((lane == 0) & flipped, sign * hi[name], line[k])
            new_hi[name] = pick(flipped, sign * end(own, 0, k), hi[name])
        return line, new_lo, new_hi

    (wl, w_lo, w_hi), (sl, s_lo, s_hi) = ghost(W, True), ghost(S, True)
    (el, e_lo, e_hi), (nl, n_lo, n_hi) = ghost(E, False), ghost(N, False)

    for d, x in ((w_lo, sl), (w_hi, nl), (s_lo, wl), (s_hi, el)):
        d["s1"] = d["s1"] - d["g"] * head(x[5])

    west, south, east, north = c == 0, r == 0, c == last, r == last
    take_w, take_s = west & ~south, south & ~west
    sw_w = {n: pick(take_s, s_lo[n], w_lo[n]) for n in ("s0", "s1")}
    sw_s = {n: pick(take_w, w_lo[n], s_lo[n]) for n in ("s0", "s1")}
    w_lo.update(sw_w)
    s_lo.update(sw_s)
    share = (("s0", "s0"), ("s1", "s1"), ("T0", "F"), ("Q", "R"), ("D", "Dn"), ("Tb", "Fb"))
    take_e, take_s = east & ~south, south & ~east
    se_s = {a: pick(take_e, e_lo[b], s_hi[a]) for a, b in share}
    e_lo["s0"] = pick(take_s, s_hi["s0"], e_lo["s0"])
    s_hi.update(se_s)
    take_n, take_w = north & ~west, west & ~north
    nw_w = {a: pick(take_n, n_lo[b], w_hi[a]) for a, b in share}
    n_lo["s0"] = pick(take_w, w_hi["s0"], n_lo["s0"])
    w_hi.update(nw_w)
    take_e, take_n = east & ~north, north & ~east
    share = (("s0", "s0"), ("T0", "F"), ("Q", "R"), ("D", "Dn"))
    ne_n = {a: pick(take_e, e_hi[b], n_hi[a]) for a, b in share}
    ne_e = {a: pick(take_n, n_hi[b], e_hi[a]) for a, b in share}
    n_hi.update(ne_n)
    e_hi.update(ne_e)

    class HeightRim:
        def __init__(self, line, lo, hi):
            self.line, self.lo, self.hi = line, lo, hi

        def at(self, n, flux):
            s0, y1, y2, z, back, t0, q, d, tb = self.line
            lo, hi = self.lo, self.hi
            if n == 0:
                return s0
            if n == 1:
                self.s1 = y1 - G * flux - G * (up_by(t0, hi["T0"]) - t0)
                return self.s1
            if n == 2:
                self.t1 = q - d * (s0 - down_by(s0, lo["s0"]))
                self.t1hi = hi["Q"] - hi["D"] * (hi["s0"] - tail(s0))
                self.s2 = y2 + 0.1 * self.s1 - G * flux - G * (up_by(self.t1, self.t1hi) - self.t1)
                return self.s2
            s1 = self.s1
            t2 = 0.8 * t0 + 0.1 * q + 0.1 * self.t1 - d * (s1 - down_by(s1, lo["s1"]))
            t2hi = 0.8 * hi["T0"] + 0.1 * hi["Q"] + 0.1 * self.t1hi - hi["D"] * (hi["s1"] - tail(s1))
            inner = s1 + G * (up_by(tb, hi["Tb"]) - tb)
            return 0.81 * s1 + 0.1 * self.s2 + z - G * back * inner - G * flux - G * (up_by(t2, t2hi) - t2)

    class FluxRim:
        def __init__(self, line, lo, hi):
            self.line, self.lo, self.hi = line, lo, hi

        def at(self, n, height):
            s0, u1, u2, r_, d_, t0, q, d, f0 = self.line
            lo, hi = self.lo, self.hi
            if n == 0:
                return f0
            if n == 1:
                self.f1 = r_ - d_ * (s0 - height)
                return self.f1
            if n == 2:
                self.s1 = u1 - G * (up_by(t0, hi["T0"]) - t0)
                self.older = 0.8 * f0 + 0.1 * r_ + 0.1 * self.f1
                self.f2 = self.older - d_ * (self.s1 - height)
                return self.f2
            t1 = q - d * (s0 - down_by(s0, lo["s0"]))
            t1hi = hi["Q"] - hi["D"] * (hi["s0"] - tail(s0))
            s2 = u2 + 0.1 * self.s1 + G * self.f1 - G * (up_by(t1, t1hi) - t1)
            return 0.8 * self.f1 + 0.1 * self.f2 + 0.1 * self.older - d_ * (s2 - height)

    rim_w, rim_s = HeightRim(wl, w_lo, w_hi), HeightRim(sl, s_lo, s_hi)
    rim_e, rim_n = FluxRim(el, e_lo, e_hi), FluxRim(nl, n_lo, n_hi)
    as_row = lambda col: jnp.sum(jnp.where(diagonal, col, 0.0), axis=0, keepdims=True)
    as_col = lambda row: jnp.sum(jnp.where(diagonal, row, 0.0), axis=1, keepdims=True)
    sp_, s_, up_, u_, vp_, v_, dw_, ds_ = (x[...] for x in fields)
    first_col, last_col = cols == 0, cols == side - 1
    first_row, last_row = rows == 0, rows == side - 1
    flux_w = flux_s = height_e = height_n = None
    snaps = []
    for n in range(SUBSTEPS):
        fw, fs = dw_ * u_, ds_ * v_
        west_line, south_line = rim_w.at(n, flux_w), rim_s.at(n, flux_s)
        east_line, north_line = rim_e.at(n, height_e), rim_n.at(n, height_n)
        flux_w, flux_s = as_row(fw[:, 0:1]), fs[0:1, :]
        height_e, height_n = as_row(s_[:, side - 1 : side]), s_[side - 1 : side, :]
        fe = jnp.where(last_col, as_col(east_line), pltpu.roll(fw, side - 1, 1))
        fn = jnp.where(last_row, north_line, pltpu.roll(fs, side - 1, 0))
        sw = jnp.where(first_col, as_col(west_line), pltpu.roll(s_, 1, 1))
        ss = jnp.where(first_row, south_line, pltpu.roll(s_, 1, 0))
        s_next = sp_ - G * ((fe - fw) + (fn - fs))
        u_next = up_ - G * (s_ - sw)
        v_next = vp_ - G * (s_ - ss)
        sp_ = s_ + 0.1 * (sp_ - 2.0 * s_ + s_next)
        up_ = u_ + 0.1 * (up_ - 2.0 * u_ + u_next)
        vp_ = v_ + 0.1 * (vp_ - 2.0 * v_ + v_next)
        s_, u_, v_ = s_next, u_next, v_next
        snaps.append(s_)
    stores = []
    for k, (x, out) in enumerate(((s_, s_out), (u_, u_out), (v_, v_out))):
        levels[k] = x
        stores.append(pltpu.make_async_copy(levels.at[k], out, out_sem.at[k]))
        stores[-1].start()
    for k in range(2 * CONSTITUENTS):
        total = coef[k : k + 1, 0:1] * snaps[0]
        for n in range(1, SUBSTEPS):
            total += coef[k : k + 1, n : n + 1] * snaps[n]
        sums[k] = total
        stores.append(pltpu.make_async_copy(sums.at[k], h_out.at[k], sum_sem.at[k]))
        stores[-1].start()
    for copy in stores:
        copy.wait()


def solution(mesh):
    def body(sp, s, up, u, vp, v, dw, ds, links, ph):
        side = s.shape[0]
        sides = mesh.shape["narrow"]
        faces = mesh.shape["wide"] // sides
        f32 = jnp.float32
        shape = lambda *dims: jax.ShapeDtypeStruct(dims, f32)
        hbm = pl.BlockSpec(memory_space=pl.ANY)
        vmem = pl.BlockSpec(memory_space=pltpu.VMEM)
        dma = pltpu.SemaphoreType.DMA
        scratch = lambda *dims: pltpu.VMEM(dims, f32)
        pairs = faces // 2
        links = jnp.transpose(links, (2, 1, 0))
        fields = (sp, s, up, u, vp, v, dw, ds)
        grant = 8 << 20
        in_hbm = [pltpu.with_memory_space_constraint(a, pltpu.HBM) for a in (links, ph, *fields)]
        got = pl.pallas_call(
            functools.partial(exchange, sides, faces),
            out_shape=(shape(4, 16, side), shape(2 * CONSTITUENTS, side)),
            in_specs=[hbm] * 10,
            out_specs=(vmem,) * 2,
            scratch_shapes=[
                pltpu.SMEM(links.shape, jnp.int32),
                pltpu.SMEM(ph.shape, f32),
                scratch(4, 9, 16, side),
                scratch(4, 16, 1, side),
                scratch(8, pairs, 4, 1, side),
                scratch(4, 4, 1, side),
                scratch(8, side, side),
                scratch(4, 2, 16, side),
                scratch(4, 1, side),
                scratch(4, pairs, 16, side),
                scratch(pairs, 4, 1, side),
                scratch(4, 4, 16, side),
                dma((8,)), dma((2,)), dma((4,)), dma((4,)), dma((4,)), dma((4,)),
                dma((4, pairs)), dma((4, pairs)), dma((pairs,)), dma((pairs,)),
                dma((4,)), dma((4,)), dma((4,)), dma((4,)), dma((1,)), dma((1,)),
            ],
            compiler_params=pltpu.CompilerParams(collective_id=0, has_side_effects=True, vmem_limit_bytes=grant),
        )(*in_hbm)
        tile = shape(side, side)
        return pl.pallas_call(
            functools.partial(substeps, sides),
            out_shape=(tile, tile, tile, shape(2 * CONSTITUENTS, side, side)),
            in_specs=[vmem] * 10,
            out_specs=(hbm,) * 4,
            scratch_shapes=[scratch(3, side, side), scratch(2 * CONSTITUENTS, side, side), dma((3,)), dma((2 * CONSTITUENTS,))],
            compiler_params=pltpu.CompilerParams(vmem_limit_bytes=grant),
        )(*got, *fields)

    tiles = P("wide", "narrow")
    return jax.shard_map(
        body,
        mesh=mesh,
        in_specs=(tiles,) * 8 + (P(), P()),
        out_specs=(tiles, tiles, tiles, P(None, "wide", "narrow")),
        check_vma=False,
    )
```

```python
import functools

import jax
import jax.numpy as jnp
from jax import lax
from jax.experimental import pallas as pl
from jax.experimental.pallas import tpu as pltpu
from jax.sharding import PartitionSpec as P

MESH = pl.DeviceIdType.MESH
SUBSTEPS = 4
CONSTITUENTS = 8
tide_omega = (
    0.0001405189,
    0.0001454441,
    0.0001378797,
    0.0001458423,
    7.292117e-05,
    6.759774e-05,
    7.251056e-05,
    6.495854e-05,
)
step_seconds = 25.0
G = 0.6
W, S, E, N = range(4)
LINES = 9


def rims(s, sp, n, np_, t, tp, dn, dt):
    last = s.shape[0] - 1
    row = lambda x, i: x[i : i + 1, :]
    a, b = last, last - 1
    n1 = row(np_, a) - G * (row(s, a) - row(s, b))
    fa = row(dn, a) * row(n, a)
    fb = row(dn, b) * row(n, b)
    back = G * row(dn, a)
    older = 0.8 * row(n, a) + 0.1 * row(np_, a) + 0.1 * n1
    high = [
        row(s, a),
        row(sp, a) + G * fa,
        0.8 * row(s, a) + 0.1 * row(sp, a) + G * (row(dn, a) * n1),
        0.08 * row(s, a)
        + 0.01 * row(sp, a)
        + G * (row(dn, a) * older + back * (row(sp, b) - G * (fa - fb))),
        back,
        row(dt, a) * row(t, a),
        row(dt, a) * row(tp, a),
        G * row(dt, a),
        row(dt, b) * row(t, b),
    ]
    a, b = 0, 1
    n1 = row(np_, b) - G * (row(s, b) - row(s, a))
    fa = row(dn, a) * row(n, a)
    fb = row(dn, b) * row(n, b)
    low = [
        row(s, a),
        row(sp, a) - G * (fb - fa),
        0.8 * row(s, a) + 0.1 * row(sp, a) - G * (row(dn, b) * n1),
        row(dn, a) * row(np_, a),
        G * row(dn, a),
        row(dt, a) * row(t, a),
        row(dt, a) * row(tp, a),
        G * row(dt, a),
        fa,
    ]
    return low, high


def merge(raw, high, lane):
    up0 = lambda x: jnp.where(lane == lane.shape[1] - 1, 0.0, pltpu.roll(x, lane.shape[1] - 1, 1))
    down0 = lambda x: jnp.where(lane == 0, 0.0, pltpu.roll(x, 1, 1))
    s0, y1, y2, a, b, t0, q, d, last_line = raw
    t1 = q - d * (s0 - down0(s0))
    if high:
        older = 0.8 * t0 + 0.1 * q + 0.1 * t1
        x3 = a - G * (up0(older) - older) - G * b * (G * (up0(last_line) - last_line))
        return [s0, y1 - G * (up0(t0) - t0), y2 - G * (up0(t1) - t1), x3, b, d]
    f0, was = last_line, a
    s1 = y1 - G * (up0(t0) - t0)
    s2 = y2 + 0.1 * s1 - G * (up0(t1) - t1)
    return [f0, was - b * s0, 0.8 * f0 + 0.1 * was - b * s1, 0.08 * f0 + 0.01 * was - b * s2, b]


def exchange(sides, faces, links_ref, ph_ref, *refs):
    fields, refs = refs[:8], refs[8:]
    (
        picked, coef,
        links, ph, rims_ref, ends_ref, table_ref, diag_ref,
        held, pack, sent, ends, ring, ring_ends, chosen,
        load_sem, links_sem, near_send, near_recv, diag_send, diag_recv, ring_send, ring_recv, ring_ends_send, ring_ends_recv,
        main_send, main_recv, ext_send, ext_recv, corner_send, corner_recv,
    ) = refs
    last = sides - 1
    pairs = faces // 2
    side = held.shape[1]
    w = lax.axis_index("wide")
    c = lax.axis_index("narrow")
    f = w // sides
    r = w % sides
    x, half = f // 2, f % 2
    at = lambda face, row, col: (face * sides + row, col)
    signal = lambda bar, d: pl.semaphore_signal(bar, inc=1, device_id=d, device_id_type=MESH)
    is_end = lambda q: (q == 0) | (q == last)
    corner = is_end(r) & is_end(c)
    rim = is_end(r) | is_end(c)
    inside = lambda row, col: (row >= 0) & (row <= last) & (col >= 0) & (col <= last)
    edges = [(W, c == 0, r, last), (S, r == 0, c, last), (E, c == last, r, 0), (N, r == last, c, 0)]
    ext_to = lambda q: (q + 1, q - 1, last - 1 - q, last + 1 - q)
    ext_from = lambda q: (q - 1, q + 1, last - 1 - q, last + 1 - q)
    corner_at = lambda i: at(x * 2 + i // 4, (i // 2) % 2 * last, i % 2 * last)
    me_corner = half * 4 + (r // last) * 2 + c // last
    ring_at = lambda k: at((f + 2 * k) % faces, r, c)

    bar = pltpu.get_barrier_semaphore()
    awaited = jnp.int32(0)
    for e, has, q, line in edges:

        @pl.when(has)
        def _(q=q, line=line):
            for h in range(2):
                g = x * 2 + h
                for p in (q, last - q):
                    for row, col in ((p, line), (line, p)):

                        @pl.when(~((g == f) & (row == r) & (col == c)))
                        def _(g=g, row=row, col=col):
                            signal(bar, at(g, row, col))

                for p in ext_from(q):

                    @pl.when((p >= 0) & (p <= last))
                    def _(g=g, p=p):
                        signal(bar, at(g, p, line))
                        signal(bar, at(g, line, p))

        ext = jnp.where(is_end(q), 8, 16)
        awaited += jnp.where(has, 8 + ext, 0)
    own = corner & (r != c)
    awaited -= jnp.where(own, 2, 0)

    @pl.when(rim)
    def _():
        for k in range(1, pairs):
            signal(bar, ring_at(k))

    @pl.when(corner)
    def _():
        for i in range(8):

            @pl.when(i != me_corner)
            def _(i=i):
                signal(bar, corner_at(i))

    awaited += jnp.where(rim, pairs - 1, 0) + jnp.where(corner, 7, 0)
    for dr in (-1, 0, 1):
        for dc in (-1, 0, 1):
            if (dr, dc) != (0, 0):
                there = inside(r + dr, c + dc)
                awaited += there.astype(jnp.int32)

                @pl.when(there)
                def _(dr=dr, dc=dc):
                    signal(bar, at(f, r + dr, c + dc))

    loads = [
        pltpu.make_async_copy(ph_ref, ph, links_sem.at[0]),
        pltpu.make_async_copy(links_ref, links, links_sem.at[1]),
    ] + [pltpu.make_async_copy(ref, held.at[k], load_sem.at[k]) for k, ref in enumerate(fields)]
    for copy in loads:
        copy.start()
    for copy in loads:
        copy.wait()

    which = lax.broadcasted_iota(jnp.int32, (CONSTITUENTS, side), 0)
    count = (lax.broadcasted_iota(jnp.int32, (CONSTITUENTS, side), 1) + 1).astype(jnp.float32)
    start = jnp.zeros((CONSTITUENTS, side), jnp.float32)
    rate = jnp.zeros((CONSTITUENTS, side), jnp.float32)
    for k in range(CONSTITUENTS):
        start = jnp.where(which == k, ph[k], start)
        rate = jnp.where(which == k, jnp.float32(tide_omega[k]) * jnp.float32(step_seconds), rate)
    angle = start + rate * count
    coef[0:CONSTITUENTS, :] = jnp.cos(angle)
    coef[CONSTITUENTS:, :] = jnp.sin(angle)

    sp, s, up, u, vp, v, dw, ds = (held.at[k] for k in range(8))
    lo, hi = rims(s[...], sp[...], v[...], vp[...], u[...], up[...], ds[...], dw[...])
    for k in range(LINES):
        pack[S, k : k + 1, :] = lo[k]
        pack[N, k : k + 1, :] = hi[k]
    flip = lambda ref: jnp.transpose(ref[...])
    lo, hi = rims(flip(s), flip(sp), flip(u), flip(up), flip(v), flip(vp), flip(dw), flip(ds))
    for k in range(LINES):
        pack[W, k : k + 1, :] = lo[k]
        pack[E, k : k + 1, :] = hi[k]
    for e in range(4):
        pack[e, LINES:16, :] = jnp.full((16 - LINES, side), G, jnp.float32)
    stacked = jnp.concatenate([pack[e] for e in range(4)] + [jnp.zeros((side - 64, side), jnp.float32)], axis=0)
    turned = jnp.transpose(stacked)
    lane = lax.broadcasted_iota(jnp.int32, (1, side), 1)
    for e in range(4):
        gathered = jnp.zeros((1, side), jnp.float32)
        for k, i in enumerate((0, 1, side - 2, side - 1)):
            moved = turned[i : i + 1, :]
            by = (16 * k - 16 * e) % side
            if by:
                moved = pltpu.roll(moved, by, 1)
            gathered = jnp.where((lane >= 16 * k) & (lane < 16 * k + 16), moved, gathered)
        ends[e] = gathered
        merged = merge([pack[e, k : k + 1, :] for k in range(LINES)], e in (E, N), lane)
        for k, line_k in enumerate(merged):
            sent[e, 0, k : k + 1, :] = line_k
        for k in range(len(merged), 7):
            sent[e, 0, k : k + 1, :] = jnp.zeros((1, side), jnp.float32)
        sent[e, 0, 7:8, :] = gathered
        sent[e, 1, 7:8, :] = gathered
    total = lax.broadcasted_iota(jnp.int32, (side, side), 0) + lax.broadcasted_iota(jnp.int32, (side, side), 1)
    mirror = (total == side - 1).astype(jnp.float32)
    whole = jnp.concatenate([sent[e, 0] for e in range(4)], axis=0)
    turned = jnp.dot(whole, mirror, precision=lax.Precision.HIGHEST, preferred_element_type=jnp.float32)
    for e in range(4):
        for k in range(7):
            line_k = turned[8 * e + k : 8 * e + k + 1, :]
            if k == 5:
                line_k = jnp.where(lane == 0, 0.0, pltpu.roll(line_k, 1, 1))
            sent[e, 1, k : k + 1, :] = jnp.where(links[2, e, f] == 1, line_k, sent[e, 0, k : k + 1, :])

    pl.semaphore_wait(bar, awaited)

    here = (w, c)
    remote = lambda a, b, ss, rs, d: pltpu.make_async_remote_copy(
        a, b, ss, rs, device_id=d, device_id_type=MESH
    )
    ring_copies = lambda e: [
        remote(sent.at[e, 1], ring.at[e, k], ring_send.at[e, k], ring_recv.at[e, k], ring_at(k))
        for k in range(1, pairs)
    ]
    ends_copies = lambda: [
        remote(ends, ring_ends.at[k], ring_ends_send.at[k], ring_ends_recv.at[k], ring_at(k)) for k in range(1, pairs)
    ]
    for e, has, q, line in edges:

        @pl.when(has)
        def _(e=e):
            for copy in ring_copies(e):
                copy.start()

    @pl.when(corner)
    def _():
        for copy in ends_copies():
            copy.start()

    near = [(E, W, 0, 1), (N, S, 1, 0), (W, E, 0, -1), (S, N, -1, 0)]
    diagonal = [(0, 1, 1), (1, 1, -1), (2, -1, 1), (3, -1, -1)]
    near_copy = lambda e, to, dr, dc: remote(
        sent.at[e, 0], rims_ref.at[to, 8], near_send.at[e], near_recv.at[e], at(f, r + dr, c + dc)
    )
    diag_copy = lambda k, dr, dc: remote(ends, diag_ref.at[k], diag_send.at[k], diag_recv.at[k], at(f, r + dr, c + dc))
    for e, to, dr, dc in near:

        @pl.when(inside(r + dr, c + dc))
        def _(e=e, to=to, dr=dr, dc=dc):
            near_copy(e, to, dr, dc).start()

    for k, dr, dc in diagonal:

        @pl.when(inside(r + dr, c + dc))
        def _(k=k, dr=dr, dc=dc):
            diag_copy(k, dr, dc).start()

    for e, has, q, line in edges:

        @pl.when(has)
        def _(e=e):
            for copy in ring_copies(e):
                copy.wait_recv()

    for e, has, q, line in edges:
        to_ws = e in (E, N)
        kind = 1 if e in (N, S) else 0
        lines = [(h, to) for h in range(2) for to in ((W, S) if to_ws else (E, N))]

        @pl.when(has)
        def _(e=e, q=q, line=line, kind=kind, lines=lines):
            ring[e, 0] = sent[e, 1]
            for j, (h, to) in enumerate(lines):
                far_x = links[0, to, x * 2 + h] // 2
                chosen[e, j] = ring[e, lax.rem(x - far_x + pairs, pairs)]
            for j, (h, to) in enumerate(lines):
                g = x * 2 + h
                place = lambda p, to=to: (p, line) if to in (W, E) else (line, p)
                for par, p in enumerate((q, last - q)):
                    slot = (half * 2 + kind) * 2 + par
                    row, col = place(p)
                    mine = (g == f) & (row == r) & (col == c)

                    @pl.when(~mine)
                    def _(j=j, to=to, slot=slot, g=g, row=row, col=col):
                        remote(
                            chosen.at[e, j], rims_ref.at[to, slot], main_send.at[e], main_recv.at[to], at(g, row, col)
                        ).start()

                    @pl.when(mine)
                    def _(j=j, to=to, slot=slot):
                        pltpu.make_async_copy(chosen.at[e, j], rims_ref.at[to, slot], main_recv.at[to]).start()

            for j, (h, to) in enumerate(lines):
                g = x * 2 + h
                place = lambda p, to=to: (p, line) if to in (W, E) else (line, p)
                for kind_x, p in enumerate(ext_to(q)):
                    slot = (half * 2 + kind) * 4 + kind_x
                    row, col = place(p)

                    @pl.when((p >= 0) & (p <= last))
                    def _(j=j, to=to, slot=slot, g=g, row=row, col=col):
                        remote(
                            chosen.at[e, j, pl.ds(7, 1)], ends_ref.at[to, slot], ext_send.at[e], ext_recv.at[to], at(g, row, col)
                        ).start()

    corner_copy = lambda i: remote(ring_ends, table_ref.at[me_corner], corner_send.at[0], corner_recv.at[0], corner_at(i))

    @pl.when(corner)
    def _():
        for copy in ends_copies():
            copy.wait_recv()
        ring_ends[0] = ends[...]
        for i in range(8):

            @pl.when(i != me_corner)
            def _(i=i):
                corner_copy(i).start()

        pltpu.make_async_copy(ring_ends, table_ref.at[me_corner], corner_recv.at[0]).start()

    take = lambda ref, ss, rs: remote(ref, ref, ss, rs, here)
    for e, to, dr, dc in near:

        @pl.when(inside(r + dr, c + dc))
        def _(e=e, to=to, dr=dr, dc=dc):
            near_copy(e, to, dr, dc).wait_send()

    for k, dr, dc in diagonal:

        @pl.when(inside(r + dr, c + dc))
        def _(k=k, dr=dr, dc=dc):
            diag_copy(k, dr, dc).wait_send()

    for e, has, q, line in edges:

        @pl.when(has)
        def _(e=e, q=q):
            for copy in ring_copies(e):
                copy.wait_send()

            @pl.when(~own)
            def _():
                take(rims_ref.at[e, pl.ds(0, 8)], main_send.at[e], main_recv.at[e]).wait_send()

            @pl.when(own)
            def _():
                take(rims_ref.at[e, pl.ds(0, 7)], main_send.at[e], main_recv.at[e]).wait_send()

            @pl.when(is_end(q))
            def _():
                take(ends_ref.at[e, pl.ds(0, 8)], ext_send.at[e], ext_recv.at[e]).wait_send()

            @pl.when(~is_end(q))
            def _():
                take(ends_ref.at[e], ext_send.at[e], ext_recv.at[e]).wait_send()

    @pl.when(corner)
    def _():
        for copy in ends_copies():
            copy.wait_send()
        take(table_ref.at[pl.ds(0, 7)], corner_send.at[0], corner_recv.at[0]).wait_send()

    for e, to, dr, dc in near:

        @pl.when(inside(r - dr, c - dc))
        def _(e=e, to=to):
            take(rims_ref.at[to, 8], near_send.at[e], near_recv.at[e]).wait_recv()

    for k, dr, dc in diagonal:

        @pl.when(inside(r - dr, c - dc))
        def _(k=k):
            take(diag_ref.at[k], diag_send.at[k], diag_recv.at[k]).wait_recv()

    link = lambda face, edge, k: links[k, edge, face]
    end = lambda row, k, line: row[:, 16 * k + line : 16 * k + line + 1]
    at_end = lambda row, high, k, line: jnp.where(high == 1, end(row, 3 - k, line), end(row, k, line))

    def corner_of(face, edge, high):
        row = jnp.where(edge == S, 0, jnp.where(edge == N, 1, high))
        col = jnp.where(edge == W, 0, jnp.where(edge == E, 1, high))
        return table_ref[face % 2 * 4 + row * 2 + col, lax.rem(x - face // 2 + pairs, pairs), edge]

    def beyond(face, edge, high):
        far, far_edge, turn = (link(face, edge, k) for k in range(3))
        stop = high ^ turn
        return at_end(corner_of(far, far_edge, stop), stop, 0, 8)

    def at_corner(face, edge, low_end):
        vertical = (edge == W) | (edge == E)
        side_edge = jnp.where(vertical, S, W) if low_end else jnp.where(vertical, N, E)
        start = (edge >= E).astype(jnp.int32)
        far, far_edge, turn = (link(face, side_edge, k) for k in range(3))
        high = start ^ turn
        row = corner_of(far, far_edge, high)
        far_vertical = (far_edge == W) | (far_edge == E)
        third = beyond(far, jnp.where(far_vertical, N, E), (far_edge >= E).astype(jnp.int32))
        ahead = jnp.where(high == 1, third, end(row, 1, 5))
        s1 = at_end(row, high, 0, 1) - G * (ahead - at_end(row, high, 0, 5))
        if low_end:
            parts = {(3, 0): at_end(row, high, 0, 0), (3, 1): s1}
        else:
            parts = {(0, 0): at_end(row, high, 0, 0)}
            across = at_end(row, high, 0, 8)
            parts.update({(0, 1): s1, (0, 5): across, (1, 5): across, (0, 6): at_end(row, high, 0, 3)})
            parts.update({(0, 7): at_end(row, high, 0, 4), (0, 8): at_end(row, high, 1, 8)})
        made = jnp.zeros((1, side), jnp.float32)
        for (k, line), value in parts.items():
            made = jnp.where(lane == 16 * k + line, value, made)
        return made

    choices = []
    for e, on_face, seg, _ in edges:
        to_ws = e in (W, S)
        across = e in (W, E)
        face, partner, turn = (link(f, e, k) for k in range(3))
        kind = (partner == (N if to_ws else S)).astype(jnp.int32)
        q = jnp.where(turn == 1, last - seg, seg)
        slot = jnp.where(on_face, (face % 2 * 2 + kind) * 2 + turn, 8)
        slot_x = jnp.where(on_face, (face % 2 * 2 + kind) * 4 + 2 * turn, 0)
        strip = (e + 2) % 4
        lo_at, hi_at = {W: (0, 2), S: (0, 1), E: (1, 3), N: (2, 3)}[e]
        flag = jnp.where(on_face, turn, 0).astype(jnp.float32)
        picked[e, 12:13, :] = jnp.zeros((1, side), jnp.float32) + flag
        choices.append((e, on_face, face, partner, q, slot, slot_x, strip, lo_at, hi_at))

    for e, has, q, line in edges:

        @pl.when(has)
        def _(e=e, q=q):
            take(rims_ref.at[e, pl.ds(0, 8)], main_send.at[0], main_recv.at[e]).wait_recv()

            @pl.when(is_end(q))
            def _():
                take(ends_ref.at[e, pl.ds(0, 8)], ext_send.at[0], ext_recv.at[e]).wait_recv()

            @pl.when(~is_end(q))
            def _():
                take(ends_ref.at[e], ext_send.at[0], ext_recv.at[e]).wait_recv()

    @pl.when(corner)
    def _():
        take(table_ref, corner_send.at[0], corner_recv.at[0]).wait_recv()

    for e, on_face, face, partner, q, slot, slot_x, strip, lo_at, hi_at in choices:
        picked[e, 0:8, :] = rims_ref[e, slot]
        picked[e, 10:11, :] = jnp.where(on_face, ends_ref[e, slot_x], diag_ref[lo_at, strip])
        picked[e, 11:12, :] = jnp.where(on_face, ends_ref[e, slot_x + 1], diag_ref[hi_at, strip])

        @pl.when(corner & on_face)
        def _(e=e, face=face, partner=partner, q=q):
            picked[e, 10:11, :] = jnp.where(q == 0, at_corner(face, partner, True), picked[e, 10:11, :])
            picked[e, 11:12, :] = jnp.where(q == last, at_corner(face, partner, False), picked[e, 11:12, :])


def substeps(sides, picked, coef, *refs):
    fields, refs = refs[:8], refs[8:]
    s_out, u_out, v_out, h_out, levels, sums, out_sem, sum_sem = refs
    last = sides - 1
    side = levels.shape[1]
    c = lax.axis_index("narrow")
    r = lax.rem(lax.axis_index("wide"), sides)
    lane = lax.broadcasted_iota(jnp.int32, (1, side), 1)
    rows = lax.broadcasted_iota(jnp.int32, (side, side), 0)
    cols = lax.broadcasted_iota(jnp.int32, (side, side), 1)
    diagonal = rows == cols
    pick = lambda cond, a, b: jnp.where(cond, a, b)
    up_by = lambda x, fill: jnp.where(lane == side - 1, fill, pltpu.roll(x, side - 1, 1))
    down_by = lambda x, fill: jnp.where(lane == 0, fill, pltpu.roll(x, 1, 1))
    head = lambda x: x[:, 0:1]
    tail = lambda x: x[:, side - 1 : side]
    end = lambda row, k, line: row[:, 16 * k + line : 16 * k + line + 1]

    def ghost(edge, to_ws):
        block = picked[edge]
        line = [block[k : k + 1, :] for k in range(6 if to_ws else 5)]
        own, lo_x, hi_x = (block[k : k + 1, :] for k in (7, 10, 11))
        flipped = block[12:13, 0:1] > 0.5
        lo = dict(
            s0=end(lo_x, 3, 0), s1=end(lo_x, 3, 1) - G * (end(own, 0, 5) - end(lo_x, 3, 5)),
            F=end(lo_x, 3, 8), R=end(lo_x, 3, 3), Dn=end(lo_x, 3, 4), Fb=end(lo_x, 2, 8), g=end(lo_x, 3, 15),
        )
        hi = dict(
            s0=end(hi_x, 0, 0), s1=end(hi_x, 0, 1) - G * (end(hi_x, 1, 5) - end(hi_x, 0, 5)),
            T0=end(hi_x, 0, 5), Q=end(hi_x, 0, 6), D=end(hi_x, 0, 7), Tb=end(hi_x, 0, 8),
            F=end(hi_x, 0, 8), R=end(hi_x, 0, 3), Dn=end(hi_x, 0, 4), Fb=end(hi_x, 1, 8), g=end(hi_x, 0, 15),
        )
        shared = ("s0", "s1", "F", "R", "Dn", "Fb", "g")
        new_lo = {n: pick(flipped, hi[n], lo[n]) for n in shared}
        new_hi = {n: pick(flipped, lo[n], hi[n]) for n in shared}
        for name in ("T0", "Q", "D", "Tb"):
            new_hi[name] = hi[name]
        if to_ws:
            line[5] = pick((lane == 0) & flipped, hi["D"], line[5])
            new_hi["D"] = pick(flipped, end(own, 0, 7), hi["D"])
        new_lo["first"] = pick(flipped, -hi["T0"], end(own, 0, 5))
        theirs = (flipped, lo, hi, own)
        return line, new_lo, new_hi, theirs

    (wl, w_lo, w_hi, w_own), (sl, s_lo, s_hi, s_own) = ghost(W, True), ghost(S, True)
    (el, e_lo, e_hi, e_own), (nl, n_lo, n_hi, n_own) = ghost(E, False), ghost(N, False)

    for d, x in ((w_lo, s_lo), (w_hi, n_lo), (s_lo, w_lo), (s_hi, e_lo)):
        d["s1"] = d["s1"] - d["g"] * x["first"]

    west, south, east, north = c == 0, r == 0, c == last, r == last
    take_w, take_s = west & ~south, south & ~west
    sw_w = {n: pick(take_s, s_lo[n], w_lo[n]) for n in ("s0", "s1")}
    sw_s = {n: pick(take_w, w_lo[n], s_lo[n]) for n in ("s0", "s1")}
    w_lo.update(sw_w)
    s_lo.update(sw_s)
    share = (("s0", "s0"), ("s1", "s1"), ("T0", "F"), ("Q", "R"), ("D", "Dn"), ("Tb", "Fb"))
    take_e, take_s = east & ~south, south & ~east
    se_s = {a: pick(take_e, e_lo[b], s_hi[a]) for a, b in share}
    e_lo["s0"] = pick(take_s, s_hi["s0"], e_lo["s0"])
    s_hi.update(se_s)
    take_n, take_w = north & ~west, west & ~north
    nw_w = {a: pick(take_n, n_lo[b], w_hi[a]) for a, b in share}
    n_lo["s0"] = pick(take_w, w_hi["s0"], n_lo["s0"])
    w_hi.update(nw_w)
    take_e, take_n = east & ~north, north & ~east
    share = (("s0", "s0"), ("T0", "F"), ("Q", "R"), ("D", "Dn"))
    ne_n = {a: pick(take_e, e_hi[b], n_hi[a]) for a, b in share}
    ne_e = {a: pick(take_n, n_hi[b], e_hi[a]) for a, b in share}
    n_hi.update(ne_n)
    e_hi.update(ne_e)

    def missing(lo, hi, theirs):
        flipped, their_lo, their_hi, own = theirs
        place = pick(flipped, side - 1 - lane, lane)
        t0, q, d, s0 = (pick(flipped, their_hi[n], hi[n]) for n in ("T0", "Q", "D", "s0"))
        tb = pick(flipped, their_hi["Tb"], hi["Tb"])
        low = end(own, 0, 7) * pick(flipped, their_lo["s0"], lo["s0"])
        t1 = q - d * (s0 - end(own, 3, 0))
        return place == side - 1, place == 0, t0, t1, 0.8 * t0 + 0.1 * q + 0.1 * t1, tb, low

    class HeightRim:
        def __init__(self, line, lo, hi, theirs):
            top, bottom, t0, t1, t2, tb, low = missing(lo, hi, theirs)
            s0, x1, x2, x3, back, d = line
            x1 = x1 - jnp.where(top, G * t0, 0.0)
            x2 = x2 - jnp.where(top, G * t1, 0.0) + jnp.where(bottom, G * low, 0.0)
            x3 = x3 - jnp.where(top, G * t2 + G * back * (G * tb), 0.0) + jnp.where(bottom, G * (0.1 * low), 0.0)
            self.line = s0, x1, x2, x3, back, d
            self.lo, self.hi = lo, hi

        def at(self, n, flux):
            s0, x1, x2, x3, back, d = self.line
            if n == 0:
                return s0
            if n == 1:
                self.s1 = x1 - G * flux
                return self.s1
            s1 = self.s1
            if n == 2:
                self.s2 = x2 + 0.1 * s1 - G * flux
                return self.s2
            slope = d * (s1 - down_by(s1, self.lo["s1"]))
            slope_hi = self.hi["D"] * (self.hi["s1"] - tail(s1))
            return x3 + 0.81 * s1 + 0.1 * self.s2 - G * back * s1 - G * flux + G * (up_by(slope, slope_hi) - slope)

    class FluxRim:
        def __init__(self, line, lo, hi, theirs):
            top, bottom, t0, t1, _, _, low = missing(lo, hi, theirs)
            f0, p1, p2, p3, d = line
            p2 = p2 + d * jnp.where(top, G * t0, 0.0)
            p3 = p3 + d * (jnp.where(top, G * (0.1 * t0 + t1), 0.0) - jnp.where(bottom, G * low, 0.0))
            self.line = f0, p1, p2, p3, d

        def at(self, n, height):
            f0, p1, p2, p3, d = self.line
            if n == 0:
                return f0
            if n == 1:
                self.f1 = p1 + d * height
                return self.f1
            if n == 2:
                self.f2 = p2 + 0.1 * self.f1 + d * height
                return self.f2
            return p3 + (0.81 - G * d) * self.f1 + 0.1 * self.f2 + d * height

    rim_w, rim_s = HeightRim(wl, w_lo, w_hi, w_own), HeightRim(sl, s_lo, s_hi, s_own)
    rim_e, rim_n = FluxRim(el, e_lo, e_hi, e_own), FluxRim(nl, n_lo, n_hi, n_own)
    as_row = lambda col: jnp.sum(jnp.where(diagonal, col, 0.0), axis=0, keepdims=True)
    as_col = lambda row: jnp.sum(jnp.where(diagonal, row, 0.0), axis=1, keepdims=True)
    sp_, s_, up_, u_, vp_, v_, dw_, ds_ = (x[...] for x in fields)
    first_col, last_col = cols == 0, cols == side - 1
    first_row, last_row = rows == 0, rows == side - 1
    flux_w = flux_s = height_e = height_n = None
    snaps = []
    for n in range(SUBSTEPS):
        fw, fs = dw_ * u_, ds_ * v_
        west_line, south_line = rim_w.at(n, flux_w), rim_s.at(n, flux_s)
        east_line, north_line = rim_e.at(n, height_e), rim_n.at(n, height_n)
        flux_w, flux_s = as_row(fw[:, 0:1]), fs[0:1, :]
        height_e, height_n = as_row(s_[:, side - 1 : side]), s_[side - 1 : side, :]
        fe = jnp.where(last_col, as_col(east_line), pltpu.roll(fw, side - 1, 1))
        fn = jnp.where(last_row, north_line, pltpu.roll(fs, side - 1, 0))
        sw = jnp.where(first_col, as_col(west_line), pltpu.roll(s_, 1, 1))
        ss = jnp.where(first_row, south_line, pltpu.roll(s_, 1, 0))
        s_next = sp_ - G * ((fe - fw) + (fn - fs))
        u_next = up_ - G * (s_ - sw)
        v_next = vp_ - G * (s_ - ss)
        sp_ = s_ + 0.1 * (sp_ - 2.0 * s_ + s_next)
        up_ = u_ + 0.1 * (up_ - 2.0 * u_ + u_next)
        vp_ = v_ + 0.1 * (vp_ - 2.0 * v_ + v_next)
        s_, u_, v_ = s_next, u_next, v_next
        snaps.append(s_)
    stores = []
    for k, (x, out) in enumerate(((s_, s_out), (u_, u_out), (v_, v_out))):
        levels[k] = x
        stores.append(pltpu.make_async_copy(levels.at[k], out, out_sem.at[k]))
        stores[-1].start()
    for k in range(2 * CONSTITUENTS):
        total = coef[k : k + 1, 0:1] * snaps[0]
        for n in range(1, SUBSTEPS):
            total += coef[k : k + 1, n : n + 1] * snaps[n]
        sums[k] = total
        stores.append(pltpu.make_async_copy(sums.at[k], h_out.at[k], sum_sem.at[k]))
        stores[-1].start()
    for copy in stores:
        copy.wait()


def solution(mesh):
    def body(sp, s, up, u, vp, v, dw, ds, links, ph):
        side = s.shape[0]
        sides = mesh.shape["narrow"]
        faces = mesh.shape["wide"] // sides
        f32 = jnp.float32
        shape = lambda *dims: jax.ShapeDtypeStruct(dims, f32)
        hbm = pl.BlockSpec(memory_space=pl.ANY)
        vmem = pl.BlockSpec(memory_space=pltpu.VMEM)
        dma = pltpu.SemaphoreType.DMA
        scratch = lambda *dims: pltpu.VMEM(dims, f32)
        pairs = faces // 2
        links = jnp.transpose(links, (2, 1, 0))
        fields = (sp, s, up, u, vp, v, dw, ds)
        grant = 8 << 20
        in_hbm = [pltpu.with_memory_space_constraint(a, pltpu.HBM) for a in (links, ph, *fields)]
        got = pl.pallas_call(
            functools.partial(exchange, sides, faces),
            out_shape=(shape(4, 16, side), shape(2 * CONSTITUENTS, side)),
            in_specs=[hbm] * 10,
            out_specs=(vmem,) * 2,
            scratch_shapes=[
                pltpu.SMEM(links.shape, jnp.int32),
                pltpu.SMEM(ph.shape, f32),
                scratch(4, 9, 8, side),
                scratch(4, 16, 1, side),
                scratch(8, pairs, 4, 1, side),
                scratch(4, 4, 1, side),
                scratch(8, side, side),
                scratch(4, 16, side),
                scratch(4, 2, 8, side),
                scratch(4, 1, side),
                scratch(4, pairs, 8, side),
                scratch(pairs, 4, 1, side),
                scratch(4, 4, 8, side),
                dma((8,)), dma((2,)), dma((4,)), dma((4,)), dma((4,)), dma((4,)),
                dma((4, pairs)), dma((4, pairs)), dma((pairs,)), dma((pairs,)),
                dma((4,)), dma((4,)), dma((4,)), dma((4,)), dma((1,)), dma((1,)),
            ],
            compiler_params=pltpu.CompilerParams(collective_id=0, has_side_effects=True, vmem_limit_bytes=grant),
        )(*in_hbm)
        tile = shape(side, side)
        return pl.pallas_call(
            functools.partial(substeps, sides),
            out_shape=(tile, tile, tile, shape(2 * CONSTITUENTS, side, side)),
            in_specs=[vmem] * 10,
            out_specs=(hbm,) * 4,
            scratch_shapes=[scratch(3, side, side), scratch(2 * CONSTITUENTS, side, side), dma((3,)), dma((2 * CONSTITUENTS,))],
            compiler_params=pltpu.CompilerParams(vmem_limit_bytes=grant),
        )(*got, *fields)

    tiles = P("wide", "narrow")
    return jax.shard_map(
        body,
        mesh=mesh,
        in_specs=(tiles,) * 8 + (P(), P()),
        out_specs=(tiles, tiles, tiles, P(None, "wide", "narrow")),
        check_vma=False,
    )
```

```python
import functools

import jax
import jax.numpy as jnp
from jax import lax
from jax.experimental import pallas as pl
from jax.experimental.pallas import tpu as pltpu
from jax.sharding import PartitionSpec as P

MESH = pl.DeviceIdType.MESH
SUBSTEPS = 4
CONSTITUENTS = 8
tide_omega = (
    0.0001405189,
    0.0001454441,
    0.0001378797,
    0.0001458423,
    7.292117e-05,
    6.759774e-05,
    7.251056e-05,
    6.495854e-05,
)
step_seconds = 25.0
G = 0.6
W, S, E, N = range(4)
LINES = 9


def rims(s, sp, n, np_, t, tp, dn, dt):
    last = s.shape[0] - 1
    row = lambda x, i: x[i : i + 1, :]
    a, b = last, last - 1
    n1 = row(np_, a) - G * (row(s, a) - row(s, b))
    fa = row(dn, a) * row(n, a)
    fb = row(dn, b) * row(n, b)
    back = G * row(dn, a)
    older = 0.8 * row(n, a) + 0.1 * row(np_, a) + 0.1 * n1
    high = [
        row(s, a),
        row(sp, a) + G * fa,
        0.8 * row(s, a) + 0.1 * row(sp, a) + G * (row(dn, a) * n1),
        0.08 * row(s, a)
        + 0.01 * row(sp, a)
        + G * (row(dn, a) * older + back * (row(sp, b) - G * (fa - fb))),
        back,
        row(dt, a) * row(t, a),
        row(dt, a) * row(tp, a),
        G * row(dt, a),
        row(dt, b) * row(t, b),
    ]
    a, b = 0, 1
    n1 = row(np_, b) - G * (row(s, b) - row(s, a))
    fa = row(dn, a) * row(n, a)
    fb = row(dn, b) * row(n, b)
    low = [
        row(s, a),
        row(sp, a) - G * (fb - fa),
        0.8 * row(s, a) + 0.1 * row(sp, a) - G * (row(dn, b) * n1),
        row(dn, a) * row(np_, a),
        G * row(dn, a),
        row(dt, a) * row(t, a),
        row(dt, a) * row(tp, a),
        G * row(dt, a),
        fa,
    ]
    return low, high


def merge(raw, high, lane):
    up0 = lambda x: jnp.where(lane == lane.shape[1] - 1, 0.0, pltpu.roll(x, lane.shape[1] - 1, 1))
    down0 = lambda x: jnp.where(lane == 0, 0.0, pltpu.roll(x, 1, 1))
    s0, y1, y2, a, b, t0, q, d, last_line = raw
    t1 = q - d * (s0 - down0(s0))
    if high:
        older = 0.8 * t0 + 0.1 * q + 0.1 * t1
        x3 = a - G * (up0(older) - older) - G * b * (G * (up0(last_line) - last_line))
        return [s0, y1 - G * (up0(t0) - t0), y2 - G * (up0(t1) - t1), x3, b, d]
    f0, was = last_line, a
    s1 = y1 - G * (up0(t0) - t0)
    s2 = y2 + 0.1 * s1 - G * (up0(t1) - t1)
    return [f0, was - b * s0, 0.8 * f0 + 0.1 * was - b * s1, 0.08 * f0 + 0.01 * was - b * s2, b]


def exchange(sides, faces, links_ref, ph_ref, *refs):
    fields, refs = refs[:8], refs[8:]
    (
        picked, coef,
        links, ph, rims_ref, ends_ref, table_ref, diag_ref,
        held, pack, sent, ends, ring, ring_ends, chosen,
        load_sem, links_sem, near_send, near_recv, diag_send, diag_recv, ring_send, ring_recv, ring_ends_send, ring_ends_recv,
        main_send, main_recv, ext_send, ext_recv, corner_send, corner_recv,
    ) = refs
    last = sides - 1
    pairs = faces // 2
    side = held.shape[1]
    w = lax.axis_index("wide")
    c = lax.axis_index("narrow")
    f = w // sides
    r = w % sides
    x, half = f // 2, f % 2
    at = lambda face, row, col: (face * sides + row, col)
    signal = lambda bar, d: pl.semaphore_signal(bar, inc=1, device_id=d, device_id_type=MESH)
    is_end = lambda q: (q == 0) | (q == last)
    corner = is_end(r) & is_end(c)
    rim = is_end(r) | is_end(c)
    inside = lambda row, col: (row >= 0) & (row <= last) & (col >= 0) & (col <= last)
    edges = [(W, c == 0, r, last), (S, r == 0, c, last), (E, c == last, r, 0), (N, r == last, c, 0)]
    ext_to = lambda q: (q + 1, q - 1, last - 1 - q, last + 1 - q)
    ext_from = lambda q: (q - 1, q + 1, last - 1 - q, last + 1 - q)
    corner_at = lambda i: at(x * 2 + i // 4, (i // 2) % 2 * last, i % 2 * last)
    me_corner = half * 4 + (r // last) * 2 + c // last
    ring_at = lambda k: at((f + 2 * k) % faces, r, c)

    bar = pltpu.get_barrier_semaphore()
    awaited = jnp.int32(0)
    for e, has, q, line in edges:

        @pl.when(has)
        def _(q=q, line=line):
            for h in range(2):
                g = x * 2 + h
                for p in (q, last - q):
                    for row, col in ((p, line), (line, p)):

                        @pl.when(~((g == f) & (row == r) & (col == c)))
                        def _(g=g, row=row, col=col):
                            signal(bar, at(g, row, col))

                for p in ext_from(q):

                    @pl.when((p >= 0) & (p <= last))
                    def _(g=g, p=p):
                        signal(bar, at(g, p, line))
                        signal(bar, at(g, line, p))

        ext = jnp.where(is_end(q), 8, 16)
        awaited += jnp.where(has, 8 + ext, 0)
    own = corner & (r != c)
    awaited -= jnp.where(own, 2, 0)

    @pl.when(rim)
    def _():
        for k in range(1, pairs):
            signal(bar, ring_at(k))

    @pl.when(corner)
    def _():
        for i in range(8):

            @pl.when(i != me_corner)
            def _(i=i):
                signal(bar, corner_at(i))

    awaited += jnp.where(rim, pairs - 1, 0) + jnp.where(corner, 7, 0)
    for dr in (-1, 0, 1):
        for dc in (-1, 0, 1):
            if (dr, dc) != (0, 0):
                there = inside(r + dr, c + dc)
                awaited += there.astype(jnp.int32)

                @pl.when(there)
                def _(dr=dr, dc=dc):
                    signal(bar, at(f, r + dr, c + dc))

    loads = [
        pltpu.make_async_copy(ph_ref, ph, links_sem.at[0]),
        pltpu.make_async_copy(links_ref, links, links_sem.at[1]),
    ] + [pltpu.make_async_copy(ref, held.at[k], load_sem.at[k]) for k, ref in enumerate(fields)]
    for copy in loads:
        copy.start()
    for copy in loads:
        copy.wait()

    which = lax.broadcasted_iota(jnp.int32, (CONSTITUENTS, side), 0)
    count = (lax.broadcasted_iota(jnp.int32, (CONSTITUENTS, side), 1) + 1).astype(jnp.float32)
    start = jnp.zeros((CONSTITUENTS, side), jnp.float32)
    rate = jnp.zeros((CONSTITUENTS, side), jnp.float32)
    for k in range(CONSTITUENTS):
        start = jnp.where(which == k, ph[k], start)
        rate = jnp.where(which == k, jnp.float32(tide_omega[k]) * jnp.float32(step_seconds), rate)
    angle = start + rate * count
    coef[0:CONSTITUENTS, :] = jnp.cos(angle)
    coef[CONSTITUENTS:, :] = jnp.sin(angle)

    sp, s, up, u, vp, v, dw, ds = (held.at[k] for k in range(8))
    lo, hi = rims(s[...], sp[...], v[...], vp[...], u[...], up[...], ds[...], dw[...])
    for k in range(LINES):
        pack[S, k : k + 1, :] = lo[k]
        pack[N, k : k + 1, :] = hi[k]
    flip = lambda ref: jnp.transpose(ref[...])
    lo, hi = rims(flip(s), flip(sp), flip(u), flip(up), flip(v), flip(vp), flip(dw), flip(ds))
    for k in range(LINES):
        pack[W, k : k + 1, :] = lo[k]
        pack[E, k : k + 1, :] = hi[k]
    for e in range(4):
        pack[e, LINES:16, :] = jnp.full((16 - LINES, side), G, jnp.float32)
    stacked = jnp.concatenate([pack[e] for e in range(4)] + [jnp.zeros((side - 64, side), jnp.float32)], axis=0)
    turned = jnp.transpose(stacked)
    lane = lax.broadcasted_iota(jnp.int32, (1, side), 1)
    for e in range(4):
        gathered = jnp.zeros((1, side), jnp.float32)
        for k, i in enumerate((0, 1, side - 2, side - 1)):
            moved = turned[i : i + 1, :]
            by = (16 * k - 16 * e) % side
            if by:
                moved = pltpu.roll(moved, by, 1)
            gathered = jnp.where((lane >= 16 * k) & (lane < 16 * k + 16), moved, gathered)
        ends[e] = gathered
        merged = merge([pack[e, k : k + 1, :] for k in range(LINES)], e in (E, N), lane)
        for k, line_k in enumerate(merged):
            sent[e, 0, k : k + 1, :] = line_k
        for k in range(len(merged), 7):
            sent[e, 0, k : k + 1, :] = jnp.zeros((1, side), jnp.float32)
        sent[e, 0, 7:8, :] = gathered
        sent[e, 1, 7:8, :] = gathered
    total = lax.broadcasted_iota(jnp.int32, (side, side), 0) + lax.broadcasted_iota(jnp.int32, (side, side), 1)
    mirror = (total == side - 1).astype(jnp.float32)
    whole = jnp.concatenate([sent[e, 0] for e in range(4)], axis=0)
    turned = jnp.dot(whole, mirror, precision=lax.Precision.HIGHEST, preferred_element_type=jnp.float32)
    for e in range(4):
        for k in range(7):
            line_k = turned[8 * e + k : 8 * e + k + 1, :]
            if k == 5:
                line_k = jnp.where(lane == 0, 0.0, pltpu.roll(line_k, 1, 1))
            sent[e, 1, k : k + 1, :] = jnp.where(links[2, e, f] == 1, line_k, sent[e, 0, k : k + 1, :])

    pl.semaphore_wait(bar, awaited)

    here = (w, c)
    remote = lambda a, b, ss, rs, d: pltpu.make_async_remote_copy(
        a, b, ss, rs, device_id=d, device_id_type=MESH
    )
    ring_copies = lambda e: [
        remote(sent.at[e, 1], ring.at[e, k], ring_send.at[e, k], ring_recv.at[e, k], ring_at(k))
        for k in range(1, pairs)
    ]
    ends_copies = lambda: [
        remote(ends, ring_ends.at[k], ring_ends_send.at[k], ring_ends_recv.at[k], ring_at(k)) for k in range(1, pairs)
    ]
    for e, has, q, line in edges:

        @pl.when(has)
        def _(e=e):
            for copy in ring_copies(e):
                copy.start()

    @pl.when(corner)
    def _():
        for copy in ends_copies():
            copy.start()

    near = [(E, W, 0, 1), (N, S, 1, 0), (W, E, 0, -1), (S, N, -1, 0)]
    diagonal = [(0, 1, 1), (1, 1, -1), (2, -1, 1), (3, -1, -1)]
    near_copy = lambda e, to, dr, dc: remote(
        sent.at[e, 0], rims_ref.at[to, 8], near_send.at[e], near_recv.at[e], at(f, r + dr, c + dc)
    )
    diag_copy = lambda k, dr, dc: remote(ends, diag_ref.at[k], diag_send.at[k], diag_recv.at[k], at(f, r + dr, c + dc))
    for e, to, dr, dc in near:

        @pl.when(inside(r + dr, c + dc))
        def _(e=e, to=to, dr=dr, dc=dc):
            near_copy(e, to, dr, dc).start()

    for k, dr, dc in diagonal:

        @pl.when(inside(r + dr, c + dc))
        def _(k=k, dr=dr, dc=dc):
            diag_copy(k, dr, dc).start()

    for e, has, q, line in edges:

        @pl.when(has)
        def _(e=e):
            for copy in ring_copies(e):
                copy.wait_recv()

    for e, has, q, line in edges:
        to_ws = e in (E, N)
        kind = 1 if e in (N, S) else 0
        lines = [(h, to) for h in range(2) for to in ((W, S) if to_ws else (E, N))]

        @pl.when(has)
        def _(e=e, q=q, line=line, kind=kind, lines=lines):
            ring[e, 0] = sent[e, 1]
            for j, (h, to) in enumerate(lines):
                far_x = links[0, to, x * 2 + h] // 2
                chosen[e, j] = ring[e, lax.rem(x - far_x + pairs, pairs)]
            for j, (h, to) in enumerate(lines):
                g = x * 2 + h
                place = lambda p, to=to: (p, line) if to in (W, E) else (line, p)
                for kind_x, p in enumerate(ext_to(q)):
                    slot = (half * 2 + kind) * 4 + kind_x
                    row, col = place(p)

                    @pl.when((p >= 0) & (p <= last))
                    def _(j=j, to=to, slot=slot, g=g, row=row, col=col):
                        remote(
                            chosen.at[e, j, pl.ds(7, 1)], ends_ref.at[to, slot], ext_send.at[e], ext_recv.at[to], at(g, row, col)
                        ).start()

            for j, (h, to) in enumerate(lines):
                g = x * 2 + h
                place = lambda p, to=to: (p, line) if to in (W, E) else (line, p)
                for par, p in enumerate((q, last - q)):
                    slot = (half * 2 + kind) * 2 + par
                    row, col = place(p)
                    mine = (g == f) & (row == r) & (col == c)

                    @pl.when(~mine)
                    def _(j=j, to=to, slot=slot, g=g, row=row, col=col):
                        remote(
                            chosen.at[e, j], rims_ref.at[to, slot], main_send.at[e], main_recv.at[to], at(g, row, col)
                        ).start()

                    @pl.when(mine)
                    def _(j=j, to=to, slot=slot):
                        pltpu.make_async_copy(chosen.at[e, j], rims_ref.at[to, slot], main_recv.at[to]).start()

    corner_copy = lambda i: remote(ring_ends, table_ref.at[me_corner], corner_send.at[0], corner_recv.at[0], corner_at(i))

    @pl.when(corner)
    def _():
        for copy in ends_copies():
            copy.wait_recv()
        ring_ends[0] = ends[...]
        for i in range(8):

            @pl.when(i != me_corner)
            def _(i=i):
                corner_copy(i).start()

        pltpu.make_async_copy(ring_ends, table_ref.at[me_corner], corner_recv.at[0]).start()

    take = lambda ref, ss, rs: remote(ref, ref, ss, rs, here)
    for e, to, dr, dc in near:

        @pl.when(inside(r + dr, c + dc))
        def _(e=e, to=to, dr=dr, dc=dc):
            near_copy(e, to, dr, dc).wait_send()

    for k, dr, dc in diagonal:

        @pl.when(inside(r + dr, c + dc))
        def _(k=k, dr=dr, dc=dc):
            diag_copy(k, dr, dc).wait_send()

    for e, has, q, line in edges:

        @pl.when(has)
        def _(e=e, q=q):
            for copy in ring_copies(e):
                copy.wait_send()

            @pl.when(~own)
            def _():
                take(rims_ref.at[e, pl.ds(0, 8)], main_send.at[e], main_recv.at[e]).wait_send()

            @pl.when(own)
            def _():
                take(rims_ref.at[e, pl.ds(0, 7)], main_send.at[e], main_recv.at[e]).wait_send()

            @pl.when(is_end(q))
            def _():
                take(ends_ref.at[e, pl.ds(0, 8)], ext_send.at[e], ext_recv.at[e]).wait_send()

            @pl.when(~is_end(q))
            def _():
                take(ends_ref.at[e], ext_send.at[e], ext_recv.at[e]).wait_send()

    @pl.when(corner)
    def _():
        for copy in ends_copies():
            copy.wait_send()
        take(table_ref.at[pl.ds(0, 7)], corner_send.at[0], corner_recv.at[0]).wait_send()

    for e, to, dr, dc in near:

        @pl.when(inside(r - dr, c - dc))
        def _(e=e, to=to):
            take(rims_ref.at[to, 8], near_send.at[e], near_recv.at[e]).wait_recv()

    for k, dr, dc in diagonal:

        @pl.when(inside(r - dr, c - dc))
        def _(k=k):
            take(diag_ref.at[k], diag_send.at[k], diag_recv.at[k]).wait_recv()

    link = lambda face, edge, k: links[k, edge, face]
    end = lambda row, k, line: row[:, 16 * k + line : 16 * k + line + 1]
    at_end = lambda row, high, k, line: jnp.where(high == 1, end(row, 3 - k, line), end(row, k, line))

    def corner_of(face, edge, high):
        row = jnp.where(edge == S, 0, jnp.where(edge == N, 1, high))
        col = jnp.where(edge == W, 0, jnp.where(edge == E, 1, high))
        return table_ref[face % 2 * 4 + row * 2 + col, lax.rem(x - face // 2 + pairs, pairs), edge]

    def beyond(face, edge, high):
        far, far_edge, turn = (link(face, edge, k) for k in range(3))
        stop = high ^ turn
        return at_end(corner_of(far, far_edge, stop), stop, 0, 8)

    def at_corner(face, edge, low_end):
        vertical = (edge == W) | (edge == E)
        side_edge = jnp.where(vertical, S, W) if low_end else jnp.where(vertical, N, E)
        start = (edge >= E).astype(jnp.int32)
        far, far_edge, turn = (link(face, side_edge, k) for k in range(3))
        high = start ^ turn
        row = corner_of(far, far_edge, high)
        far_vertical = (far_edge == W) | (far_edge == E)
        third = beyond(far, jnp.where(far_vertical, N, E), (far_edge >= E).astype(jnp.int32))
        ahead = jnp.where(high == 1, third, end(row, 1, 5))
        s1 = at_end(row, high, 0, 1) - G * (ahead - at_end(row, high, 0, 5))
        if low_end:
            parts = {(3, 0): at_end(row, high, 0, 0), (3, 1): s1}
        else:
            parts = {(0, 0): at_end(row, high, 0, 0)}
            across = at_end(row, high, 0, 8)
            parts.update({(0, 1): s1, (0, 5): across, (1, 5): across, (0, 6): at_end(row, high, 0, 3)})
            parts.update({(0, 7): at_end(row, high, 0, 4), (0, 8): at_end(row, high, 1, 8)})
        made = jnp.zeros((1, side), jnp.float32)
        for (k, line), value in parts.items():
            made = jnp.where(lane == 16 * k + line, value, made)
        return made

    choices = []
    for e, on_face, seg, _ in edges:
        to_ws = e in (W, S)
        across = e in (W, E)
        face, partner, turn = (link(f, e, k) for k in range(3))
        kind = (partner == (N if to_ws else S)).astype(jnp.int32)
        q = jnp.where(turn == 1, last - seg, seg)
        slot = jnp.where(on_face, (face % 2 * 2 + kind) * 2 + turn, 8)
        slot_x = jnp.where(on_face, (face % 2 * 2 + kind) * 4 + 2 * turn, 0)
        strip = (e + 2) % 4
        lo_at, hi_at = {W: (0, 2), S: (0, 1), E: (1, 3), N: (2, 3)}[e]
        flag = jnp.where(on_face, turn, 0).astype(jnp.float32)
        picked[e, 12:13, :] = jnp.zeros((1, side), jnp.float32) + flag
        choices.append((e, on_face, face, partner, q, slot, slot_x, strip, lo_at, hi_at))

    for e, has, q, line in edges:

        @pl.when(has)
        def _(e=e, q=q):
            take(rims_ref.at[e, pl.ds(0, 8)], main_send.at[0], main_recv.at[e]).wait_recv()

            @pl.when(is_end(q))
            def _():
                take(ends_ref.at[e, pl.ds(0, 8)], ext_send.at[0], ext_recv.at[e]).wait_recv()

            @pl.when(~is_end(q))
            def _():
                take(ends_ref.at[e], ext_send.at[0], ext_recv.at[e]).wait_recv()

    @pl.when(corner)
    def _():
        take(table_ref, corner_send.at[0], corner_recv.at[0]).wait_recv()

    for e, on_face, face, partner, q, slot, slot_x, strip, lo_at, hi_at in choices:
        picked[e, 0:8, :] = rims_ref[e, slot]
        picked[e, 10:11, :] = jnp.where(on_face, ends_ref[e, slot_x], diag_ref[lo_at, strip])
        picked[e, 11:12, :] = jnp.where(on_face, ends_ref[e, slot_x + 1], diag_ref[hi_at, strip])

        @pl.when(corner & on_face)
        def _(e=e, face=face, partner=partner, q=q):
            picked[e, 10:11, :] = jnp.where(q == 0, at_corner(face, partner, True), picked[e, 10:11, :])
            picked[e, 11:12, :] = jnp.where(q == last, at_corner(face, partner, False), picked[e, 11:12, :])


def substeps(sides, picked, coef, *refs):
    fields, refs = refs[:8], refs[8:]
    s_out, u_out, v_out, h_out, levels, sums, out_sem, sum_sem = refs
    last = sides - 1
    side = levels.shape[1]
    c = lax.axis_index("narrow")
    r = lax.rem(lax.axis_index("wide"), sides)
    lane = lax.broadcasted_iota(jnp.int32, (1, side), 1)
    rows = lax.broadcasted_iota(jnp.int32, (side, side), 0)
    cols = lax.broadcasted_iota(jnp.int32, (side, side), 1)
    diagonal = rows == cols
    pick = lambda cond, a, b: jnp.where(cond, a, b)
    up_by = lambda x, fill: jnp.where(lane == side - 1, fill, pltpu.roll(x, side - 1, 1))
    down_by = lambda x, fill: jnp.where(lane == 0, fill, pltpu.roll(x, 1, 1))
    head = lambda x: x[:, 0:1]
    tail = lambda x: x[:, side - 1 : side]
    end = lambda row, k, line: row[:, 16 * k + line : 16 * k + line + 1]

    def ghost(edge, to_ws):
        block = picked[edge]
        line = [block[k : k + 1, :] for k in range(6 if to_ws else 5)]
        own, lo_x, hi_x = (block[k : k + 1, :] for k in (7, 10, 11))
        flipped = block[12:13, 0:1] > 0.5
        lo = dict(
            s0=end(lo_x, 3, 0), s1=end(lo_x, 3, 1) - G * (end(own, 0, 5) - end(lo_x, 3, 5)),
            F=end(lo_x, 3, 8), R=end(lo_x, 3, 3), Dn=end(lo_x, 3, 4), Fb=end(lo_x, 2, 8), g=end(lo_x, 3, 15),
        )
        hi = dict(
            s0=end(hi_x, 0, 0), s1=end(hi_x, 0, 1) - G * (end(hi_x, 1, 5) - end(hi_x, 0, 5)),
            T0=end(hi_x, 0, 5), Q=end(hi_x, 0, 6), D=end(hi_x, 0, 7), Tb=end(hi_x, 0, 8),
            F=end(hi_x, 0, 8), R=end(hi_x, 0, 3), Dn=end(hi_x, 0, 4), Fb=end(hi_x, 1, 8), g=end(hi_x, 0, 15),
        )
        shared = ("s0", "s1", "F", "R", "Dn", "Fb", "g")
        new_lo = {n: pick(flipped, hi[n], lo[n]) for n in shared}
        new_hi = {n: pick(flipped, lo[n], hi[n]) for n in shared}
        for name in ("T0", "Q", "D", "Tb"):
            new_hi[name] = hi[name]
        if to_ws:
            line[5] = pick((lane == 0) & flipped, hi["D"], line[5])
            new_hi["D"] = pick(flipped, end(own, 0, 7), hi["D"])
        new_lo["first"] = pick(flipped, -hi["T0"], end(own, 0, 5))
        theirs = (flipped, lo, hi, own)
        return line, new_lo, new_hi, theirs

    (wl, w_lo, w_hi, w_own), (sl, s_lo, s_hi, s_own) = ghost(W, True), ghost(S, True)
    (el, e_lo, e_hi, e_own), (nl, n_lo, n_hi, n_own) = ghost(E, False), ghost(N, False)

    for d, x in ((w_lo, s_lo), (w_hi, n_lo), (s_lo, w_lo), (s_hi, e_lo)):
        d["s1"] = d["s1"] - d["g"] * x["first"]

    west, south, east, north = c == 0, r == 0, c == last, r == last
    take_w, take_s = west & ~south, south & ~west
    sw_w = {n: pick(take_s, s_lo[n], w_lo[n]) for n in ("s0", "s1")}
    sw_s = {n: pick(take_w, w_lo[n], s_lo[n]) for n in ("s0", "s1")}
    w_lo.update(sw_w)
    s_lo.update(sw_s)
    share = (("s0", "s0"), ("s1", "s1"), ("T0", "F"), ("Q", "R"), ("D", "Dn"), ("Tb", "Fb"))
    take_e, take_s = east & ~south, south & ~east
    se_s = {a: pick(take_e, e_lo[b], s_hi[a]) for a, b in share}
    e_lo["s0"] = pick(take_s, s_hi["s0"], e_lo["s0"])
    s_hi.update(se_s)
    take_n, take_w = north & ~west, west & ~north
    nw_w = {a: pick(take_n, n_lo[b], w_hi[a]) for a, b in share}
    n_lo["s0"] = pick(take_w, w_hi["s0"], n_lo["s0"])
    w_hi.update(nw_w)
    take_e, take_n = east & ~north, north & ~east
    share = (("s0", "s0"), ("T0", "F"), ("Q", "R"), ("D", "Dn"))
    ne_n = {a: pick(take_e, e_hi[b], n_hi[a]) for a, b in share}
    ne_e = {a: pick(take_n, n_hi[b], e_hi[a]) for a, b in share}
    n_hi.update(ne_n)
    e_hi.update(ne_e)

    def missing(lo, hi, theirs):
        flipped, their_lo, their_hi, own = theirs
        place = pick(flipped, side - 1 - lane, lane)
        t0, q, d, s0 = (pick(flipped, their_hi[n], hi[n]) for n in ("T0", "Q", "D", "s0"))
        tb = pick(flipped, their_hi["Tb"], hi["Tb"])
        low = end(own, 0, 7) * pick(flipped, their_lo["s0"], lo["s0"])
        t1 = q - d * (s0 - end(own, 3, 0))
        return place == side - 1, place == 0, t0, t1, 0.8 * t0 + 0.1 * q + 0.1 * t1, tb, low

    class HeightRim:
        def __init__(self, line, lo, hi, theirs):
            top, bottom, t0, t1, t2, tb, low = missing(lo, hi, theirs)
            s0, x1, x2, x3, back, d = line
            x1 = x1 - jnp.where(top, G * t0, 0.0)
            x2 = x2 - jnp.where(top, G * t1, 0.0) + jnp.where(bottom, G * low, 0.0)
            x3 = x3 - jnp.where(top, G * t2 + G * back * (G * tb), 0.0) + jnp.where(bottom, G * (0.1 * low), 0.0)
            self.line = s0, x1, x2, x3, back, d
            self.lo, self.hi = lo, hi

        def at(self, n, flux):
            s0, x1, x2, x3, back, d = self.line
            if n == 0:
                return s0
            if n == 1:
                self.s1 = x1 - G * flux
                return self.s1
            s1 = self.s1
            if n == 2:
                self.s2 = x2 + 0.1 * s1 - G * flux
                return self.s2
            slope = d * (s1 - down_by(s1, self.lo["s1"]))
            slope_hi = self.hi["D"] * (self.hi["s1"] - tail(s1))
            return x3 + 0.81 * s1 + 0.1 * self.s2 - G * back * s1 - G * flux + G * (up_by(slope, slope_hi) - slope)

    class FluxRim:
        def __init__(self, line, lo, hi, theirs):
            top, bottom, t0, t1, _, _, low = missing(lo, hi, theirs)
            f0, p1, p2, p3, d = line
            p2 = p2 + d * jnp.where(top, G * t0, 0.0)
            p3 = p3 + d * (jnp.where(top, G * (0.1 * t0 + t1), 0.0) - jnp.where(bottom, G * low, 0.0))
            self.line = f0, p1, p2, p3, d

        def at(self, n, height):
            f0, p1, p2, p3, d = self.line
            if n == 0:
                return f0
            if n == 1:
                self.f1 = p1 + d * height
                return self.f1
            if n == 2:
                self.f2 = p2 + 0.1 * self.f1 + d * height
                return self.f2
            return p3 + (0.81 - G * d) * self.f1 + 0.1 * self.f2 + d * height

    rim_w, rim_s = HeightRim(wl, w_lo, w_hi, w_own), HeightRim(sl, s_lo, s_hi, s_own)
    rim_e, rim_n = FluxRim(el, e_lo, e_hi, e_own), FluxRim(nl, n_lo, n_hi, n_own)
    as_row = lambda col: jnp.sum(jnp.where(diagonal, col, 0.0), axis=0, keepdims=True)
    as_col = lambda row: jnp.sum(jnp.where(diagonal, row, 0.0), axis=1, keepdims=True)
    sp_, s_, up_, u_, vp_, v_, dw_, ds_ = (x[...] for x in fields)
    first_col, last_col = cols == 0, cols == side - 1
    first_row, last_row = rows == 0, rows == side - 1
    flux_w = flux_s = height_e = height_n = None
    snaps = []
    for n in range(SUBSTEPS):
        fw, fs = dw_ * u_, ds_ * v_
        west_line, south_line = rim_w.at(n, flux_w), rim_s.at(n, flux_s)
        east_line, north_line = rim_e.at(n, height_e), rim_n.at(n, height_n)
        flux_w, flux_s = as_row(fw[:, 0:1]), fs[0:1, :]
        height_e, height_n = as_row(s_[:, side - 1 : side]), s_[side - 1 : side, :]
        fe = jnp.where(last_col, as_col(east_line), pltpu.roll(fw, side - 1, 1))
        fn = jnp.where(last_row, north_line, pltpu.roll(fs, side - 1, 0))
        sw = jnp.where(first_col, as_col(west_line), pltpu.roll(s_, 1, 1))
        ss = jnp.where(first_row, south_line, pltpu.roll(s_, 1, 0))
        s_next = sp_ - G * ((fe - fw) + (fn - fs))
        u_next = up_ - G * (s_ - sw)
        v_next = vp_ - G * (s_ - ss)
        sp_ = s_ + 0.1 * (sp_ - 2.0 * s_ + s_next)
        up_ = u_ + 0.1 * (up_ - 2.0 * u_ + u_next)
        vp_ = v_ + 0.1 * (vp_ - 2.0 * v_ + v_next)
        s_, u_, v_ = s_next, u_next, v_next
        snaps.append(s_)
    stores = []
    for k, (x, out) in enumerate(((s_, s_out), (u_, u_out), (v_, v_out))):
        levels[k] = x
        stores.append(pltpu.make_async_copy(levels.at[k], out, out_sem.at[k]))
        stores[-1].start()
    for k in range(2 * CONSTITUENTS):
        total = coef[k : k + 1, 0:1] * snaps[0]
        for n in range(1, SUBSTEPS):
            total += coef[k : k + 1, n : n + 1] * snaps[n]
        sums[k] = total
        stores.append(pltpu.make_async_copy(sums.at[k], h_out.at[k], sum_sem.at[k]))
        stores[-1].start()
    for copy in stores:
        copy.wait()


def solution(mesh):
    def body(sp, s, up, u, vp, v, dw, ds, links, ph):
        side = s.shape[0]
        sides = mesh.shape["narrow"]
        faces = mesh.shape["wide"] // sides
        f32 = jnp.float32
        shape = lambda *dims: jax.ShapeDtypeStruct(dims, f32)
        hbm = pl.BlockSpec(memory_space=pl.ANY)
        vmem = pl.BlockSpec(memory_space=pltpu.VMEM)
        dma = pltpu.SemaphoreType.DMA
        scratch = lambda *dims: pltpu.VMEM(dims, f32)
        pairs = faces // 2
        links = jnp.transpose(links, (2, 1, 0))
        fields = (sp, s, up, u, vp, v, dw, ds)
        grant = 8 << 20
        in_hbm = [pltpu.with_memory_space_constraint(a, pltpu.HBM) for a in (links, ph, *fields)]
        got = pl.pallas_call(
            functools.partial(exchange, sides, faces),
            out_shape=(shape(4, 16, side), shape(2 * CONSTITUENTS, side)),
            in_specs=[hbm] * 10,
            out_specs=(vmem,) * 2,
            scratch_shapes=[
                pltpu.SMEM(links.shape, jnp.int32),
                pltpu.SMEM(ph.shape, f32),
                scratch(4, 9, 8, side),
                scratch(4, 16, 1, side),
                scratch(8, pairs, 4, 1, side),
                scratch(4, 4, 1, side),
                scratch(8, side, side),
                scratch(4, 16, side),
                scratch(4, 2, 8, side),
                scratch(4, 1, side),
                scratch(4, pairs, 8, side),
                scratch(pairs, 4, 1, side),
                scratch(4, 4, 8, side),
                dma((8,)), dma((2,)), dma((4,)), dma((4,)), dma((4,)), dma((4,)),
                dma((4, pairs)), dma((4, pairs)), dma((pairs,)), dma((pairs,)),
                dma((4,)), dma((4,)), dma((4,)), dma((4,)), dma((1,)), dma((1,)),
            ],
            compiler_params=pltpu.CompilerParams(collective_id=0, has_side_effects=True, vmem_limit_bytes=grant),
        )(*in_hbm)
        tile = shape(side, side)
        return pl.pallas_call(
            functools.partial(substeps, sides),
            out_shape=(tile, tile, tile, shape(2 * CONSTITUENTS, side, side)),
            in_specs=[vmem] * 10,
            out_specs=(hbm,) * 4,
            scratch_shapes=[scratch(3, side, side), scratch(2 * CONSTITUENTS, side, side), dma((3,)), dma((2 * CONSTITUENTS,))],
            compiler_params=pltpu.CompilerParams(vmem_limit_bytes=grant),
        )(*got, *fields)

    tiles = P("wide", "narrow")
    return jax.shard_map(
        body,
        mesh=mesh,
        in_specs=(tiles,) * 8 + (P(), P()),
        out_specs=(tiles, tiles, tiles, P(None, "wide", "narrow")),
        check_vma=False,
    )
```

```python
import functools

import jax
import jax.numpy as jnp
from jax import lax
from jax.experimental import pallas as pl
from jax.experimental.pallas import tpu as pltpu
from jax.sharding import PartitionSpec as P

MESH = pl.DeviceIdType.MESH
SUBSTEPS = 4
CONSTITUENTS = 8
tide_omega = (
    0.0001405189,
    0.0001454441,
    0.0001378797,
    0.0001458423,
    7.292117e-05,
    6.759774e-05,
    7.251056e-05,
    6.495854e-05,
)
step_seconds = 25.0
G = 0.6
W, S, E, N = range(4)
LINES = 9


def rims(s, sp, n, np_, t, tp, dn, dt):
    last = s.shape[0] - 1
    row = lambda x, i: x[i : i + 1, :]
    a, b = last, last - 1
    n1 = row(np_, a) - G * (row(s, a) - row(s, b))
    fa = row(dn, a) * row(n, a)
    fb = row(dn, b) * row(n, b)
    back = G * row(dn, a)
    older = 0.8 * row(n, a) + 0.1 * row(np_, a) + 0.1 * n1
    high = [
        row(s, a),
        row(sp, a) + G * fa,
        0.8 * row(s, a) + 0.1 * row(sp, a) + G * (row(dn, a) * n1),
        0.08 * row(s, a)
        + 0.01 * row(sp, a)
        + G * (row(dn, a) * older + back * (row(sp, b) - G * (fa - fb))),
        back,
        row(dt, a) * row(t, a),
        row(dt, a) * row(tp, a),
        G * row(dt, a),
        row(dt, b) * row(t, b),
    ]
    a, b = 0, 1
    n1 = row(np_, b) - G * (row(s, b) - row(s, a))
    fa = row(dn, a) * row(n, a)
    fb = row(dn, b) * row(n, b)
    low = [
        row(s, a),
        row(sp, a) - G * (fb - fa),
        0.8 * row(s, a) + 0.1 * row(sp, a) - G * (row(dn, b) * n1),
        row(dn, a) * row(np_, a),
        G * row(dn, a),
        row(dt, a) * row(t, a),
        row(dt, a) * row(tp, a),
        G * row(dt, a),
        fa,
    ]
    return low, high


def merge(raw, high, lane):
    up0 = lambda x: jnp.where(lane == lane.shape[1] - 1, 0.0, pltpu.roll(x, lane.shape[1] - 1, 1))
    down0 = lambda x: jnp.where(lane == 0, 0.0, pltpu.roll(x, 1, 1))
    s0, y1, y2, a, b, t0, q, d, last_line = raw
    t1 = q - d * (s0 - down0(s0))
    if high:
        older = 0.8 * t0 + 0.1 * q + 0.1 * t1
        x3 = a - G * (up0(older) - older) - G * b * (G * (up0(last_line) - last_line))
        return [s0, y1 - G * (up0(t0) - t0), y2 - G * (up0(t1) - t1), x3, b, d]
    f0, was = last_line, a
    s1 = y1 - G * (up0(t0) - t0)
    s2 = y2 + 0.1 * s1 - G * (up0(t1) - t1)
    return [f0, was - b * s0, 0.8 * f0 + 0.1 * was - b * s1, 0.08 * f0 + 0.01 * was - b * s2, b]


def exchange(sides, faces, links_ref, ph_ref, *refs):
    fields, refs = refs[:8], refs[8:]
    (
        picked, coef,
        links, ph, rims_ref, ends_ref, table_ref, diag_ref,
        held, pack, sent, ends, ring, ring_ends, chosen,
        load_sem, links_sem, near_send, near_recv, diag_send, diag_recv, ring_send, ring_recv, ring_ends_send, ring_ends_recv,
        main_send, main_recv, ext_send, ext_recv, corner_send, corner_recv,
    ) = refs
    last = sides - 1
    pairs = faces // 2
    side = held.shape[1]
    w = lax.axis_index("wide")
    c = lax.axis_index("narrow")
    f = w // sides
    r = w % sides
    x, half = f // 2, f % 2
    at = lambda face, row, col: (face * sides + row, col)
    signal = lambda bar, d: pl.semaphore_signal(bar, inc=1, device_id=d, device_id_type=MESH)
    is_end = lambda q: (q == 0) | (q == last)
    corner = is_end(r) & is_end(c)
    rim = is_end(r) | is_end(c)
    inside = lambda row, col: (row >= 0) & (row <= last) & (col >= 0) & (col <= last)
    edges = [(W, c == 0, r, last), (S, r == 0, c, last), (E, c == last, r, 0), (N, r == last, c, 0)]
    ext_to = lambda q: (q + 1, q - 1, last - 1 - q, last + 1 - q)
    ext_from = lambda q: (q - 1, q + 1, last - 1 - q, last + 1 - q)
    corner_at = lambda i: at(x * 2 + i // 4, (i // 2) % 2 * last, i % 2 * last)
    me_corner = half * 4 + (r // last) * 2 + c // last
    ring_at = lambda k: at((f + 2 * k) % faces, r, c)

    bar = pltpu.get_barrier_semaphore()
    awaited = jnp.int32(0)
    for e, has, q, line in edges:

        @pl.when(has)
        def _(q=q, line=line):
            for h in range(2):
                g = x * 2 + h
                for p in (q, last - q):
                    for row, col in ((p, line), (line, p)):

                        @pl.when(~((g == f) & (row == r) & (col == c)))
                        def _(g=g, row=row, col=col):
                            signal(bar, at(g, row, col))

                for p in ext_from(q):

                    @pl.when((p >= 0) & (p <= last))
                    def _(g=g, p=p):
                        signal(bar, at(g, p, line))
                        signal(bar, at(g, line, p))

        ext = jnp.where(is_end(q), 8, 16)
        awaited += jnp.where(has, 8 + ext, 0)
    own = corner & (r != c)
    awaited -= jnp.where(own, 2, 0)

    @pl.when(rim)
    def _():
        for k in range(1, pairs):
            signal(bar, ring_at(k))

    @pl.when(corner)
    def _():
        for i in range(8):

            @pl.when(i != me_corner)
            def _(i=i):
                signal(bar, corner_at(i))

    awaited += jnp.where(rim, pairs - 1, 0) + jnp.where(corner, 7, 0)
    for dr in (-1, 0, 1):
        for dc in (-1, 0, 1):
            if (dr, dc) != (0, 0):
                there = inside(r + dr, c + dc)
                awaited += there.astype(jnp.int32)

                @pl.when(there)
                def _(dr=dr, dc=dc):
                    signal(bar, at(f, r + dr, c + dc))

    loads = [
        pltpu.make_async_copy(ph_ref, ph, links_sem.at[0]),
        pltpu.make_async_copy(links_ref, links, links_sem.at[1]),
    ] + [pltpu.make_async_copy(ref, held.at[k], load_sem.at[k]) for k, ref in enumerate(fields)]
    for copy in loads:
        copy.start()
    for copy in loads:
        copy.wait()

    which = lax.broadcasted_iota(jnp.int32, (CONSTITUENTS, side), 0)
    count = (lax.broadcasted_iota(jnp.int32, (CONSTITUENTS, side), 1) + 1).astype(jnp.float32)
    start = jnp.zeros((CONSTITUENTS, side), jnp.float32)
    rate = jnp.zeros((CONSTITUENTS, side), jnp.float32)
    for k in range(CONSTITUENTS):
        start = jnp.where(which == k, ph[k], start)
        rate = jnp.where(which == k, jnp.float32(tide_omega[k]) * jnp.float32(step_seconds), rate)
    angle = start + rate * count
    coef[0:CONSTITUENTS, :] = jnp.cos(angle)
    coef[CONSTITUENTS:, :] = jnp.sin(angle)

    sp, s, up, u, vp, v, dw, ds = (held.at[k] for k in range(8))
    lo, hi = rims(s[...], sp[...], v[...], vp[...], u[...], up[...], ds[...], dw[...])
    for k in range(LINES):
        pack[S, k : k + 1, :] = lo[k]
        pack[N, k : k + 1, :] = hi[k]
    flip = lambda ref: jnp.transpose(ref[...])
    lo, hi = rims(flip(s), flip(sp), flip(u), flip(up), flip(v), flip(vp), flip(dw), flip(ds))
    for k in range(LINES):
        pack[W, k : k + 1, :] = lo[k]
        pack[E, k : k + 1, :] = hi[k]
    for e in range(4):
        pack[e, LINES:16, :] = jnp.full((16 - LINES, side), G, jnp.float32)
    stacked = jnp.concatenate([pack[e] for e in range(4)] + [jnp.zeros((side - 64, side), jnp.float32)], axis=0)
    turned = jnp.transpose(stacked)
    lane = lax.broadcasted_iota(jnp.int32, (1, side), 1)
    for e in range(4):
        gathered = jnp.zeros((1, side), jnp.float32)
        for k, i in enumerate((0, 1, side - 2, side - 1)):
            moved = turned[i : i + 1, :]
            by = (16 * k - 16 * e) % side
            if by:
                moved = pltpu.roll(moved, by, 1)
            gathered = jnp.where((lane >= 16 * k) & (lane < 16 * k + 16), moved, gathered)
        ends[e] = gathered
        merged = merge([pack[e, k : k + 1, :] for k in range(LINES)], e in (E, N), lane)
        for k, line_k in enumerate(merged):
            sent[e, 0, k : k + 1, :] = line_k
        for k in range(len(merged), 7):
            sent[e, 0, k : k + 1, :] = jnp.zeros((1, side), jnp.float32)
        sent[e, 0, 7:8, :] = gathered
        sent[e, 1, 7:8, :] = gathered
    total = lax.broadcasted_iota(jnp.int32, (side, side), 0) + lax.broadcasted_iota(jnp.int32, (side, side), 1)
    mirror = (total == side - 1).astype(jnp.float32)
    whole = jnp.concatenate([sent[e, 0] for e in range(4)], axis=0)
    turned = jnp.dot(whole, mirror, precision=lax.Precision.HIGHEST, preferred_element_type=jnp.float32)
    for e in range(4):
        for k in range(7):
            line_k = turned[8 * e + k : 8 * e + k + 1, :]
            if k == 5:
                line_k = jnp.where(lane == 0, 0.0, pltpu.roll(line_k, 1, 1))
            sent[e, 1, k : k + 1, :] = jnp.where(links[2, e, f] == 1, line_k, sent[e, 0, k : k + 1, :])

    pl.semaphore_wait(bar, awaited)

    here = (w, c)
    remote = lambda a, b, ss, rs, d: pltpu.make_async_remote_copy(
        a, b, ss, rs, device_id=d, device_id_type=MESH
    )
    ring_copies = lambda e: [
        remote(sent.at[e, 1], ring.at[e, k], ring_send.at[e, k], ring_recv.at[e, k], ring_at(k))
        for k in (2, 1, 3)
    ]
    ends_copies = lambda: [
        remote(ends, ring_ends.at[k], ring_ends_send.at[k], ring_ends_recv.at[k], ring_at(k)) for k in range(1, pairs)
    ]
    for e, has, q, line in edges:

        @pl.when(has)
        def _(e=e):
            for copy in ring_copies(e):
                copy.start()

    @pl.when(corner)
    def _():
        for copy in ends_copies():
            copy.start()

    near = [(E, W, 0, 1), (N, S, 1, 0), (W, E, 0, -1), (S, N, -1, 0)]
    diagonal = [(0, 1, 1), (1, 1, -1), (2, -1, 1), (3, -1, -1)]
    near_copy = lambda e, to, dr, dc: remote(
        sent.at[e, 0], rims_ref.at[to, 8], near_send.at[e], near_recv.at[e], at(f, r + dr, c + dc)
    )
    diag_copy = lambda k, dr, dc: remote(ends, diag_ref.at[k], diag_send.at[k], diag_recv.at[k], at(f, r + dr, c + dc))
    for e, to, dr, dc in near:

        @pl.when(inside(r + dr, c + dc))
        def _(e=e, to=to, dr=dr, dc=dc):
            near_copy(e, to, dr, dc).start()

    for k, dr, dc in diagonal:

        @pl.when(inside(r + dr, c + dc))
        def _(k=k, dr=dr, dc=dc):
            diag_copy(k, dr, dc).start()

    for e, has, q, line in edges:

        @pl.when(has)
        def _(e=e):
            for copy in ring_copies(e):
                copy.wait_recv()

    for e, has, q, line in edges:
        to_ws = e in (E, N)
        kind = 1 if e in (N, S) else 0
        lines = [(h, to) for h in range(2) for to in ((W, S) if to_ws else (E, N))]

        @pl.when(has)
        def _(e=e, q=q, line=line, kind=kind, lines=lines):
            ring[e, 0] = sent[e, 1]
            for j, (h, to) in enumerate(lines):
                far_x = links[0, to, x * 2 + h] // 2
                chosen[e, j] = ring[e, lax.rem(x - far_x + pairs, pairs)]
            for j, (h, to) in enumerate(lines):
                g = x * 2 + h
                place = lambda p, to=to: (p, line) if to in (W, E) else (line, p)
                for kind_x, p in enumerate(ext_to(q)):
                    slot = (half * 2 + kind) * 4 + kind_x
                    row, col = place(p)

                    @pl.when((p >= 0) & (p <= last))
                    def _(j=j, to=to, slot=slot, g=g, row=row, col=col):
                        remote(
                            chosen.at[e, j, pl.ds(7, 1)], ends_ref.at[to, slot], ext_send.at[e], ext_recv.at[to], at(g, row, col)
                        ).start()

            for j, (h, to) in enumerate(lines):
                g = x * 2 + h
                place = lambda p, to=to: (p, line) if to in (W, E) else (line, p)
                for par, p in enumerate((q, last - q)):
                    slot = (half * 2 + kind) * 2 + par
                    row, col = place(p)
                    mine = (g == f) & (row == r) & (col == c)

                    @pl.when(~mine)
                    def _(j=j, to=to, slot=slot, g=g, row=row, col=col):
                        remote(
                            chosen.at[e, j], rims_ref.at[to, slot], main_send.at[e], main_recv.at[to], at(g, row, col)
                        ).start()

                    @pl.when(mine)
                    def _(j=j, to=to, slot=slot):
                        pltpu.make_async_copy(chosen.at[e, j], rims_ref.at[to, slot], main_recv.at[to]).start()

    corner_copy = lambda i: remote(ring_ends, table_ref.at[me_corner], corner_send.at[0], corner_recv.at[0], corner_at(i))

    @pl.when(corner)
    def _():
        for copy in ends_copies():
            copy.wait_recv()
        ring_ends[0] = ends[...]
        for i in range(8):

            @pl.when(i != me_corner)
            def _(i=i):
                corner_copy(i).start()

        pltpu.make_async_copy(ring_ends, table_ref.at[me_corner], corner_recv.at[0]).start()

    take = lambda ref, ss, rs: remote(ref, ref, ss, rs, here)
    for e, to, dr, dc in near:

        @pl.when(inside(r + dr, c + dc))
        def _(e=e, to=to, dr=dr, dc=dc):
            near_copy(e, to, dr, dc).wait_send()

    for k, dr, dc in diagonal:

        @pl.when(inside(r + dr, c + dc))
        def _(k=k, dr=dr, dc=dc):
            diag_copy(k, dr, dc).wait_send()

    for e, has, q, line in edges:

        @pl.when(has)
        def _(e=e, q=q):
            for copy in ring_copies(e):
                copy.wait_send()

            @pl.when(~own)
            def _():
                take(rims_ref.at[e, pl.ds(0, 8)], main_send.at[e], main_recv.at[e]).wait_send()

            @pl.when(own)
            def _():
                take(rims_ref.at[e, pl.ds(0, 7)], main_send.at[e], main_recv.at[e]).wait_send()

            @pl.when(is_end(q))
            def _():
                take(ends_ref.at[e, pl.ds(0, 8)], ext_send.at[e], ext_recv.at[e]).wait_send()

            @pl.when(~is_end(q))
            def _():
                take(ends_ref.at[e], ext_send.at[e], ext_recv.at[e]).wait_send()

    @pl.when(corner)
    def _():
        for copy in ends_copies():
            copy.wait_send()
        take(table_ref.at[pl.ds(0, 7)], corner_send.at[0], corner_recv.at[0]).wait_send()

    for e, to, dr, dc in near:

        @pl.when(inside(r - dr, c - dc))
        def _(e=e, to=to):
            take(rims_ref.at[to, 8], near_send.at[e], near_recv.at[e]).wait_recv()

    for k, dr, dc in diagonal:

        @pl.when(inside(r - dr, c - dc))
        def _(k=k):
            take(diag_ref.at[k], diag_send.at[k], diag_recv.at[k]).wait_recv()

    link = lambda face, edge, k: links[k, edge, face]
    end = lambda row, k, line: row[:, 16 * k + line : 16 * k + line + 1]
    at_end = lambda row, high, k, line: jnp.where(high == 1, end(row, 3 - k, line), end(row, k, line))

    def corner_of(face, edge, high):
        row = jnp.where(edge == S, 0, jnp.where(edge == N, 1, high))
        col = jnp.where(edge == W, 0, jnp.where(edge == E, 1, high))
        return table_ref[face % 2 * 4 + row * 2 + col, lax.rem(x - face // 2 + pairs, pairs), edge]

    def beyond(face, edge, high):
        far, far_edge, turn = (link(face, edge, k) for k in range(3))
        stop = high ^ turn
        return at_end(corner_of(far, far_edge, stop), stop, 0, 8)

    def at_corner(face, edge, low_end):
        vertical = (edge == W) | (edge == E)
        side_edge = jnp.where(vertical, S, W) if low_end else jnp.where(vertical, N, E)
        start = (edge >= E).astype(jnp.int32)
        far, far_edge, turn = (link(face, side_edge, k) for k in range(3))
        high = start ^ turn
        row = corner_of(far, far_edge, high)
        far_vertical = (far_edge == W) | (far_edge == E)
        third = beyond(far, jnp.where(far_vertical, N, E), (far_edge >= E).astype(jnp.int32))
        ahead = jnp.where(high == 1, third, end(row, 1, 5))
        s1 = at_end(row, high, 0, 1) - G * (ahead - at_end(row, high, 0, 5))
        if low_end:
            parts = {(3, 0): at_end(row, high, 0, 0), (3, 1): s1}
        else:
            parts = {(0, 0): at_end(row, high, 0, 0)}
            across = at_end(row, high, 0, 8)
            parts.update({(0, 1): s1, (0, 5): across, (1, 5): across, (0, 6): at_end(row, high, 0, 3)})
            parts.update({(0, 7): at_end(row, high, 0, 4), (0, 8): at_end(row, high, 1, 8)})
        made = jnp.zeros((1, side), jnp.float32)
        for (k, line), value in parts.items():
            made = jnp.where(lane == 16 * k + line, value, made)
        return made

    choices = []
    for e, on_face, seg, _ in edges:
        to_ws = e in (W, S)
        across = e in (W, E)
        face, partner, turn = (link(f, e, k) for k in range(3))
        kind = (partner == (N if to_ws else S)).astype(jnp.int32)
        q = jnp.where(turn == 1, last - seg, seg)
        slot = jnp.where(on_face, (face % 2 * 2 + kind) * 2 + turn, 8)
        slot_x = jnp.where(on_face, (face % 2 * 2 + kind) * 4 + 2 * turn, 0)
        strip = (e + 2) % 4
        lo_at, hi_at = {W: (0, 2), S: (0, 1), E: (1, 3), N: (2, 3)}[e]
        flag = jnp.where(on_face, turn, 0).astype(jnp.float32)
        picked[e, 12:13, :] = jnp.zeros((1, side), jnp.float32) + flag
        choices.append((e, on_face, face, partner, q, slot, slot_x, strip, lo_at, hi_at))

    for e, has, q, line in edges:

        @pl.when(has)
        def _(e=e, q=q):
            take(rims_ref.at[e, pl.ds(0, 8)], main_send.at[0], main_recv.at[e]).wait_recv()

            @pl.when(is_end(q))
            def _():
                take(ends_ref.at[e, pl.ds(0, 8)], ext_send.at[0], ext_recv.at[e]).wait_recv()

            @pl.when(~is_end(q))
            def _():
                take(ends_ref.at[e], ext_send.at[0], ext_recv.at[e]).wait_recv()

    @pl.when(corner)
    def _():
        take(table_ref, corner_send.at[0], corner_recv.at[0]).wait_recv()

    for e, on_face, face, partner, q, slot, slot_x, strip, lo_at, hi_at in choices:
        picked[e, 0:8, :] = rims_ref[e, slot]
        picked[e, 10:11, :] = jnp.where(on_face, ends_ref[e, slot_x], diag_ref[lo_at, strip])
        picked[e, 11:12, :] = jnp.where(on_face, ends_ref[e, slot_x + 1], diag_ref[hi_at, strip])

        @pl.when(corner & on_face)
        def _(e=e, face=face, partner=partner, q=q):
            picked[e, 10:11, :] = jnp.where(q == 0, at_corner(face, partner, True), picked[e, 10:11, :])
            picked[e, 11:12, :] = jnp.where(q == last, at_corner(face, partner, False), picked[e, 11:12, :])


def substeps(sides, picked, coef, *refs):
    fields, refs = refs[:8], refs[8:]
    s_out, u_out, v_out, h_out, levels, sums, out_sem, sum_sem = refs
    last = sides - 1
    side = levels.shape[1]
    c = lax.axis_index("narrow")
    r = lax.rem(lax.axis_index("wide"), sides)
    lane = lax.broadcasted_iota(jnp.int32, (1, side), 1)
    rows = lax.broadcasted_iota(jnp.int32, (side, side), 0)
    cols = lax.broadcasted_iota(jnp.int32, (side, side), 1)
    diagonal = rows == cols
    pick = lambda cond, a, b: jnp.where(cond, a, b)
    up_by = lambda x, fill: jnp.where(lane == side - 1, fill, pltpu.roll(x, side - 1, 1))
    down_by = lambda x, fill: jnp.where(lane == 0, fill, pltpu.roll(x, 1, 1))
    head = lambda x: x[:, 0:1]
    tail = lambda x: x[:, side - 1 : side]
    end = lambda row, k, line: row[:, 16 * k + line : 16 * k + line + 1]

    def ghost(edge, to_ws):
        block = picked[edge]
        line = [block[k : k + 1, :] for k in range(6 if to_ws else 5)]
        own, lo_x, hi_x = (block[k : k + 1, :] for k in (7, 10, 11))
        flipped = block[12:13, 0:1] > 0.5
        lo = dict(
            s0=end(lo_x, 3, 0), s1=end(lo_x, 3, 1) - G * (end(own, 0, 5) - end(lo_x, 3, 5)),
            F=end(lo_x, 3, 8), R=end(lo_x, 3, 3), Dn=end(lo_x, 3, 4), Fb=end(lo_x, 2, 8), g=end(lo_x, 3, 15),
        )
        hi = dict(
            s0=end(hi_x, 0, 0), s1=end(hi_x, 0, 1) - G * (end(hi_x, 1, 5) - end(hi_x, 0, 5)),
            T0=end(hi_x, 0, 5), Q=end(hi_x, 0, 6), D=end(hi_x, 0, 7), Tb=end(hi_x, 0, 8),
            F=end(hi_x, 0, 8), R=end(hi_x, 0, 3), Dn=end(hi_x, 0, 4), Fb=end(hi_x, 1, 8), g=end(hi_x, 0, 15),
        )
        shared = ("s0", "s1", "F", "R", "Dn", "Fb", "g")
        new_lo = {n: pick(flipped, hi[n], lo[n]) for n in shared}
        new_hi = {n: pick(flipped, lo[n], hi[n]) for n in shared}
        for name in ("T0", "Q", "D", "Tb"):
            new_hi[name] = hi[name]
        if to_ws:
            line[5] = pick((lane == 0) & flipped, hi["D"], line[5])
            new_hi["D"] = pick(flipped, end(own, 0, 7), hi["D"])
        new_lo["first"] = pick(flipped, -hi["T0"], end(own, 0, 5))
        theirs = (flipped, lo, hi, own)
        return line, new_lo, new_hi, theirs

    (wl, w_lo, w_hi, w_own), (sl, s_lo, s_hi, s_own) = ghost(W, True), ghost(S, True)
    (el, e_lo, e_hi, e_own), (nl, n_lo, n_hi, n_own) = ghost(E, False), ghost(N, False)

    for d, x in ((w_lo, s_lo), (w_hi, n_lo), (s_lo, w_lo), (s_hi, e_lo)):
        d["s1"] = d["s1"] - d["g"] * x["first"]

    west, south, east, north = c == 0, r == 0, c == last, r == last
    take_w, take_s = west & ~south, south & ~west
    sw_w = {n: pick(take_s, s_lo[n], w_lo[n]) for n in ("s0", "s1")}
    sw_s = {n: pick(take_w, w_lo[n], s_lo[n]) for n in ("s0", "s1")}
    w_lo.update(sw_w)
    s_lo.update(sw_s)
    share = (("s0", "s0"), ("s1", "s1"), ("T0", "F"), ("Q", "R"), ("D", "Dn"), ("Tb", "Fb"))
    take_e, take_s = east & ~south, south & ~east
    se_s = {a: pick(take_e, e_lo[b], s_hi[a]) for a, b in share}
    e_lo["s0"] = pick(take_s, s_hi["s0"], e_lo["s0"])
    s_hi.update(se_s)
    take_n, take_w = north & ~west, west & ~north
    nw_w = {a: pick(take_n, n_lo[b], w_hi[a]) for a, b in share}
    n_lo["s0"] = pick(take_w, w_hi["s0"], n_lo["s0"])
    w_hi.update(nw_w)
    take_e, take_n = east & ~north, north & ~east
    share = (("s0", "s0"), ("T0", "F"), ("Q", "R"), ("D", "Dn"))
    ne_n = {a: pick(take_e, e_hi[b], n_hi[a]) for a, b in share}
    ne_e = {a: pick(take_n, n_hi[b], e_hi[a]) for a, b in share}
    n_hi.update(ne_n)
    e_hi.update(ne_e)

    def missing(lo, hi, theirs):
        flipped, their_lo, their_hi, own = theirs
        place = pick(flipped, side - 1 - lane, lane)
        t0, q, d, s0 = (pick(flipped, their_hi[n], hi[n]) for n in ("T0", "Q", "D", "s0"))
        tb = pick(flipped, their_hi["Tb"], hi["Tb"])
        low = end(own, 0, 7) * pick(flipped, their_lo["s0"], lo["s0"])
        t1 = q - d * (s0 - end(own, 3, 0))
        return place == side - 1, place == 0, t0, t1, 0.8 * t0 + 0.1 * q + 0.1 * t1, tb, low

    class HeightRim:
        def __init__(self, line, lo, hi, theirs):
            top, bottom, t0, t1, t2, tb, low = missing(lo, hi, theirs)
            s0, x1, x2, x3, back, d = line
            x1 = x1 - jnp.where(top, G * t0, 0.0)
            x2 = x2 - jnp.where(top, G * t1, 0.0) + jnp.where(bottom, G * low, 0.0)
            x3 = x3 - jnp.where(top, G * t2 + G * back * (G * tb), 0.0) + jnp.where(bottom, G * (0.1 * low), 0.0)
            self.line = s0, x1, x2, x3, back, d
            self.lo, self.hi = lo, hi

        def at(self, n, flux):
            s0, x1, x2, x3, back, d = self.line
            if n == 0:
                return s0
            if n == 1:
                self.s1 = x1 - G * flux
                return self.s1
            s1 = self.s1
            if n == 2:
                self.s2 = x2 + 0.1 * s1 - G * flux
                return self.s2
            slope = d * (s1 - down_by(s1, self.lo["s1"]))
            slope_hi = self.hi["D"] * (self.hi["s1"] - tail(s1))
            return x3 + 0.81 * s1 + 0.1 * self.s2 - G * back * s1 - G * flux + G * (up_by(slope, slope_hi) - slope)

    class FluxRim:
        def __init__(self, line, lo, hi, theirs):
            top, bottom, t0, t1, _, _, low = missing(lo, hi, theirs)
            f0, p1, p2, p3, d = line
            p2 = p2 + d * jnp.where(top, G * t0, 0.0)
            p3 = p3 + d * (jnp.where(top, G * (0.1 * t0 + t1), 0.0) - jnp.where(bottom, G * low, 0.0))
            self.line = f0, p1, p2, p3, d

        def at(self, n, height):
            f0, p1, p2, p3, d = self.line
            if n == 0:
                return f0
            if n == 1:
                self.f1 = p1 + d * height
                return self.f1
            if n == 2:
                self.f2 = p2 + 0.1 * self.f1 + d * height
                return self.f2
            return p3 + (0.81 - G * d) * self.f1 + 0.1 * self.f2 + d * height

    rim_w, rim_s = HeightRim(wl, w_lo, w_hi, w_own), HeightRim(sl, s_lo, s_hi, s_own)
    rim_e, rim_n = FluxRim(el, e_lo, e_hi, e_own), FluxRim(nl, n_lo, n_hi, n_own)
    as_row = lambda col: jnp.sum(jnp.where(diagonal, col, 0.0), axis=0, keepdims=True)
    as_col = lambda row: jnp.sum(jnp.where(diagonal, row, 0.0), axis=1, keepdims=True)
    sp_, s_, up_, u_, vp_, v_, dw_, ds_ = (x[...] for x in fields)
    first_col, last_col = cols == 0, cols == side - 1
    first_row, last_row = rows == 0, rows == side - 1
    flux_w = flux_s = height_e = height_n = None
    snaps = []
    for n in range(SUBSTEPS):
        fw, fs = dw_ * u_, ds_ * v_
        west_line, south_line = rim_w.at(n, flux_w), rim_s.at(n, flux_s)
        east_line, north_line = rim_e.at(n, height_e), rim_n.at(n, height_n)
        flux_w, flux_s = as_row(fw[:, 0:1]), fs[0:1, :]
        height_e, height_n = as_row(s_[:, side - 1 : side]), s_[side - 1 : side, :]
        fe = jnp.where(last_col, as_col(east_line), pltpu.roll(fw, side - 1, 1))
        fn = jnp.where(last_row, north_line, pltpu.roll(fs, side - 1, 0))
        sw = jnp.where(first_col, as_col(west_line), pltpu.roll(s_, 1, 1))
        ss = jnp.where(first_row, south_line, pltpu.roll(s_, 1, 0))
        s_next = sp_ - G * ((fe - fw) + (fn - fs))
        u_next = up_ - G * (s_ - sw)
        v_next = vp_ - G * (s_ - ss)
        sp_ = s_ + 0.1 * (sp_ - 2.0 * s_ + s_next)
        up_ = u_ + 0.1 * (up_ - 2.0 * u_ + u_next)
        vp_ = v_ + 0.1 * (vp_ - 2.0 * v_ + v_next)
        s_, u_, v_ = s_next, u_next, v_next
        snaps.append(s_)
    stores = []
    for k, (x, out) in enumerate(((s_, s_out), (u_, u_out), (v_, v_out))):
        levels[k] = x
        stores.append(pltpu.make_async_copy(levels.at[k], out, out_sem.at[k]))
        stores[-1].start()
    for k in range(2 * CONSTITUENTS):
        total = coef[k : k + 1, 0:1] * snaps[0]
        for n in range(1, SUBSTEPS):
            total += coef[k : k + 1, n : n + 1] * snaps[n]
        sums[k] = total
        stores.append(pltpu.make_async_copy(sums.at[k], h_out.at[k], sum_sem.at[k]))
        stores[-1].start()
    for copy in stores:
        copy.wait()


def solution(mesh):
    def body(sp, s, up, u, vp, v, dw, ds, links, ph):
        side = s.shape[0]
        sides = mesh.shape["narrow"]
        faces = mesh.shape["wide"] // sides
        f32 = jnp.float32
        shape = lambda *dims: jax.ShapeDtypeStruct(dims, f32)
        hbm = pl.BlockSpec(memory_space=pl.ANY)
        vmem = pl.BlockSpec(memory_space=pltpu.VMEM)
        dma = pltpu.SemaphoreType.DMA
        scratch = lambda *dims: pltpu.VMEM(dims, f32)
        pairs = faces // 2
        links = jnp.transpose(links, (2, 1, 0))
        fields = (sp, s, up, u, vp, v, dw, ds)
        grant = 8 << 20
        in_hbm = [pltpu.with_memory_space_constraint(a, pltpu.HBM) for a in (links, ph, *fields)]
        got = pl.pallas_call(
            functools.partial(exchange, sides, faces),
            out_shape=(shape(4, 16, side), shape(2 * CONSTITUENTS, side)),
            in_specs=[hbm] * 10,
            out_specs=(vmem,) * 2,
            scratch_shapes=[
                pltpu.SMEM(links.shape, jnp.int32),
                pltpu.SMEM(ph.shape, f32),
                scratch(4, 9, 8, side),
                scratch(4, 16, 1, side),
                scratch(8, pairs, 4, 1, side),
                scratch(4, 4, 1, side),
                scratch(8, side, side),
                scratch(4, 16, side),
                scratch(4, 2, 8, side),
                scratch(4, 1, side),
                scratch(4, pairs, 8, side),
                scratch(pairs, 4, 1, side),
                scratch(4, 4, 8, side),
                dma((8,)), dma((2,)), dma((4,)), dma((4,)), dma((4,)), dma((4,)),
                dma((4, pairs)), dma((4, pairs)), dma((pairs,)), dma((pairs,)),
                dma((4,)), dma((4,)), dma((4,)), dma((4,)), dma((1,)), dma((1,)),
            ],
            compiler_params=pltpu.CompilerParams(collective_id=0, has_side_effects=True, vmem_limit_bytes=grant),
        )(*in_hbm)
        tile = shape(side, side)
        return pl.pallas_call(
            functools.partial(substeps, sides),
            out_shape=(tile, tile, tile, shape(2 * CONSTITUENTS, side, side)),
            in_specs=[vmem] * 10,
            out_specs=(hbm,) * 4,
            scratch_shapes=[scratch(3, side, side), scratch(2 * CONSTITUENTS, side, side), dma((3,)), dma((2 * CONSTITUENTS,))],
            compiler_params=pltpu.CompilerParams(vmem_limit_bytes=grant),
        )(*got, *fields)

    tiles = P("wide", "narrow")
    return jax.shard_map(
        body,
        mesh=mesh,
        in_specs=(tiles,) * 8 + (P(), P()),
        out_specs=(tiles, tiles, tiles, P(None, "wide", "narrow")),
        check_vma=False,
    )
```
